32 devices in a mesh: img: 8 (over z, y), row: 2 (over x), col: 2 (over core).
Axes of the slice: x: 2, y: 2, z: 4, core: 2. Of those that a mesh axis runs over, the one named last changes fastest.
Arguments:
- latents: bfloat16 [24, 4, 64, 64], P('img', None, 'row', 'col'), may hold values from -6 to 6
- time_bin: int32 [24], P('img'), may hold values from 0 to 99
- class_label: int32 [24], P('img'), may hold values from 0 to 1000
- live: int32 [24], P('img'), may hold values from 0 to 1, as said below
- time_table: bfloat16 [100, 384], replicated, may hold values from -4 to 4
- class_table: bfloat16 [1001, 384], replicated, may hold values from -4 to 4
- patch_weight: bfloat16 [16, 384], replicated, may hold values from -1.5 to 1.5
- patch_bias: bfloat16 [384], replicated, may hold values from -3 to 3
- ada_weight: bfloat16 [384, 2304], replicated, may hold values from -0.3125 to 0.3125
- ada_bias: bfloat16 [2304], replicated, may hold values from -3 to 3
- qkv_weight: bfloat16 [384, 1152], replicated, may hold values from -0.3125 to 0.3125
- qv_bias: bfloat16 [768], replicated, may hold values from -2 to 2
- proj_weight: bfloat16 [384, 384], replicated, may hold values from -1.25 to 1.25
- proj_bias: bfloat16 [384], replicated, may hold values from -2 to 2
- fc1_weight: bfloat16 [384, 1536], replicated, may hold values from -0.3125 to 0.3125
- fc1_bias: bfloat16 [1536], replicated, may hold values from -3 to 3
- fc2_weight: bfloat16 [1536, 384], replicated, may hold values from -0.21875 to 0.21875
- fc2_bias: bfloat16 [384], replicated, may hold values from -2 to 2
- final_ada_weight: bfloat16 [384, 768], replicated, may hold values from -0.3125 to 0.3125
- final_ada_bias: bfloat16 [768], replicated, may hold values from -3 to 3
- out_weight: bfloat16 [384, 16], replicated, may hold values from -0.3125 to 0.3125
- out_bias: bfloat16 [16], replicated, may hold values from -3 to 3
- cotangent: bfloat16 [24, 4, 64, 64], P('img', None, 'row', 'col'), may hold values from -6 to 6
Outputs:
- out_latents: bfloat16 [24, 4, 64, 64], P('img', None, 'row', 'col')
- latent_grad: float32 [24, 4, 64, 64], P('img', None, 'row', 'col')
- time_grad: float32 [100, 384], replicated
- class_grad: float32 [1001, 384], replicated
- patch_weight_grad: float32 [16, 384], replicated
- patch_bias_grad: float32 [384], replicated
- ada_weight_grad: float32 [384, 2304], replicated
- ada_bias_grad: float32 [2304], replicated
- qkv_weight_grad: float32 [384, 1152], replicated
- qv_bias_grad: float32 [768], replicated
- proj_weight_grad: float32 [384, 384], replicated
- proj_bias_grad: float32 [384], replicated
- fc1_weight_grad: float32 [384, 1536], replicated
- fc1_bias_grad: float32 [1536], replicated
- fc2_weight_grad: float32 [1536, 384], replicated
- fc2_bias_grad: float32 [384], replicated
- final_ada_weight_grad: float32 [384, 768], replicated
- final_ada_bias_grad: float32 [768], replicated
- out_weight_grad: float32 [384, 16], replicated
- out_bias_grad: float32 [16], replicated
The draws below stay inside these ranges and needn't reach their ends.
Inputs may be any that keep to these rules, and one draw needn't show every extreme that they name: Within each aligned block of 3 slots (those of one index of img) the live slots come first; every block has at least one and some block is full.
All inputs are finite; a program needn't handle non-finite values.
Results may differ from the reference program's by a relative error of at most 0.011.
Values may be sent and summed in bfloat16 or wider, within the bound.
A program may use at most 192 MiB of HBM per device.

```python
import math
import jax
import jax.numpy as jnp
import numpy as np
from jax import lax

D = 384
HEADS = 6
HEAD_DIM = 64
FF = 1536
CLASSES = 1001
BINS = 100
CHANNELS = 4
LATENT = 64
SLOTS = 3
IMAGES = 24
PATCH_IN = 16


def draw_live(key, part):
    groups = IMAGES // SLOTS
    counts = jax.random.randint(jax.random.fold_in(key, 11), (groups,), 1, SLOTS + 1)
    full_at = jax.random.randint(jax.random.fold_in(key, 12), (), 0, groups)
    counts = jnp.where(jnp.arange(groups) == full_at, SLOTS, counts)
    marks = jnp.arange(SLOTS)[None, :] < counts[:, None]
    return marks.reshape(-1).astype(jnp.int32)


def plant(values, stream_key, low, largest):
    extent = values.shape
    index_at = [jax.random.randint(jax.random.fold_in(stream_key, axis), (), 0, extent[axis]) for axis in range(len(extent))]
    values = values.at[tuple(index_at)].set(low)
    longest = extent.index(max(extent))
    index_at[longest] = (index_at[longest] + 1) % extent[longest]
    return values.at[tuple(index_at)].set(largest)


def levels(rng, dims, shards, least, top_value):
    level = 1.0
    for dim, shards_of in shards:
        heights = jax.random.uniform(jax.random.fold_in(jax.random.fold_in(rng, 6), dim), (shards_of,), jnp.float32, least / len(shards), top_value / len(shards))
        level = level * jnp.repeat(jnp.exp(heights), dims[dim] // shards_of).reshape((-1,) + (1,) * (len(dims) - 1 - dim))
    return level


def rank_table(number_of, slope):
    portions = [(1 << 20) // math.isqrt(standing ** slope) + 1 for standing in range(1, number_of + 1)]
    deviation = 1 + sum(portions) // (1 << 30)
    return np.cumsum(np.array([max(1, weight // deviation) for weight in portions]))


def skewed_ids(stream_key, shape, number_of, skew):
    table = rank_table(number_of, skew)
    ticket = jax.random.randint(jax.random.fold_in(stream_key, 1), shape, 0, int(table[number_of - 1]))
    grade = jnp.searchsorted(jnp.asarray(table, jnp.int32), ticket, side="right")
    return jax.random.permutation(jax.random.fold_in(stream_key, 2), number_of)[grade].astype(jnp.int32)


def bell_draw(key, shape, scale, limit, cuts=(), held_as=jnp.bfloat16):
    drawn = scale * jax.random.normal(key, shape, jnp.float32)
    if cuts:
        drawn = drawn * levels(key, shape, cuts, -0.22, 0.18)
    return jnp.clip(drawn, -limit, limit).astype(held_as)


def setup_inputs(seed: int = 0) -> dict:
    keys = jax.random.split(jax.random.key(seed), 24)
    latents = bell_draw(keys[0], (IMAGES, CHANNELS, LATENT, LATENT), 1.0, 6.0, ((0, 8), (2, 2), (3, 2)))
    time_bin = plant(jax.random.randint(keys[1], (IMAGES,), 0, BINS), jax.random.fold_in(keys[1], 1), 0, BINS - 1).astype(jnp.int32)
    class_label = plant(skewed_ids(keys[2], (IMAGES,), CLASSES, 1), jax.random.fold_in(keys[2], 3), 0, CLASSES - 1).astype(jnp.int32)
    live = draw_live(jax.random.fold_in(keys[23], 71), 0)
    time_table = bell_draw(keys[4], (BINS, D), 0.7, 4.0)
    class_table = bell_draw(keys[5], (CLASSES, D), 0.7, 4.0)
    patch_weight = bell_draw(keys[6], (PATCH_IN, D), PATCH_IN ** -0.5, 1.5)
    patch_bias = bell_draw(keys[7], (D,), 0.5, 3.0)
    ada_weight = bell_draw(keys[8], (D, 6 * D), D ** -0.5, 0.3125)
    ada_bias = bell_draw(keys[9], (6 * D,), 0.5, 3.0)
    qkv_weight = bell_draw(keys[10], (D, 3 * D), D ** -0.5, 0.3125)
    qv_bias = bell_draw(keys[11], (2 * D,), 0.3, 2.0)
    proj_weight = bell_draw(keys[12], (D, D), (D // 16) ** -0.5, 1.25)
    proj_bias = bell_draw(keys[13], (D,), 0.3, 2.0)
    fc1_weight = bell_draw(keys[14], (D, FF), D ** -0.5, 0.3125)
    fc1_bias = bell_draw(keys[15], (FF,), 0.5, 3.0)
    fc2_weight = bell_draw(keys[16], (FF, D), (FF // 2) ** -0.5, 0.21875)
    fc2_bias = bell_draw(keys[17], (D,), 0.3, 2.0)
    final_ada_weight = bell_draw(keys[18], (D, 2 * D), D ** -0.5, 0.3125)
    final_ada_bias = bell_draw(keys[19], (2 * D,), 0.5, 3.0)
    out_weight = bell_draw(keys[20], (D, PATCH_IN), D ** -0.5, 0.3125)
    out_bias = bell_draw(keys[21], (PATCH_IN,), 0.5, 3.0)
    cotangent = bell_draw(keys[22], (IMAGES, CHANNELS, LATENT, LATENT), 1.0, 6.0, ((0, 8), (2, 2), (3, 2)))
    return dict(latents=latents, time_bin=time_bin, class_label=class_label, live=live, time_table=time_table, class_table=class_table, patch_weight=patch_weight, patch_bias=patch_bias, ada_weight=ada_weight, ada_bias=ada_bias, qkv_weight=qkv_weight, qv_bias=qv_bias, proj_weight=proj_weight, proj_bias=proj_bias, fc1_weight=fc1_weight, fc1_bias=fc1_bias, fc2_weight=fc2_weight, fc2_bias=fc2_bias, final_ada_weight=final_ada_weight, final_ada_bias=final_ada_bias, out_weight=out_weight, out_bias=out_bias, cotangent=cotangent)


@jax.custom_vjp
def low(v):
    return lax.optimization_barrier(v.astype(jnp.bfloat16)).astype(jnp.float32)

@jax.custom_vjp
def low_back(v):
    return v

def low_keep(v):
    return (low(v), None)

def low_pass(kept, grad):
    return (grad,)

def back_keep(v):
    return (v, None)

def back_low(kept, grad):
    return (low(grad),)
low.defvjp(low_keep, low_pass)
low_back.defvjp(back_keep, back_low)

def positions(grid, width):
    quarter = width // 4
    omega = 1.0 / 10000.0 ** (jnp.arange(quarter, dtype=jnp.float32) / quarter)
    places = jnp.arange(grid, dtype=jnp.float32)
    angles = places[:, None] * omega[None, :]
    single = jnp.concatenate([jnp.sin(angles), jnp.cos(angles)], axis=1)
    first = jnp.broadcast_to(single[:, None, :], (grid, grid, width // 2))
    second = jnp.broadcast_to(single[None, :, :], (grid, grid, width // 2))
    return jnp.concatenate([first, second], axis=2)

def to_patches(tile):
    slots, chans, height, wide = tile.shape
    shaped = tile.reshape(slots, chans, height // 2, 2, wide // 2, 2).transpose(0, 2, 4, 1, 3, 5)
    return shaped.reshape(slots, height // 2 * (wide // 2), chans * 4)

def from_patches(rows, chans, height, wide):
    slots = rows.shape[0]
    shaped = rows.reshape(slots, height // 2, wide // 2, chans, 2, 2).transpose(0, 3, 1, 4, 2, 5)
    return shaped.reshape(slots, chans, height, wide)

def modulate(value, shift, scale):
    centred = value - lax.optimization_barrier(jnp.mean(value, axis=-1, keepdims=True))
    spread = lax.optimization_barrier(jnp.mean(centred * centred, axis=-1, keepdims=True))
    return centred * lax.rsqrt(spread + 1e-06) * (1.0 + scale[:, None, :]) + shift[:, None, :]

def swish(v):
    return v * jax.nn.sigmoid(v)

def linear(value, weight):
    return jnp.einsum('spd,de->spe', value, weight, precision=lax.Precision.HIGHEST)

def reference(latents, time_bin, class_label, live, time_table, class_table, patch_weight, patch_bias, ada_weight, ada_bias, qkv_weight, qv_bias, proj_weight, proj_bias, fc1_weight, fc1_bias, fc2_weight, fc2_bias, final_ada_weight, final_ada_bias, out_weight, out_bias, cotangent):
    highest = lax.Precision.HIGHEST
    weights = tuple((w.astype(jnp.float32) for w in (time_table, class_table, patch_weight, patch_bias, ada_weight, ada_bias, qkv_weight, qv_bias, proj_weight, proj_bias, fc1_weight, fc1_bias, fc2_weight, fc2_bias, final_ada_weight, final_ada_bias, out_weight, out_bias)))
    live_f = live.astype(jnp.float32)
    onehot_time = (time_bin[:, None] == jnp.arange(BINS, dtype=jnp.int32)[None, :]).astype(jnp.float32)
    onehot_class = (class_label[:, None] == jnp.arange(CLASSES, dtype=jnp.int32)[None, :]).astype(jnp.float32)
    scale = 1.0 / HEAD_DIM ** 0.5

    def attend_one(parts):
        query, key, value = parts
        scores = low_back(jnp.einsum('qhd,khd->hqk', query, key, precision=highest) * scale)
        top = lax.optimization_barrier(jnp.max(scores, axis=-1, keepdims=True))
        expo = jnp.exp(scores - top)
        prob = expo / lax.optimization_barrier(jnp.sum(expo, axis=-1, keepdims=True))
        return jnp.einsum('hqk,khd->qhd', low(prob), value, precision=highest)

    def forward(lat, tt, ct, pw, pb, aw, ab, qw, qb, ow, ob, w1, b1, w2, b2, fw, fb, yw, yb):
        true = jnp.roll(lat, (1, 1), axis=(2, 3))
        patches = to_patches(true)
        grid = LATENT // 2
        pos = positions(grid, D).reshape(grid * grid, D)
        tok0 = jnp.einsum('spk,kd->spd', patches, pw, precision=highest) + pb + pos[None]
        cond = jnp.dot(onehot_time, tt, precision=highest) + jnp.dot(onehot_class, ct, precision=highest)
        cact = swish(cond)
        mod = jnp.dot(cact, aw, precision=highest) + ab
        sh1, sc1, g1, sh2, sc2, g2 = jnp.split(mod, 6, axis=1)
        fmod = jnp.dot(cact, fw, precision=highest) + fb
        shf, scf = jnp.split(fmod, 2, axis=1)
        x1 = low(modulate(tok0, sh1, sc1))
        bias_full = jnp.concatenate([qb[:D], jnp.zeros((D,), jnp.float32), qb[D:]])
        qkv = low(low_back(linear(x1, qw) + bias_full))
        images, tokens = (qkv.shape[0], qkv.shape[1])
        query = qkv[:, :, :D].reshape(images, tokens, HEADS, HEAD_DIM)
        key = qkv[:, :, D:2 * D].reshape(images, tokens, HEADS, HEAD_DIM)
        value = qkv[:, :, 2 * D:].reshape(images, tokens, HEADS, HEAD_DIM)
        att = lax.map(jax.checkpoint(attend_one), (query, key, value)).reshape(images, tokens, D)
        att = low(low_back(att))
        branch = low_back(linear(att, ow) + ob)
        resid = tok0 + g1[:, None, :] * branch
        x2 = low(modulate(resid, sh2, sc2))
        hidden_in = low_back(linear(x2, w1) + b1)
        hidden = low(jax.nn.gelu(hidden_in, approximate=True))
        mlp = low_back(linear(hidden, w2) + b2)
        x3 = resid + g2[:, None, :] * mlp
        xf = low(modulate(x3, shf, scf))
        rows = linear(xf, yw) + yb
        image = from_patches(rows, CHANNELS, LATENT, LATENT)
        return jnp.roll(image, (-1, -1), axis=(2, 3)) * live_f[:, None, None, None]
    result, pull = jax.vjp(forward, latents.astype(jnp.float32), *weights)
    grads = pull(cotangent.astype(jnp.float32))
    return (result.astype(jnp.bfloat16), grads[0], grads[1], grads[2], grads[3], grads[4], grads[5], grads[6], grads[7], grads[8], grads[9], grads[10], grads[11], grads[12], grads[13], grads[14], grads[15], grads[16], grads[17], grads[18])
```

```python
import functools

import jax
import jax.numpy as jnp
import numpy as np
from jax import lax
from jax.experimental import pallas as pl
from jax.experimental.pallas import tpu as pltpu
from jax.sharding import PartitionSpec as P

F32 = jnp.float32
BF16 = jnp.bfloat16
HEADS = 6
LATENT = 64
MESH = pl.DeviceIdType.MESH
VMEM = pl.BlockSpec(memory_space=pltpu.VMEM)
SMEM = pl.BlockSpec(memory_space=pltpu.SMEM)
ROUNDS = 3


def nn(a, b):
    return lax.dot_general(a, b, (((1,), (0,)), ((), ())), preferred_element_type=F32)


def nt(a, b):
    return lax.dot_general(a, b, (((1,), (1,)), ((), ())), preferred_element_type=F32)


def tn(a, b):
    return lax.dot_general(a, b, (((0,), (0,)), ((), ())), preferred_element_type=F32)


def parts(v, many):
    out = []
    for _ in range(many):
        piece = v.astype(BF16)
        out.append(piece)
        v = v - piece.astype(F32)
    return out


def iota(shape, dim):
    return lax.broadcasted_iota(jnp.int32, shape, dim)


def flag(cond):
    return jnp.where(cond, 1.0, 0.0)


def swish(v):
    return v / (1.0 + jnp.exp(-v))


def position_tables(grid, width):
    quarter = width // 4
    omega = np.float32(1.0) / np.power(
        np.float32(10000.0), np.arange(quarter, dtype=np.float32) / np.float32(quarter)
    )
    angles = np.arange(grid, dtype=np.float32)[:, None] * omega[None, :].astype(np.float32)
    single = np.concatenate([np.sin(angles), np.cos(angles)], axis=1).astype(np.float32)
    blank = np.zeros_like(single)
    return np.concatenate([single, blank], axis=1), np.concatenate([blank, single], axis=1)


def plane_maps(slots, chans, side, halves):
    rows = slots * chans * side
    lanes = halves * halves
    spread = []
    keep = flag(iota((rows, lanes), 0) % side // 2 == iota((rows, lanes), 1) // halves)
    pick = []
    for j in range(2):
        col = iota((side, lanes), 0)
        spread.append(flag(col == iota((side, lanes), 1) % halves * 2 + j).astype(BF16))
        many = slots * chans * 4
        out, src = iota((many, rows), 0), iota((many, rows), 1)
        same = (out // 4 == src // side) & (out % 4 // 2 == src % 2) & (out % 2 == j)
        pick.append(flag(same).astype(BF16))
    return keep, spread, pick


def shift_masks(halves):
    row, lane = iota((16, halves * halves), 0), iota((16, halves * halves), 1)
    return row % 4 >= 2, row % 2 == 1, lane, halves


def shift_in(planes, masks):
    odd_row, odd_col, lane, side = masks
    full = side * side
    down = [
        jnp.where(
            odd_row,
            jnp.where(lane < side, pltpu.roll(planes[s ^ 2], side, 1), pltpu.roll(planes[s], side, 1)),
            planes[s],
        )
        for s in range(4)
    ]
    return [
        jnp.where(
            odd_col,
            jnp.where(
                lane % side == 0, pltpu.roll(down[s ^ 1], full - side + 1, 1), pltpu.roll(down[s], 1, 1)
            ),
            down[s],
        )
        for s in range(4)
    ]


def shift_out(planes, masks):
    odd_row, odd_col, lane, side = masks
    full = side * side
    up = [
        jnp.where(
            odd_row,
            jnp.where(
                lane >= full - side,
                pltpu.roll(planes[s ^ 2], full - side, 1),
                pltpu.roll(planes[s], full - side, 1),
            ),
            planes[s],
        )
        for s in range(4)
    ]
    return [
        jnp.where(
            odd_col,
            jnp.where(
                lane % side == side - 1, pltpu.roll(up[s ^ 1], side - 1, 1), pltpu.roll(up[s], full - 1, 1)
            ),
            up[s],
        )
        for s in range(4)
    ]


def mate(slot):
    row, col = lax.axis_index("row"), lax.axis_index("col")
    return {"row": row ^ (slot >> 1), "col": col ^ (slot & 1)}


def greet(devices):
    barrier = pltpu.get_barrier_semaphore()
    for device in devices:
        pl.semaphore_signal(barrier, inc=1, device_id=device, device_id_type=MESH)
    pl.semaphore_wait(barrier, len(devices))


def gather_kernel(lat_ref, cot_ref, out_ref, send_sem, recv_sem):
    slots, chans, side, _ = lat_ref.shape
    greet([mate(s) for s in (1, 2, 3)])
    keep, spread, pick = plane_maps(slots, chans, side, side // 2)
    for k, ref in enumerate((lat_ref, cot_ref)):
        tile = ref[...].reshape(slots * chans * side, side)
        total = None
        for j in range(2):
            wide = (nn(tile, spread[j]) * keep).astype(BF16)
            term = nn(pick[j], wide)
            total = term if total is None else total + term
        out_ref[0, k] = total.astype(BF16)
    copies = []
    for s in (1, 2, 3):
        copy = pltpu.make_async_remote_copy(
            src_ref=out_ref.at[0],
            dst_ref=out_ref.at[s],
            send_sem=send_sem.at[s - 1],
            recv_sem=recv_sem.at[s - 1],
            device_id=mate(s),
            device_id_type=MESH,
        )
        copy.start()
        copies.append(copy)
    for copy in copies:
        copy.wait()


def gather_planes(latents, cotangent):
    slots, chans, side, _ = latents.shape
    return pl.pallas_call(
        gather_kernel,
        out_shape=jax.ShapeDtypeStruct((4, 2, slots * chans * 4, side * side // 4), BF16),
        in_specs=[VMEM] * 2,
        out_specs=VMEM,
        scratch_shapes=[pltpu.SemaphoreType.DMA((3,)), pltpu.SemaphoreType.DMA((3,))],
        compiler_params=pltpu.CompilerParams(collective_id=0, has_side_effects=True),
        name="gather_planes",
    )(latents, cotangent)


def norm(v):
    share = 1.0 / v.shape[-1]
    centred = v - jnp.sum(v, axis=-1, keepdims=True) * share
    spread = jnp.sum(centred * centred, axis=-1, keepdims=True) * share
    inv = lax.rsqrt(spread + 1e-06)
    return centred * inv, inv


def norm_back(hat, inv, grad):
    share = 1.0 / hat.shape[-1]
    first = jnp.sum(grad, axis=-1, keepdims=True) * share
    second = jnp.sum(grad * hat, axis=-1, keepdims=True) * share
    return inv * (grad - first - hat * second)


def col_sum(v):
    return jnp.sum(v, axis=0, keepdims=True)


BIAS_PATCH, BIAS_QV, BIAS_PROJ, BIAS_FC1, BIAS_FC2, BIAS_ADA, BIAS_OUT = 0, 384, 1152, 1536, 3072, 3456, 6528
ROW_PATCH, ROW_OUT, ROW_PATCH_B, ROW_PROJ_B, ROW_FC2_B, ROW_Q_B, ROW_V_B, ROW_FC1_B, ROW_OUT_B = (
    0, 16, 32, 33, 34, 35, 36, 37, 41,
)
SMALL_ROWS = 48
MOD_ROWS = 32


def step_kernel(
    time_ref, class_ref, live_ref, planes_ref, bias_ref, pos_a_ref, pos_b_ref,
    time_table_ref, class_table_ref, patch_w_ref, ada_ref, fada_ref, qkv_ref, proj_ref, fc1_ref, fc2_ref, out_w_ref,
    grads_ref, small_ref, mod_out_ref, edge_ref,
    mod_s, pos_s, pt_s, gy_s, wp_s, wo_s, x1_s, hat_s, inv_s, k_s, v_s, q_s, e_s, s_s, linv_s, delta_s,
    of_s, ob_s, h_s, gp_s, du_s, dm_s, x2t_s, da_s, dx_s, dot_s, dom_s, dk_s, dv_s, dq_s, acc_s, dx1_s, edge_s,
):
    d = qkv_ref.shape[0]
    slots = x1_s.shape[0] // 4
    toks = x1_s.shape[1]
    pairs = HEADS // 2
    ff = fc1_ref.shape[1]
    blocks = ff // d
    half = 16
    live = [live_ref[i].astype(F32) for i in range(slots)]
    bins, classes = time_table_ref.shape[0], class_table_ref.shape[0]

    def onehot(ids_ref, many):
        row, lane = iota((16, many), 0), iota((16, many), 1)
        hit = jnp.zeros((16, many), F32)
        for i in range(slots):
            hit = hit + flag((row == i) & (lane == ids_ref[i]))
        return hit.astype(BF16)

    cond = nn(onehot(time_ref, bins), time_table_ref[...]) + nn(
        onehot(class_ref, classes), class_table_ref[...]
    )
    cond = cond[:8]
    act = parts(swish(cond), 3)
    act = jnp.concatenate([p.astype(F32) for p in act] + [jnp.zeros((8, d), F32)], axis=0).astype(BF16)
    for p in range(8):
        w = ada_ref[:, p * d : (p + 1) * d] if p < 6 else fada_ref[:, (p - 6) * d : (p - 5) * d]
        m = nn(act, w)
        mod_s[p] = m[0:8] + m[8:16] + m[16:24] + bias_ref[:, BIAS_ADA + p * d : BIAS_ADA + (p + 1) * d]

    small_ref[...] = jnp.zeros_like(small_ref)
    row, lane = iota((8, d), 0), iota((8, d), 1)
    ids = jnp.zeros((8, d), F32)
    for i in range(slots):
        ids = ids + jnp.where((row == 3) & (lane == i), 0.25 * time_ref[i].astype(F32), 0.0)
        ids = ids + jnp.where((row == 3) & (lane == slots + i), 0.25 * class_ref[i].astype(F32), 0.0)
    mod_out_ref[24:32, :] = jnp.where(row < 3, 0.25 * cond, 0.0) + ids

    swap = flag(iota((16, 16), 0) == (iota((16, 16), 1) ^ 3)).astype(BF16)
    wp_s[...] = nn(swap, patch_w_ref[...]).astype(BF16)
    wo_s[...] = nt(swap, out_w_ref[...]).astype(BF16)
    out_bias = bias_ref[:, BIAS_OUT : BIAS_OUT + 128]
    pick = flag(iota((16, 128), 1) == (iota((16, 128), 0) ^ 3))
    out_bias = jnp.sum(pick * out_bias, axis=1, keepdims=True)

    my_row, my_col = lax.axis_index("row"), lax.axis_index("col")
    for s in range(4):
        ta = pos_a_ref[pl.ds(pl.multiple_of((my_row ^ (s >> 1)) * half, half), half), :]
        tb = pos_b_ref[pl.ds(pl.multiple_of((my_col ^ (s & 1)) * half, half), half), :]
        tb = tb + bias_ref[:, BIAS_PATCH : BIAS_PATCH + d]
        for a in range(half):
            pos_s[s, a * half : (a + 1) * half, :] = ta[a : a + 1, :] + tb

    masks = shift_masks(half)
    for i in range(slots):
        lat = shift_in([planes_ref[s, 0, i * 16 : (i + 1) * 16, :].astype(F32) for s in range(4)], masks)
        cot = shift_in([planes_ref[s, 1, i * 16 : (i + 1) * 16, :].astype(F32) for s in range(4)], masks)
        for s in range(4):
            pt_s[i * 4 + s] = lat[s].astype(BF16)
        gy_s[i] = (cot[0] * live[i]).astype(BF16)

    def tokens(t, carry):
        img, slot = t // 4, t % 4
        tok = tn(pt_s[t], wp_s[...]) + pos_s[slot]
        hat, inv = norm(tok)
        hat_s[t] = hat
        inv_s[t] = inv
        x1 = (hat * (1.0 + mod_s[1, pl.ds(img, 1), :]) + mod_s[0, pl.ds(img, 1), :]).astype(BF16)
        x1_s[t] = x1
        keys = nn(x1, qkv_ref[:, d : 2 * d]).astype(BF16)
        vals = (nn(x1, qkv_ref[:, 2 * d :]) + bias_ref[:, BIAS_QV + d : BIAS_QV + 2 * d]).astype(BF16)
        for p in range(pairs):
            k_s[img * pairs + p, slot] = keys[:, p * 128 : (p + 1) * 128]
            v_s[img * pairs + p, slot] = vals[:, p * 128 : (p + 1) * 128]
        return carry

    lax.fori_loop(0, slots * 4, tokens, 0)

    lane128 = iota((1, 128), 1) // 64
    head_mask = [flag(lane128 == h) for h in range(2)]

    def image(img, carry):
        at = pl.ds(img, 1)
        query = nn(x1_s[img * 4], qkv_ref[:, :d]) + bias_ref[:, BIAS_QV : BIAS_QV + d]
        query = query.astype(BF16).astype(F32) * 0.125
        for p in range(pairs):
            for h in range(2):
                q_s[img * HEADS + p * 2 + h] = (query[:, p * 128 : (p + 1) * 128] * head_mask[h]).astype(BF16)

        def attend(p, inner):
            idx = img * pairs + p
            for h in range(2):
                head = idx * 2 + h
                top = None
                for c in range(4):
                    s = nt(k_s[idx, c], q_s[head])
                    s_s[c] = s
                    m = jnp.max(s, axis=0, keepdims=True)
                    top = m if top is None else jnp.maximum(top, m)
                total, acc = None, None
                for c in range(4):
                    e = jnp.exp(s_s[c] - top)
                    l = col_sum(e)
                    total = l if total is None else total + l
                    eb = e.astype(BF16)
                    e_s[head, c] = eb
                    o = tn(v_s[idx, c], eb)[h * 64 : (h + 1) * 64]
                    acc = o if acc is None else acc + o
                linv = 1.0 / total
                linv_s[head] = linv
                of_s[img, pl.ds(pl.multiple_of(p * 128 + h * 64, 64), 64), :] = acc * linv
            return inner

        lax.fori_loop(0, pairs, attend, 0)

        def mod_row(p):
            return mod_s[p, at, :]

        ot = of_s[img].astype(BF16)
        ob_s[img] = ot
        branch = tn(ot, proj_ref[...]) + bias_ref[:, BIAS_PROJ : BIAS_PROJ + d]
        tok = tn(pt_s[img * 4], wp_s[...]) + pos_s[0]
        g1 = mod_row(2)
        resid = tok + g1 * branch
        hat2, inv2 = norm(resid)
        x2 = (hat2 * (1.0 + mod_row(4)) + mod_row(3)).astype(BF16)
        x2t_s[img] = x2.T
        mlp = jnp.zeros((toks, d), F32)
        k0, k1 = 0.7978845608028654, 0.044715
        for b in range(blocks):
            at_b = slice(b * d, (b + 1) * d)
            u = nn(x2, fc1_ref[:, at_b]) + bias_ref[:, BIAS_FC1 + b * d : BIAS_FC1 + (b + 1) * d]
            sq = u * u
            t = jnp.tanh(k0 * u * (1.0 + k1 * sq))
            cdf = 0.5 * (1.0 + t)
            hidden = (u * cdf).astype(BF16)
            h_s[img, :, at_b] = hidden
            gp_s[:, at_b] = cdf + (0.5 * k0) * u * (1.0 - t * t) * (1.0 + (3.0 * k1) * sq)
            mlp = mlp + nn(hidden, fc2_ref[at_b, :])
        mlp = mlp + bias_ref[:, BIAS_FC2 : BIAS_FC2 + d]
        g2 = mod_row(5)
        x3 = resid + g2 * mlp
        hatf, invf = norm(x3)
        scf = 1.0 + mod_row(7)
        xf = (hatf * scf + mod_row(6)).astype(BF16)
        live_i = live_ref[img].astype(F32)
        edge_s[4, img] = (nt(wo_s[...], xf) + out_bias) * live_i
        gy = gy_s[img]
        small_ref[ROW_OUT : ROW_OUT + 16, :] += nn(gy, xf)
        ones = jnp.ones((8, toks), BF16)
        small_ref[ROW_OUT_B : ROW_OUT_B + 1, 0:16] += nt(ones, gy)[0:1]
        dxf = tn(gy, wo_s[...])

        def put_mod(p, v):
            mod_out_ref[pl.ds(p * slots + img, 1), :] = v

        put_mod(6, col_sum(dxf))
        put_mod(7, col_sum(dxf * hatf))
        dx3 = norm_back(hatf, invf, dxf * scf)
        dm = (g2 * dx3).astype(BF16)
        dm_s[img] = dm
        put_mod(5, col_sum(mlp * dx3))
        small_ref[ROW_FC2_B : ROW_FC2_B + 1, :] += col_sum(dm.astype(F32))
        dx2 = jnp.zeros((toks, d), F32)
        for b in range(blocks):
            at_b = slice(b * d, (b + 1) * d)
            du = (nt(dm, fc2_ref[at_b, :]) * gp_s[:, at_b]).astype(BF16)
            du_s[img, :, at_b] = du
            small_ref[ROW_FC1_B + b : ROW_FC1_B + b + 1, :] += col_sum(du.astype(F32))
            dx2 = dx2 + nt(du, fc1_ref[:, at_b])
        put_mod(3, col_sum(dx2))
        put_mod(4, col_sum(dx2 * hat2))
        dx = dx3 + norm_back(hat2, inv2, dx2 * (1.0 + mod_row(4)))
        dx_s[img] = dx
        put_mod(2, col_sum(branch * dx))
        da = (g1 * dx).astype(BF16)
        da_s[img] = da
        small_ref[ROW_PROJ_B : ROW_PROJ_B + 1, :] += col_sum(da.astype(F32))
        dot = nt(proj_ref[...], da)
        blank = jnp.zeros((64, toks), F32)
        for hd in range(HEADS):
            head = img * HEADS + hd
            piece = dot[hd * 64 : (hd + 1) * 64]
            linv = linv_s[head]
            delta_s[head] = col_sum(piece * of_s[img, hd * 64 : (hd + 1) * 64, :]) * linv
            piece = piece * linv
            wide = jnp.concatenate([piece, blank] if hd % 2 == 0 else [blank, piece], axis=0).astype(BF16)
            dot_s[head] = wide
            dom_s[head] = wide.T
        return carry

    lax.fori_loop(0, slots, image, 0)

    for b in range(blocks):
        at_b = slice(b * d, (b + 1) * d)
        total = None
        for img in range(slots):
            term = tn(h_s[img, :, at_b], dm_s[img])
            total = term if total is None else total + term
        grads_ref[b * d : (b + 1) * d, :] = total.astype(BF16)
        total = None
        for img in range(slots):
            term = nn(x2t_s[img], du_s[img, :, at_b])
            total = term if total is None else total + term
        grads_ref[ff + b * d : ff + (b + 1) * d, :] = total.astype(BF16)
    total = None
    for img in range(slots):
        term = nn(ob_s[img], da_s[img])
        total = term if total is None else total + term
    grads_ref[2 * ff : 2 * ff + d, :] = total.astype(BF16)

    def attend_back(idx, carry):
        dqt = [None, None]
        for c in range(4):
            dk, dv = None, None
            kt = k_s[idx, c].T
            for h in range(2):
                head = idx * 2 + h
                e = e_s[head, c]
                dp = nn(v_s[idx, c], dot_s[head])
                ds = (e.astype(F32) * (dp - delta_s[head])).astype(BF16)
                dk_h, dv_h = nn(ds, q_s[head]), nn(e, dom_s[head])
                dk = dk_h if dk is None else dk + dk_h
                dv = dv_h if dv is None else dv + dv_h
                dq_h = nn(kt[h * 64 : (h + 1) * 64], ds)
                dqt[h] = dq_h if dqt[h] is None else dqt[h] + dq_h
            dk_s[idx, c] = dk.astype(BF16)
            dv_s[idx, c] = dv.astype(BF16)
        dq_s[idx] = (jnp.concatenate(dqt, axis=0) * 0.125).T.astype(BF16)
        return carry

    lax.fori_loop(0, slots * pairs, attend_back, 0)

    acc_s[...] = jnp.zeros_like(acc_s)
    for p in (0, 1):
        mod_out_ref[p * slots : (p + 1) * slots, :] = jnp.zeros((slots, d), F32)

    def tokens_back(t, carry):
        img, slot = t // 4, t % 4

        def joined(ref):
            return jnp.concatenate([ref[img * pairs + p, slot] for p in range(pairs)], axis=1)

        dk, dv = joined(dk_s), joined(dv_s)
        x1t = x1_s[t].T
        acc_s[1] += nn(x1t, dk)
        acc_s[2] += nn(x1t, dv)
        small_ref[ROW_V_B : ROW_V_B + 1, :] += col_sum(dv.astype(F32))
        dx1_s[...] = nt(dk, qkv_ref[:, d : 2 * d]) + nt(dv, qkv_ref[:, 2 * d :])

        @pl.when(slot == 0)
        def _():
            dq = jnp.concatenate([dq_s[img * pairs + p] for p in range(pairs)], axis=1)
            acc_s[0] += nn(x1t, dq)
            small_ref[ROW_Q_B : ROW_Q_B + 1, :] += col_sum(dq.astype(F32))
            dx1_s[...] += nt(dq, qkv_ref[:, :d])

        dx1 = dx1_s[...]
        hat = hat_s[t]
        mod_out_ref[pl.ds(img, 1), :] += col_sum(dx1)
        mod_out_ref[pl.ds(slots + img, 1), :] += col_sum(dx1 * hat)
        dx1_s[...] = norm_back(hat, inv_s[t], dx1 * (1.0 + mod_s[1, pl.ds(img, 1), :]))

        @pl.when(slot == 0)
        def _():
            dx1_s[...] += dx_s[img]

        dtok = dx1_s[...]
        small_ref[ROW_PATCH_B : ROW_PATCH_B + 1, :] += col_sum(dtok)
        hi, lo = parts(dtok, 2)
        small_ref[ROW_PATCH : ROW_PATCH + 16, :] += nn(pt_s[t], hi) + nn(pt_s[t], lo)
        edge_s[slot, img] = nt(wp_s[...], hi) + nt(wp_s[...], lo)
        return carry

    lax.fori_loop(0, slots * 4, tokens_back, 0)
    for k in range(3):
        grads_ref[2 * ff + (k + 1) * d : 2 * ff + (k + 2) * d, :] = acc_s[k].astype(BF16)

    blank = jnp.zeros((16, toks), F32)
    for i in range(slots):
        lat = shift_out([edge_s[s, i] for s in range(4)], masks)
        out = shift_out([edge_s[4, i], blank, blank, blank], masks)
        for s in range(4):
            edge_ref[s, 0, i * 16 : (i + 1) * 16, :] = lat[s]
            edge_ref[s, 1, i * 16 : (i + 1) * 16, :] = out[s]


def step(time_bin, class_label, live, planes, bias, pos_a, pos_b, *weights):
    qkv_weight, fc1_weight = weights[5], weights[7]
    d, ff = qkv_weight.shape[0], fc1_weight.shape[1]
    slots, toks = time_bin.shape[0], planes.shape[-1]
    pairs = HEADS // 2
    heads = slots * HEADS
    out_shape = (
        jax.ShapeDtypeStruct((2 * ff + 4 * d, d), BF16),
        jax.ShapeDtypeStruct((SMALL_ROWS, d), F32),
        jax.ShapeDtypeStruct((MOD_ROWS, d), F32),
        jax.ShapeDtypeStruct((4,) + planes.shape[1:], F32),
    )
    scratch = [
        ((8, 8, d), F32), ((4, toks, d), F32), ((slots * 4, 16, toks), BF16), ((slots, 16, toks), BF16),
        ((16, d), BF16), ((16, d), BF16), ((slots * 4, toks, d), BF16), ((slots * 4, toks, d), F32),
        ((slots * 4, toks, 1), F32), ((slots * pairs, 4, toks, 128), BF16), ((slots * pairs, 4, toks, 128), BF16),
        ((heads, toks, 128), BF16), ((heads, 4, toks, toks), BF16), ((4, toks, toks), F32),
        ((heads, 1, toks), F32), ((heads, 1, toks), F32), ((slots, d, toks), F32), ((slots, d, toks), BF16),
        ((slots, toks, ff), BF16), ((toks, ff), F32), ((slots, toks, ff), BF16), ((slots, toks, d), BF16),
        ((slots, d, toks), BF16), ((slots, toks, d), BF16), ((slots, toks, d), F32), ((heads, 128, toks), BF16),
        ((heads, toks, 128), BF16), ((slots * pairs, 4, toks, 128), BF16), ((slots * pairs, 4, toks, 128), BF16),
        ((slots * pairs, toks, 128), BF16), ((3, d, d), F32), ((toks, d), F32), ((5, slots, 16, toks), F32),
    ]
    return pl.pallas_call(
        step_kernel,
        out_shape=out_shape,
        in_specs=[SMEM] * 3 + [VMEM] * (4 + len(weights)),
        out_specs=(VMEM,) * 4,
        scratch_shapes=[pltpu.VMEM(shape, kind) for shape, kind in scratch],
        compiler_params=pltpu.CompilerParams(vmem_limit_bytes=64 * 1024 * 1024 - 65536),
        name="step",
    )(time_bin, class_label, live, planes, bias, pos_a, pos_b, *weights)


def axes_of(images):
    bits = max(images.bit_length() - 1, 0)
    return ("col", 0), ("row", 0), [("img", k) for k in range(bits)]


def other(axis):
    name, bit = axis
    return {name: lax.axis_index(name) ^ (1 << bit)}


def side_of(axis):
    name, bit = axis
    return (lax.axis_index(name) >> bit) & 1


def orders(images):
    col, row, img = axes_of(images)
    first, rest = img[:ROUNDS], img[ROUNDS:]
    scatter = [
        [col, row] + first,
        [col] + first[:1] + [row] + first[1:],
        [col] + first[1:] + [row] + first[:1],
    ]
    return scatter, rest


def reduce_kernel(images, grads_ref, small_ref, mod_ref, edge_ref, grads_out, small_out, mod_out, edge_out, *scratch):
    scatter, rest = orders(images)
    groups = len(scatter)
    depth = len(scatter[0])
    turns = depth + len(rest)
    col, row, img_bits = axes_of(images)
    all_axes = [col, row] + img_bits
    recv = scratch[: turns]
    work = scratch[turns : 2 * turns]
    srecv, swork, erecv, send, got, gsend, ggot, ssend, sgot, msend, mgot, esend, egot = scratch[2 * turns :]
    greet([other(a) for a in all_axes] + [mate(3)])

    rows = grads_ref.shape[0] // groups
    live = []

    def copy(src, dst, s, r, device):
        c = pltpu.make_async_remote_copy(
            src_ref=src, dst_ref=dst, send_sem=s, recv_sem=r, device_id=device, device_id_type=MESH
        )
        c.start()
        live.append(c)
        return c

    planes = [copy(edge_ref.at[s], erecv.at[s - 1], esend.at[s - 1], egot.at[s - 1], mate(s)) for s in (1, 2, 3)]

    swork[0, : small_ref.shape[0], :] = small_ref[...]
    swork[0, small_ref.shape[0] :, :] = mod_ref[...]
    cut = small_ref.shape[0]

    flight = [None] * groups
    base = [g * rows for g in range(groups)]
    inside = [jnp.int32(0)] * groups

    def view(g, k, start, many):
        if k == 0:
            return grads_ref.at[pl.ds(pl.multiple_of(base[g] + start, 16), many), :]
        return work[k - 1].at[g, pl.ds(pl.multiple_of(start, 16), many), :]

    def start_round(g, k):
        axis = (scatter[g] + rest)[k]
        if k < depth:
            many = rows >> (k + 1)
            src = view(g, k, (1 - side_of(axis)) * many, many)
        else:
            many = rows >> depth
            src = view(g, k, 0, many)
        flight[g] = copy(src, recv[k].at[g], send.at[g, k], got.at[g, k], other(axis))

    def end_round(g, k):
        axis = (scatter[g] + rest)[k]
        flight[g].wait_recv()
        if k < depth:
            many = rows >> (k + 1)
            start = side_of(axis) * many
            inside[g] = inside[g] + start
        else:
            many, start = rows >> depth, 0
        mine = view(g, k, start, many)[...]
        work[k][g] = (mine.astype(F32) + recv[k][g].astype(F32)).astype(BF16)

    small = [None]

    def start_small(k):
        axis = all_axes[k]
        if k < 2:
            small[0] = [copy(swork.at[k], srecv.at[k], ssend.at[k], sgot.at[k], other(axis))]
        else:
            b = 1 << axis[1]
            start = lax.axis_index("img") // b * b
            at = mod_out.at[pl.ds(start, b)]
            small[0] = [
                copy(swork.at[k, 0:cut], srecv.at[k, 0:cut], ssend.at[k], sgot.at[k], other(axis)),
                copy(at, at, msend.at[k], mgot.at[k], other(axis)),
            ]

    def end_small(k):
        small[0][0].wait_recv()
        if k < 2:
            swork[k + 1] = swork[k] + srecv[k]
            if k == 1:
                mod_out[pl.ds(lax.axis_index("img"), 1)] = swork[k + 1, cut:, :][None]
        else:
            small[0][1].wait_recv()
            swork[k + 1, 0:cut] = swork[k, 0:cut] + srecv[k, 0:cut]

    for k in range(max(turns, len(all_axes))):
        for g in range(groups):
            if 0 < k <= turns:
                end_round(g, k - 1)
            if k < turns:
                start_round(g, k)
        if 0 < k <= len(all_axes):
            end_small(k - 1)
        if k < len(all_axes):
            start_small(k)
    for g in range(groups):
        end_round(g, turns - 1)

    piece = rows >> depth
    offset = list(inside)
    for g in range(groups):
        at = pl.ds(pl.multiple_of(base[g] + offset[g], 16), piece)
        grads_out[at, :] = work[turns - 1][g]
    for k in range(depth):
        for g in range(groups):
            axis = scatter[g][depth - 1 - k]
            many = piece << k
            if k > 0:
                flight[g].wait_recv()
                offset[g] = offset[g] - side_of(scatter[g][depth - k]) * (many // 2)
            at = grads_out.at[pl.ds(pl.multiple_of(base[g] + offset[g], 16), many), :]
            flight[g] = copy(at, at, gsend.at[g, k], ggot.at[g, k], other(axis))
    end_small(len(all_axes) - 1)
    small_out[...] = swork[len(all_axes), 0:cut]
    for c in planes:
        c.wait_recv()
    edge_out[...] = (edge_ref[0] + erecv[1]) + (erecv[0] + erecv[2])
    for g in range(groups):
        flight[g].wait_recv()
    for c in live:
        c.wait_send()


def reduce_all(images, grads, small, mod, edge):
    scatter, rest = orders(images)
    groups, depth = len(scatter), len(scatter[0])
    turns = depth + len(rest)
    steps = 2 + len(axes_of(images)[2])
    d = grads.shape[1]
    rows = grads.shape[0] // groups
    lens = [rows >> (k + 1) for k in range(depth)] + [rows >> depth] * len(rest)
    pieces = [pltpu.VMEM((groups, n, d), BF16) for n in lens]
    dma = pltpu.SemaphoreType.DMA
    both = small.shape[0] + mod.shape[0]
    return pl.pallas_call(
        functools.partial(reduce_kernel, images),
        out_shape=(
            jax.ShapeDtypeStruct(grads.shape, BF16),
            jax.ShapeDtypeStruct(small.shape, F32),
            jax.ShapeDtypeStruct((images,) + mod.shape, F32),
            jax.ShapeDtypeStruct(edge.shape[1:], F32),
        ),
        in_specs=[VMEM] * 4,
        out_specs=(VMEM,) * 4,
        scratch_shapes=pieces
        + pieces
        + [
            pltpu.VMEM((steps, both, d), F32),
            pltpu.VMEM((steps + 1, both, d), F32),
            pltpu.VMEM((3,) + edge.shape[1:], F32),
            dma((groups, turns)),
            dma((groups, turns)),
            dma((groups, depth)),
            dma((groups, depth)),
            dma((steps,)),
            dma((steps,)),
            dma((steps,)),
            dma((steps,)),
            dma((3,)),
            dma((3,)),
        ],
        compiler_params=pltpu.CompilerParams(
            collective_id=1, has_side_effects=True, vmem_limit_bytes=56 * 1024 * 1024
        ),
        name="reduce_all",
    )(grads, small, mod, edge)


def finish_kernel(
    bins, classes, grads_ref, small_ref, mod_ref, edge_ref, ada_ref, fada_ref,
    out_ref, lat_ref, time_ref, class_ref, patch_ref, ada_g_ref, qkv_g_ref, proj_g_ref, fc1_g_ref, fc2_g_ref, fada_g_ref,
    out_g_ref, bias_ref,
):
    d = ada_ref.shape[0]
    ff = fc1_g_ref.shape[1]
    slots, chans, side, _ = lat_ref.shape
    groups = mod_ref.shape[0]
    images = groups * slots
    held = -(-images // 32) * 32

    fc2_g_ref[...] = grads_ref[0:ff, :].astype(F32)
    for b in range(ff // d):
        fc1_g_ref[:, b * d : (b + 1) * d] = grads_ref[ff + b * d : ff + (b + 1) * d, :].astype(F32)
    proj_g_ref[...] = grads_ref[2 * ff : 2 * ff + d, :].astype(F32)
    for k in range(3):
        qkv_g_ref[:, k * d : (k + 1) * d] = grads_ref[2 * ff + (k + 1) * d : 2 * ff + (k + 2) * d, :].astype(F32)

    swap = flag(iota((16, 16), 0) == (iota((16, 16), 1) ^ 3)).astype(BF16)
    total = None
    for p in parts(small_ref[ROW_PATCH : ROW_PATCH + 16, :], 3):
        term = nn(swap, p)
        total = term if total is None else total + term
    patch_ref[...] = total
    total = None
    for p in parts(small_ref[ROW_OUT : ROW_OUT + 16, :], 3):
        term = tn(p, swap)
        total = term if total is None else total + term
    out_g_ref[...] = total
    for row, at in (
        (ROW_PATCH_B, BIAS_PATCH), (ROW_Q_B, BIAS_QV), (ROW_V_B, BIAS_QV + d), (ROW_PROJ_B, BIAS_PROJ),
        (ROW_FC1_B, BIAS_FC1), (ROW_FC1_B + 1, BIAS_FC1 + d), (ROW_FC1_B + 2, BIAS_FC1 + 2 * d),
        (ROW_FC1_B + 3, BIAS_FC1 + 3 * d), (ROW_FC2_B, BIAS_FC2),
    ):
        bias_ref[:, at : at + d] = small_ref[row : row + 1, :]
    total = None
    spot = flag(iota((128, 16), 0) == (iota((128, 16), 1) ^ 3)).astype(BF16)
    tail = jnp.broadcast_to(small_ref[ROW_OUT_B : ROW_OUT_B + 1, 0:128], (8, 128))
    back = flag((iota((128, 128), 0) == (iota((128, 128), 1) ^ 3)) & (iota((128, 128), 1) < 16)).astype(BF16)
    for p in parts(tail, 3):
        term = nn(p, back)
        total = term if total is None else total + term
    bias_ref[:, BIAS_OUT : BIAS_OUT + 128] = total[0:1]

    everything = mod_ref[...].reshape(groups * MOD_ROWS, d)
    pieces = parts(everything, 3)
    out_row, src = iota((held, groups * MOD_ROWS), 0), iota((held, groups * MOD_ROWS), 1)

    def of(p):
        sel = flag(
            (out_row < images) & (src // MOD_ROWS == out_row // slots) & (src % MOD_ROWS == p * slots + out_row % slots)
        ).astype(BF16)
        return nn(sel, pieces[0]) + nn(sel, pieces[1]) + nn(sel, pieces[2])

    cond = of(8)
    sel = flag((out_row < images) & (src // MOD_ROWS == out_row // slots) & (src % MOD_ROWS == 9 * slots)).astype(BF16)
    ids = nn(sel, pieces[0]) + nn(sel, pieces[1]) + nn(sel, pieces[2])
    img_row, lane = iota((held, d), 0), iota((held, d), 1)
    time_id = jnp.sum(jnp.where(lane == img_row % slots, ids, 0.0), axis=1, keepdims=True)
    class_id = jnp.sum(jnp.where(lane == slots + img_row % slots, ids, 0.0), axis=1, keepdims=True)

    act = swish(cond)
    a1, a2, a3 = parts(act, 3)
    left = jnp.concatenate([a1, a1, a2, a2, a1, a3], axis=0).T
    dact = jnp.zeros((held, d), F32)
    for p in range(8):
        dmod = of(p)
        d1, d2, d3 = parts(dmod, 3)
        right = jnp.concatenate([d1, d2, d1, d2, d3, d1], axis=0)
        grad = nn(left, right)
        if p < 6:
            ada_g_ref[:, p * d : (p + 1) * d] = grad
            w = ada_ref[:, p * d : (p + 1) * d]
        else:
            fada_g_ref[:, (p - 6) * d : (p - 5) * d] = grad
            w = fada_ref[:, (p - 6) * d : (p - 5) * d]
        bias_ref[:, BIAS_ADA + p * d : BIAS_ADA + (p + 1) * d] = col_sum(dmod)
        m = nt(jnp.concatenate([d1, d2, d3], axis=0), w)
        dact = dact + (m[0:held] + m[held : 2 * held] + m[2 * held :])
    sig = 1.0 / (1.0 + jnp.exp(-cond))
    dcond = dact * (sig * (1.0 + cond * (1.0 - sig)))
    stack = jnp.concatenate(parts(dcond, 3), axis=0)
    for ref, ids_col, many in ((time_ref, time_id, bins), (class_ref, class_id, classes)):
        wide = -(-many // 128) * 128
        at = iota((held, wide), 1).astype(F32)
        hit = flag((at == ids_col) & (iota((held, wide), 0) < images)).astype(BF16)
        hits = jnp.concatenate([hit, hit, hit], axis=0)
        ref[...] = tn(hits, stack)[:many]

    half = side // 2
    keep, spread, pick = plane_maps(slots, chans, side, half)
    for k, ref in ((0, lat_ref), (1, out_ref)):
        total = None
        splits = parts(edge_ref[k], 3 if k == 0 else 1)
        for piece in splits:
            for j in range(2):
                wide = (tn(pick[j], piece) * keep).astype(BF16)
                term = nt(wide, spread[j])
                total = term if total is None else total + term
        ref[...] = total.reshape(ref.shape).astype(ref.dtype)


def finish(bins, classes, latents, grads, small, mod, edge, ada_weight, fada_weight, ff):
    d = ada_weight.shape[0]
    f = lambda *shape: jax.ShapeDtypeStruct(shape, F32)
    out_shape = (
        jax.ShapeDtypeStruct(latents.shape, BF16), f(*latents.shape), f(bins, d), f(classes, d), f(16, d),
        f(d, 6 * d), f(d, 3 * d), f(d, d), f(d, ff), f(ff, d), f(d, 2 * d), f(d, 16), f(1, BIAS_OUT + 128),
    )
    return pl.pallas_call(
        functools.partial(finish_kernel, bins, classes),
        out_shape=out_shape,
        in_specs=[VMEM] * 6,
        out_specs=(VMEM,) * len(out_shape),
        compiler_params=pltpu.CompilerParams(vmem_limit_bytes=60 * 1024 * 1024),
        name="finish",
    )(grads, small, mod, edge, ada_weight, fada_weight)


def local(
    images, latents, time_bin, class_label, live, time_table, class_table, patch_weight, patch_bias, ada_weight, ada_bias,
    qkv_weight, qv_bias, proj_weight, proj_bias, fc1_weight, fc1_bias, fc2_weight, fc2_bias, final_ada_weight,
    final_ada_bias, out_weight, out_bias, cotangent,
):
    d, ff = qkv_weight.shape[0], fc1_weight.shape[1]
    bins, classes = time_table.shape[0], class_table.shape[0]
    bias = jnp.concatenate(
        [patch_bias, qv_bias, proj_bias, fc1_bias, fc2_bias, ada_bias, final_ada_bias, out_bias,
         jnp.zeros((128 - out_bias.shape[0],), BF16)]
    ).astype(F32)[None]
    pos_a, pos_b = position_tables(LATENT // 2, d)
    planes = gather_planes(latents, cotangent)
    grads, small, mod, edge = step(
        time_bin, class_label, live, planes, bias, jnp.asarray(pos_a), jnp.asarray(pos_b),
        time_table, class_table, patch_weight, ada_weight, final_ada_weight, qkv_weight, proj_weight, fc1_weight,
        fc2_weight, out_weight,
    )
    grads, small, mod, edge = reduce_all(images, grads, small, mod, edge)
    (out, lat_g, time_g, class_g, patch_g, ada_g, qkv_g, proj_g, fc1_g, fc2_g, fada_g, out_g, bias_g) = finish(
        bins, classes, latents, grads, small, mod, edge, ada_weight, final_ada_weight, ff
    )
    bias_g = bias_g[0]
    return (
        out, lat_g, time_g, class_g, patch_g, bias_g[BIAS_PATCH : BIAS_PATCH + d],
        ada_g, bias_g[BIAS_ADA : BIAS_ADA + 6 * d],
        qkv_g, bias_g[BIAS_QV : BIAS_QV + 2 * d],
        proj_g, bias_g[BIAS_PROJ : BIAS_PROJ + d],
        fc1_g, bias_g[BIAS_FC1 : BIAS_FC1 + ff],
        fc2_g, bias_g[BIAS_FC2 : BIAS_FC2 + d],
        fada_g, bias_g[BIAS_ADA + 6 * d : BIAS_ADA + 8 * d],
        out_g, bias_g[BIAS_OUT : BIAS_OUT + out_bias.shape[0]],
    )


def solution(mesh):
    tiles = P("img", None, "row", "col")
    return jax.shard_map(
        functools.partial(local, mesh.shape["img"]),
        mesh=mesh,
        in_specs=(tiles,) + (P("img"),) * 3 + (P(),) * 18 + (tiles,),
        out_specs=(tiles, tiles) + (P(),) * 18,
        check_vma=False,
    )
```

```python
import functools

import jax
import jax.numpy as jnp
import numpy as np
from jax import lax
from jax.experimental import pallas as pl
from jax.experimental.pallas import tpu as pltpu
from jax.sharding import PartitionSpec as P

F32 = jnp.float32
BF16 = jnp.bfloat16
HEADS = 6
LATENT = 64
MESH = pl.DeviceIdType.MESH
VMEM = pl.BlockSpec(memory_space=pltpu.VMEM)
SMEM = pl.BlockSpec(memory_space=pltpu.SMEM)
ANY = pl.BlockSpec(memory_space=pl.ANY)


def nn(a, b):
    return lax.dot_general(a, b, (((1,), (0,)), ((), ())), preferred_element_type=F32)


def nt(a, b):
    return lax.dot_general(a, b, (((1,), (1,)), ((), ())), preferred_element_type=F32)


def tn(a, b):
    return lax.dot_general(a, b, (((0,), (0,)), ((), ())), preferred_element_type=F32)


def parts(v, many):
    out = []
    for _ in range(many):
        piece = v.astype(BF16)
        out.append(piece)
        v = v - piece.astype(F32)
    return out


def iota(shape, dim):
    return lax.broadcasted_iota(jnp.int32, shape, dim)


def flag(cond):
    return jnp.where(cond, 1.0, 0.0)


def swish(v):
    return v / (1.0 + jnp.exp(-v))


def position_tables(grid, width):
    quarter = width // 4
    omega = np.float32(1.0) / np.power(
        np.float32(10000.0), np.arange(quarter, dtype=np.float32) / np.float32(quarter)
    )
    angles = np.arange(grid, dtype=np.float32)[:, None] * omega[None, :].astype(np.float32)
    single = np.concatenate([np.sin(angles), np.cos(angles)], axis=1).astype(np.float32)
    blank = np.zeros_like(single)
    return np.concatenate([single, blank], axis=1), np.concatenate([blank, single], axis=1)


def plane_maps(slots, chans, side, halves):
    rows = slots * chans * side
    lanes = halves * halves
    spread = []
    keep = flag(iota((rows, lanes), 0) % side // 2 == iota((rows, lanes), 1) // halves)
    pick = []
    for j in range(2):
        col = iota((side, lanes), 0)
        spread.append(flag(col == iota((side, lanes), 1) % halves * 2 + j).astype(BF16))
        many = slots * chans * 4
        out, src = iota((many, rows), 0), iota((many, rows), 1)
        same = (out // 4 == src // side) & (out % 4 // 2 == src % 2) & (out % 2 == j)
        pick.append(flag(same).astype(BF16))
    return keep, spread, pick


def shift_masks(halves):
    row, lane = iota((16, halves * halves), 0), iota((16, halves * halves), 1)
    return row % 4 >= 2, row % 2 == 1, lane, halves


def shift_in(planes, masks):
    odd_row, odd_col, lane, side = masks
    full = side * side
    down = [
        jnp.where(
            odd_row,
            jnp.where(lane < side, pltpu.roll(planes[s ^ 2], side, 1), pltpu.roll(planes[s], side, 1)),
            planes[s],
        )
        for s in range(4)
    ]
    return [
        jnp.where(
            odd_col,
            jnp.where(
                lane % side == 0, pltpu.roll(down[s ^ 1], full - side + 1, 1), pltpu.roll(down[s], 1, 1)
            ),
            down[s],
        )
        for s in range(4)
    ]


def shift_out(planes, masks):
    odd_row, odd_col, lane, side = masks
    full = side * side
    up = [
        jnp.where(
            odd_row,
            jnp.where(
                lane >= full - side,
                pltpu.roll(planes[s ^ 2], full - side, 1),
                pltpu.roll(planes[s], full - side, 1),
            ),
            planes[s],
        )
        for s in range(4)
    ]
    return [
        jnp.where(
            odd_col,
            jnp.where(
                lane % side == side - 1, pltpu.roll(up[s ^ 1], side - 1, 1), pltpu.roll(up[s], full - 1, 1)
            ),
            up[s],
        )
        for s in range(4)
    ]


def mate(slot):
    row, col = lax.axis_index("row"), lax.axis_index("col")
    return {"row": row ^ (slot >> 1), "col": col ^ (slot & 1)}


def greet(devices):
    barrier = pltpu.get_barrier_semaphore()
    for device in devices:
        pl.semaphore_signal(barrier, inc=1, device_id=device, device_id_type=MESH)
    pl.semaphore_wait(barrier, len(devices))


def norm(v):
    share = 1.0 / v.shape[-1]
    centred = v - jnp.sum(v, axis=-1, keepdims=True) * share
    spread = jnp.sum(centred * centred, axis=-1, keepdims=True) * share
    inv = lax.rsqrt(spread + 1e-06)
    return centred * inv, inv


def norm_back(hat, inv, grad):
    share = 1.0 / hat.shape[-1]
    first = jnp.sum(grad, axis=-1, keepdims=True) * share
    second = jnp.sum(grad * hat, axis=-1, keepdims=True) * share
    return inv * (grad - first - hat * second)


def col_sum(v):
    return jnp.sum(v, axis=0, keepdims=True)


E_OUT, E_PROJ_B, E_FC2_B, E_Q_B, E_V_B, E_FC1_B, E_OUT_B, E_MOD, E_COND, E_IDS, E_ROWS = 0, 16, 17, 18, 19, 20, 24, 32, 50, 56, 64
L_PATCH, L_PATCH_B, L_MOD, L_ROWS = 0, 16, 18, 32


def tree(terms):
    while len(terms) > 1:
        terms = [terms[i] + terms[i + 1] for i in range(0, len(terms), 2)]
    return terms[0]


class Copies:
    def __init__(self, send_sem, recv_sem):
        self.send_sem, self.recv_sem, self.known = send_sem, recv_sem, {}

    def make(self, key, src, dst, device):
        at = self.known.setdefault(key, len(self.known))
        return pltpu.make_async_remote_copy(
            src_ref=src, dst_ref=dst, send_sem=self.send_sem.at[at], recv_sem=self.recv_sem.at[at],
            device_id=device, device_id_type=MESH,
        )


class Stage:
    def __init__(self, copies, reduce=None):
        self.copies, self.reduce = copies, reduce

    def start(self):
        for c in self.copies():
            c.start()

    def finish(self):
        for c in self.copies():
            c.wait_recv()
        if self.reduce is not None:
            self.reduce()

    def drain(self):
        for c in self.copies():
            c.wait_send()


def far(distance):
    return {"img": lax.axis_index("img") ^ distance}


def rows_at(start, many):
    return pl.ds(pl.multiple_of(start, 16), many)


def ways(images, plan):
    bits = images.bit_length() - 1
    return [way for way in plan if isinstance(way, str) or way[0] + way[1] <= bits]


def shared_bits(images, plan):
    return max([way[0] + way[1] for way in ways(images, plan) if not isinstance(way, str)] + [0])


def members(way):
    return {"col": 2, "row": 2, "four": 4}[way] if isinstance(way, str) else 1 << way[1]


def position(way):
    row, col = lax.axis_index("row"), lax.axis_index("col")
    if isinstance(way, str):
        return {"col": col, "row": row, "four": col * 2 + row}[way]
    return (lax.axis_index("img") >> way[0]) & ((1 << way[1]) - 1)


def partner(way, delta):
    row, col = lax.axis_index("row"), lax.axis_index("col")
    if way == "col":
        return {"col": 1 - col}
    if way == "row":
        return {"row": 1 - row}
    if way == "four":
        return {"row": row ^ (delta & 1), "col": col ^ (delta >> 1)}
    return far(delta << way[0])


def group_shapes(images, rows, plan):
    d, shapes = 384, []
    for way in ways(images, plan):
        many = members(way)
        rows //= many
        shapes += [(many - 1, rows, d), (rows, d)]
    high = images >> shared_bits(images, plan)
    if high > 1:
        shapes += [(high - 1, rows, d), (rows, d)]
    return shapes


def group_copies(images, plan):
    return 2 * sum(members(way) - 1 for way in ways(images, plan)) + (images >> shared_bits(images, plan)) - 1


def group_stages(name, images, base, rows, plan, grads, out, bufs, net):
    bufs = list(bufs)
    known = ways(images, plan)
    shared = shared_bits(images, plan)
    high = images >> shared

    def add(*refs):
        return tree([r.astype(F32) for r in refs]).astype(BF16)

    def scatter(k, way, held, many, got, total, last):
        count = members(way)

        def copies():
            return [
                net.make(f"{name}s{k}.{e}", held((position(way) ^ e) * many, many), got.at[e - 1], partner(way, e))
                for e in range(1, count)
            ]

        def reduce():
            total[...] = add(held(position(way) * many, many)[...], *[got[e] for e in range(count - 1)])
            if last:
                out[rows_at(base + start(len(known)), many), :] = total[...]

        return Stage(copies, reduce)

    sizes = [rows]
    for way in known:
        sizes.append(sizes[-1] // members(way))

    def start(level):
        total = 0
        for k in range(level):
            total = total + position(known[k]) * sizes[k + 1]
        return total

    stages = []

    def held(at, many):
        return grads.at[rows_at(base + at, many), :]

    for k, way in enumerate(known):
        got, total = bufs[:2]
        del bufs[:2]
        stages.append(scatter(k, way, held, sizes[k + 1], got, total, high == 1 and k == len(known) - 1))

        def held(at, many, total=total):
            return total.at[rows_at(at, many), :]

    if high > 1:
        got, final = bufs[:2]
        summed, many = total, sizes[-1]

        def copies():
            return [net.make(f"{name}h{e}", summed, got.at[e - 1], far(e << shared)) for e in range(1, high)]

        def reduce():
            final[...] = add(summed[...], *[got[e] for e in range(high - 1)])
            out[rows_at(base + start(len(known)), many), :] = final[...]

        stages.append(Stage(copies, reduce))

    def gather(k, way):
        def copies():
            at = out.at[rows_at(base + start(k + 1), sizes[k + 1]), :]
            return [net.make(f"{name}g{k}.{e}", at, at, partner(way, e)) for e in range(1, members(way))]

        return Stage(copies)

    for k in reversed(range(len(known))):
        stages.append(gather(k, known[k]))
    return stages


def sum_stages(name, images, block, got, total, out, net):
    def c0():
        return [net.make(name + "m" + str(s), block, got.at[s - 1], mate(s)) for s in (1, 2, 3)]

    def r0():
        t = tree([block[...], got[0], got[1], got[2]]).astype(BF16)
        total[...] = t
        out[lax.axis_index("img")] = t

    def c1():
        at = out.at[lax.axis_index("img")]
        return [net.make(name + "i" + str(d), total, at, far(d)) for d in range(1, images)]

    return [Stage(c0, r0), Stage(c1)]


def edge_stages(name, edge, got, out, k, net):
    def c0():
        return [net.make(name + str(s), edge.at[s], got.at[s - 1], mate(s)) for s in (1, 2, 3)]

    def r0():
        out[k] = tree([r.astype(F32) for r in (edge[0], got[1], got[0], got[2])])

    return [Stage(c0, r0)]


FF_PLANS = (("col", "row", (0, 2), (2, 1)), ("col", (0, 2), "row", (2, 1)))
PAIR_PLANS = (("col", "row", (0, 3)), ("col", (0, 2), "row", (2, 1)), ("four", (0, 3)))


def group_list(d, ff):
    base = 2 * ff
    out = [(0, ff, FF_PLANS[0]), (ff, ff, FF_PLANS[1])]
    for k in range(3):
        out.append((base + k * (d + d // 3), d + d // 3, PAIR_PLANS[k]))
    return out


def step_kernel(images, count, *refs):
    refs = list(refs)

    def take(n):
        out = refs[:n]
        del refs[:n]
        return out

    (time_ref, class_ref, live_ref, lat_ref, cot_ref, patch_b_ref, ada_b_ref, qv_b_ref, proj_b_ref, fc1_b_ref, fc2_b_ref,
     fada_b_ref, out_b_ref, pos_a_ref, pos_b_ref, patch_w_ref, out_wt_ref) = take(17)
    hbm = take(8)
    out_ref, early_out, late_out, planes_out = take(4)
    held = take(4)
    qkv_ref, proj_ref, fc1_ref, fc2_ref = held
    (planes_ref, mod_s, pt_s, gy_s, wp_s, wo_s, x1_s, x1t_s, hat_s, inv_s, k_s, v_s, q_s, e_s, sa_s, sb_s, top_s,
     linv_s, delta_s, of_s, a_s, b_s, dm_s, x2t_s, da_s, dx_s, edge_s,
     grads_ref, early_ref, late_ref, edge_y, edge_l, early_got, early_sum, late_got, late_sum, edge_y_got, edge_l_got) = take(38)
    load_sem, gather_send, gather_recv, send_sem, recv_sem = take(5)
    bufs = refs

    d = qkv_ref.shape[0]
    slots, chans, side, _ = lat_ref.shape
    toks = x1_s.shape[0]
    pairs = HEADS // 2
    ff = fc1_ref.shape[1]
    blocks = ff // d
    half = side // 2
    bins, classes = hbm[0].shape[0], hbm[1].shape[0]

    loads = [pltpu.make_async_copy(a, b, load_sem.at[4 + i]) for i, (a, b) in enumerate(zip(hbm[4:], held))]
    net = Copies(send_sem, recv_sem)
    groups = []
    for g, (base, rows, plan) in enumerate(group_list(d, ff)):
        n = len(group_shapes(images, rows, plan))
        groups.append(group_stages("g" + str(g), images, base, rows, plan, grads_ref, out_ref, bufs[:n], net))
        del bufs[:n]
    groups.append(sum_stages("e", images, early_ref, early_got, early_sum, early_out, net))
    groups.append(sum_stages("l", images, late_ref, late_got, late_sum, late_out, net))
    groups.append(edge_stages("y", edge_y, edge_y_got, planes_out, 1, net))
    groups.append(edge_stages("x", edge_l, edge_l_got, planes_out, 0, net))
    FC2, FC1, PAIR, EARLY, LATE, EDGE_Y, EDGE_L = 0, 1, 2, 5, 6, 7, 8

    def advance(g, k):
        if k > 0:
            groups[g][k - 1].finish()
        if k < len(groups[g]):
            groups[g][k].start()

    def row_of(ref, start, many):
        return ref[...].astype(F32).reshape(1, ref.shape[0])[:, start : start + many]

    early_ref[...] = jnp.zeros_like(early_ref)
    late_ref[...] = jnp.zeros_like(late_ref)

    swap = flag(iota((16, 16), 0) == (iota((16, 16), 1) ^ 3)).astype(BF16)
    wp_s[...] = nn(swap, patch_w_ref[...]).astype(BF16)
    wo_s[...] = nn(swap, out_wt_ref[...]).astype(BF16)
    out_bias = jnp.sum(
        flag(iota((16, 16), 1) == (iota((16, 16), 0) ^ 3)) * row_of(out_b_ref, 0, 16), axis=1, keepdims=True
    )

    inv_lane = iota((toks, 128), 1)

    def opening(time_table_ref, class_table_ref, ada_ref, fada_ref, pos_s):
        tables = [
            pltpu.make_async_copy(a, b, load_sem.at[i])
            for i, (a, b) in enumerate(zip(hbm[:4], (time_table_ref, class_table_ref, ada_ref, fada_ref)))
        ]
        for c in tables + loads:
            c.start()
        greet([mate(s) for s in (1, 2, 3)] + [far(k) for k in range(1, images)])
        keep, spread, pick = plane_maps(slots, chans, side, half)
        for k, ref in enumerate((lat_ref, cot_ref)):
            tile = ref[...].reshape(slots * chans * side, side)
            total = None
            for j in range(2):
                wide = (nn(tile, spread[j]) * keep).astype(BF16)
                term = nn(pick[j], wide)
                total = term if total is None else total + term
            planes_ref[0, k] = total.astype(BF16)
        gathers = []
        for s in (1, 2, 3):
            c = pltpu.make_async_remote_copy(
                src_ref=planes_ref.at[0], dst_ref=planes_ref.at[s], send_sem=gather_send.at[s - 1], recv_sem=gather_recv.at[s - 1],
                device_id=mate(s), device_id_type=MESH,
            )
            c.start()
            gathers.append(c)

        my_row, my_col = lax.axis_index("row"), lax.axis_index("col")
        patch_b = row_of(patch_b_ref, 0, d)
        for s in range(4):
            ta = pos_a_ref[pl.ds(pl.multiple_of((my_row ^ (s >> 1)) * half, half), half), :]
            tb = pos_b_ref[pl.ds(pl.multiple_of((my_col ^ (s & 1)) * half, half), half), :] + patch_b
            for a in range(half):
                pos_s[s, a * half : (a + 1) * half, :] = ta[a : a + 1, :] + tb

        def onehot(ids_ref, many):
            row, lane = iota((16, many), 0), iota((16, many), 1)
            hit = jnp.zeros((16, many), F32)
            for i in range(slots):
                hit = hit + flag((row == i) & (lane == ids_ref[i]))
            return hit.astype(BF16)

        for c in tables:
            c.wait()
        cond = nn(onehot(time_ref, bins), time_table_ref[...]) + nn(onehot(class_ref, classes), class_table_ref[...])
        cond = cond[:8]
        act = parts(swish(cond), 3)
        act = jnp.concatenate([p.astype(F32) for p in act] + [jnp.zeros((8, d), F32)], axis=0).astype(BF16)
        for p in range(8):
            w = ada_ref[:, p * d : (p + 1) * d] if p < 6 else fada_ref[:, (p - 6) * d : (p - 5) * d]
            m = nn(act, w)
            b = row_of(ada_b_ref, p * d, d) if p < 6 else row_of(fada_b_ref, (p - 6) * d, d)
            mod_s[p] = m[0:8] + m[8:16] + m[16:24] + b
        row, lane = iota((8, d), 0), iota((8, d), 1)
        ids = jnp.zeros((8, d), F32)
        for i in range(slots):
            for k, v in enumerate((time_ref[i], class_ref[i] // 256, class_ref[i] % 256)):
                ids = ids + jnp.where((row == 0) & (lane == k * slots + i), 0.25 * v.astype(F32), 0.0)
        high = cond.astype(BF16).astype(F32)
        early_ref[E_COND : E_COND + slots, :] = 0.25 * high[:slots]
        early_ref[E_COND + slots : E_COND + 2 * slots, :] = 0.25 * (cond - high)[:slots]
        early_ref[E_IDS : E_IDS + 1, :] = ids[0:1]

        for c in gathers:
            c.wait_recv()
        masks = shift_masks(half)
        live = [live_ref[i].astype(F32) for i in range(slots)]
        for i in range(slots):
            lat = shift_in([planes_ref[s, 0, i * 16 : (i + 1) * 16, :].astype(F32) for s in range(4)], masks)
            cot = shift_in([planes_ref[s, 1, i * 16 : (i + 1) * 16, :].astype(F32) for s in range(4)], masks)
            for s in range(4):
                pt_s[i * 4 + s] = lat[s].astype(BF16)
            gy_s[i] = (cot[0] * live[i]).astype(BF16)

        v_bias = row_of(qv_b_ref, d, d)

        def token_norm(t):
            img, slot = t // 4, t % 4
            tok = tn(pt_s[t], wp_s[...]) + pos_s[slot]
            dx_s[img] = tok
            hat, inv = norm(tok)
            hat_s[t] = hat
            inv_s[...] = jnp.where(inv_lane == t, inv, inv_s[...])
            x1_s[...] = (hat * (1.0 + mod_s[1, pl.ds(img, 1), :]) + mod_s[0, pl.ds(img, 1), :]).astype(BF16)

        token_norm(jnp.int32(3))
        loads[0].wait()

        def reverse(n):
            return n // 4 * 4 + 3 - n % 4

        def tokens(n, carry):
            t = reverse(n)
            img, slot = t // 4, t % 4
            x1 = x1_s[...]
            x1t_s[t] = x1.T
            keys = nn(x1, qkv_ref[:, d : 2 * d]).astype(BF16)
            vals = (nn(x1, qkv_ref[:, 2 * d :]) + v_bias).astype(BF16)
            for p in range(pairs):
                k_s[img * pairs + p, slot] = keys[:, p * 128 : (p + 1) * 128]
                v_s[img * pairs + p, slot] = vals[:, p * 128 : (p + 1) * 128]
            token_norm(reverse(jnp.minimum(n + 1, slots * 4 - 1)))
            return carry

        lax.fori_loop(0, slots * 4, tokens, 0)

        for c in gathers:
            c.wait_send()

    pl.run_scoped(
        opening,
        *[pltpu.VMEM(hbm[i].shape, BF16) for i in range(4)],
        pltpu.VMEM((4, toks, d), F32),
    )
    masks = shift_masks(half)

    lane128 = iota((1, 128), 1) // 64
    head_mask = [flag(lane128 == h) for h in range(2)]

    q_bias = row_of(qv_b_ref, 0, d)

    def queries(img, carry):
        query = tn(x1t_s[img * 4], qkv_ref[:, :d]) + q_bias
        query = query.astype(BF16).astype(F32) * 0.125
        for p in range(pairs):
            for h in range(2):
                q_s[img * HEADS + p * 2 + h] = (query[:, p * 128 : (p + 1) * 128] * head_mask[h]).astype(BF16)
        return carry

    lax.fori_loop(0, slots, queries, 0)

    def scores(idx, h, buf):
        top = None
        for c in range(4):
            s = nt(k_s[idx, c], q_s[idx * 2 + h])
            buf[2 * c] = s[:, :128]
            buf[2 * c + 1] = s[:, 128:]
            m = jnp.max(s, axis=0, keepdims=True)
            top = m if top is None else jnp.maximum(top, m)
        top_s[h] = top

    def softmax(idx, h, buf, vt):
        head = idx * 2 + h
        top, total, acc = top_s[h], None, None
        for c in range(4):
            e = jnp.exp(jnp.concatenate([buf[2 * c], buf[2 * c + 1]], axis=1) - top)
            l = col_sum(e)
            total = l if total is None else total + l
            eb = e.astype(BF16)
            e_s[head, c] = eb
            o = nn(vt[c][h * 64 : (h + 1) * 64], eb)
            acc = o if acc is None else acc + o
        linv = 1.0 / total
        linv_s[head] = linv
        of_s[head] = acc * linv

    scores(jnp.int32(0), 0, sa_s)

    def attend(idx, carry):
        vt = [v_s[idx, c].T for c in range(4)]
        scores(idx, 1, sb_s)
        softmax(idx, 0, sa_s, vt)
        scores(jnp.minimum(idx + 1, slots * pairs - 1), 0, sa_s)
        softmax(idx, 1, sb_s, vt)
        return carry

    lax.fori_loop(0, slots * pairs, attend, 0)
    for c in loads[1:]:
        c.wait()
    proj_b, fc1_b, fc2_b = row_of(proj_b_ref, 0, d), row_of(fc1_b_ref, 0, ff), row_of(fc2_b_ref, 0, d)

    def slope_at(j):
        return sa_s.at[j] if j < 8 else sb_s.at[j - 8]

    def closing(dot_s, dom_s, dq_s, dxq_s, acc_s, dx1_s):
        def image(img, carry):
            def mod_row(p):
                return mod_s[p, pl.ds(img, 1), :]

            ot = jnp.concatenate([of_s[img * HEADS + h] for h in range(HEADS)], axis=0).astype(BF16)
            branch = tn(ot, proj_ref[...]) + proj_b
            g1 = mod_row(2)
            resid = dx_s[img] + g1 * branch
            hat2, inv2 = norm(resid)
            x2 = (hat2 * (1.0 + mod_row(4)) + mod_row(3)).astype(BF16)
            x2t_s[img] = x2.T
            mlp = jnp.zeros((toks, d), F32)
            k0, k1 = 0.7978845608028654, 0.044715
            for b in range(blocks):
                at_b = slice(b * d, (b + 1) * d)
                u = nn(x2, fc1_ref[:, at_b]) + fc1_b[:, at_b]
                sq = u * u
                cdf = 0.5 + 0.5 * jnp.tanh(u * (k0 + (k0 * k1) * sq))
                hidden = u * cdf
                slope = cdf + hidden * (1.0 - cdf) * ((2.0 * k0) + (6.0 * k0 * k1) * sq)
                for j in range(3):
                    slope_at(b * 3 + j)[...] = slope[:, j * 128 : (j + 1) * 128]
                hidden = hidden.astype(BF16)
                for j in range(3):
                    a_s[img * 12 + b * 3 + j] = hidden[:, j * 128 : (j + 1) * 128]
                mlp = mlp + nn(hidden, fc2_ref[at_b, :])
            mlp = mlp + fc2_b
            g2 = mod_row(5)
            x3 = resid + g2 * mlp
            hatf, invf = norm(x3)
            scf = 1.0 + mod_row(7)
            xf = (hatf * scf + mod_row(6)).astype(BF16)
            edge_s[4, img] = (nt(wo_s[...], xf) + out_bias) * live_ref[img].astype(F32)
            gy = gy_s[img]
            early_ref[E_OUT : E_OUT + 16, :] += nn(gy, xf)
            early_ref[E_OUT_B : E_OUT_B + 1, 0:16] += nt(jnp.ones((8, toks), BF16), gy)[0:1]
            dxf = tn(gy, wo_s[...])

            def put_mod(p, v):
                early_ref[pl.ds(E_MOD + (p - 2) * slots + img, 1), :] = v

            put_mod(6, col_sum(dxf))
            put_mod(7, col_sum(dxf * hatf))
            dx3 = norm_back(hatf, invf, dxf * scf)
            dm = (g2 * dx3).astype(BF16)
            dm_s[img] = dm
            put_mod(5, col_sum(mlp * dx3))
            early_ref[E_FC2_B : E_FC2_B + 1, :] += col_sum(dm.astype(F32))
            dx2 = jnp.zeros((toks, d), F32)
            for b in range(blocks):
                at_b = slice(b * d, (b + 1) * d)
                slope = jnp.concatenate([slope_at(b * 3 + j)[...] for j in range(3)], axis=1)
                du = (nt(dm, fc2_ref[at_b, :]) * slope).astype(BF16)
                for j in range(3):
                    b_s[img * 12 + b * 3 + j] = du[:, j * 128 : (j + 1) * 128]
                early_ref[E_FC1_B + b : E_FC1_B + b + 1, :] += col_sum(du.astype(F32))
                dx2 = dx2 + nt(du, fc1_ref[:, at_b])
            put_mod(3, col_sum(dx2))
            put_mod(4, col_sum(dx2 * hat2))
            dx = dx3 + norm_back(hat2, inv2, dx2 * (1.0 + mod_row(4)))
            dx_s[img] = dx
            put_mod(2, col_sum(branch * dx))
            da = (g1 * dx).astype(BF16)
            da_s[img] = da
            early_ref[E_PROJ_B : E_PROJ_B + 1, :] += col_sum(da.astype(F32))
            dot = nt(proj_ref[...], da)
            blank = jnp.zeros((64, toks), F32)
            for hd in range(HEADS):
                head = img * HEADS + hd
                piece = dot[hd * 64 : (hd + 1) * 64]
                linv = linv_s[head]
                delta_s[head] = col_sum(piece * of_s[head]) * linv
                piece = piece * linv
                wide = jnp.concatenate([piece, blank] if hd % 2 == 0 else [blank, piece], axis=0).astype(BF16)
                dot_s[head] = wide
                dom_s[head] = wide.T
            return carry

        lax.fori_loop(0, slots, image, 0)

        def pair_row(k):
            return 2 * ff + k * (d + d // 3)

        def wide(ref, img, b):
            return jnp.concatenate([ref[img * 12 + b * 3 + j] for j in range(3)], axis=1)

        def fc2_grad(b, carry):
            total = tree([tn(wide(a_s, img, b), dm_s[img]) for img in range(2)])
            for img in range(2, slots):
                total = total + tn(wide(a_s, img, b), dm_s[img])
            grads_ref[rows_at(b * d, d), :] = total.astype(BF16)
            return carry

        def fc1_grad(b, carry):
            total = tree([nn(x2t_s[img], wide(b_s, img, b)) for img in range(2)])
            for img in range(2, slots):
                total = total + nn(x2t_s[img], wide(b_s, img, b))
            grads_ref[rows_at(ff + b * d, d), :] = total.astype(BF16)
            return carry

        lax.fori_loop(0, blocks, fc2_grad, 0)
        advance(FC2, 0)
        lax.fori_loop(0, blocks, fc1_grad, 0)
        advance(FC1, 0)
        total = None
        for img in range(slots):
            ot = jnp.concatenate([of_s[img * HEADS + h] for h in range(HEADS)], axis=0).astype(BF16)
            term = nn(ot, da_s[img])
            total = term if total is None else total + term
        for k in range(pairs):
            grads_ref[pair_row(k) + d : pair_row(k + 1), :] = total[k * (d // 3) : (k + 1) * (d // 3)].astype(BF16)
        blank = jnp.zeros((16, toks), F32)
        for i in range(slots):
            out = shift_out([edge_s[4, i], blank, blank, blank], masks)
            for s in range(4):
                edge_y[s, i * 16 : (i + 1) * 16, :] = out[s].astype(BF16)
        advance(EDGE_Y, 0)

        def when_at(i, plan):
            for at, events in plan.items():

                @pl.when(i == at)
                def _():
                    for g, k in events:
                        advance(g, k)

        back_plan, tail_plan = {}, {}

        def place(plan, at, g, k):
            plan.setdefault(at, []).append((g, k))

        deep = len(groups[FC2])
        for k in range(1, deep + 1):
            place(back_plan, k, FC2, k)
            place(back_plan, k, FC1, k)
        place(back_plan, 1, EDGE_Y, 1)
        for pair in range(pairs):
            for k in range(1, len(groups[PAIR + pair]) + 1):
                place(tail_plan, min(11, 2 * k - 1), PAIR + pair, k)
        place(tail_plan, 4, EARLY, 1)
        place(tail_plan, 8, EARLY, 2)

        acc_s[...] = jnp.zeros_like(acc_s)

        def attend_back(it, carry):
            when_at(it, back_plan)
            p, img = it // slots, it % slots
            idx = img * pairs + p
            dqt = [None, None]
            jobs = [(c, h) for c in range(4) for h in range(2)]

            def product(job):
                return nn(v_s[idx, job[0]], dot_s[idx * 2 + job[1]])

            dp = product(jobs[0])
            gathered = None
            sum_v = None
            for n, (c, h) in enumerate(jobs):
                head = idx * 2 + h
                ahead = product(jobs[n + 1]) if n + 1 < len(jobs) else None
                if h == 0:
                    kt = k_s[idx, c].T
                    dk, dv = None, None
                e = e_s[head, c]
                ds = (e.astype(F32) * (dp - delta_s[head])).astype(BF16)
                dk_h, dv_h = nn(ds, q_s[head]), nn(e, dom_s[head])
                dk = dk_h if dk is None else dk + dk_h
                dv = dv_h if dv is None else dv + dv_h
                dq_h = nn(kt[h * 64 : (h + 1) * 64], ds)
                dqt[h] = dq_h if dqt[h] is None else dqt[h] + dq_h
                dp = ahead
                if h == 1:
                    dk, dv = dk.astype(BF16), dv.astype(BF16)
                    a_s[idx * 4 + c] = dk
                    b_s[idx * 4 + c] = dv
                    sv = col_sum(dv.astype(F32))
                    sum_v = sv if sum_v is None else sum_v + sv
                    term = nn(x1t_s[img * 4 + c], jnp.concatenate([dk, dv], axis=1))
                    gathered = term if gathered is None else gathered + term
            dq = (jnp.concatenate(dqt, axis=0) * 0.125).T.astype(BF16)
            dq_s[idx] = dq
            lanes = pl.ds(pl.multiple_of(p * 128, 128), 128)
            early_ref[E_V_B : E_V_B + 1, lanes] += sum_v
            early_ref[E_Q_B : E_Q_B + 1, lanes] += col_sum(dq.astype(F32))
            acc_s[:, 128:] += gathered
            acc_s[:, :128] += nn(x1t_s[img * 4], dq)

            for pair in range(pairs):

                @pl.when(it == pair * slots + slots - 1)
                def _():
                    at = pair_row(pair)
                    grads_ref[at : at + d, :] = acc_s[...].astype(BF16)
                    acc_s[...] = jnp.zeros_like(acc_s)
                    advance(PAIR + pair, 0)

            return carry

        lax.fori_loop(0, slots * pairs, attend_back, 0)
        advance(EARLY, 0)

        def joined(ref, img, slot):
            return [ref[(img * pairs + p) * 4 + slot] for p in range(pairs)]

        def query_back(img, carry):
            dq = jnp.concatenate([dq_s[img * pairs + p] for p in range(pairs)], axis=1)
            dxq_s[img] = nt(dq, qkv_ref[:, :d])
            return carry

        lax.fori_loop(0, slots, query_back, 0)

        def product_back(t):
            img, slot = t // 4, t % 4
            dkv = jnp.concatenate(joined(a_s, img, slot) + joined(b_s, img, slot), axis=1)
            own = jnp.where(slot == 0, 1.0, 0.0)
            return nt(dkv, qkv_ref[:, d:]) + dxq_s[img] * own

        dx1_s[...] = product_back(jnp.int32(0))
        def tokens_back(t, carry):
            when_at(t, tail_plan)
            img, slot = t // 4, t % 4
            dx1 = dx1_s[...]
            ahead = product_back(jnp.minimum(t + 1, slots * 4 - 1))
            hat = hat_s[t]
            late_ref[pl.ds(L_MOD + img, 1), :] += col_sum(dx1)
            late_ref[pl.ds(L_MOD + slots + img, 1), :] += col_sum(dx1 * hat)
            own = jnp.where(slot == 0, 1.0, 0.0)
            dtok = norm_back(hat, jnp.sum(jnp.where(inv_lane == t, inv_s[...], 0.0), axis=1, keepdims=True), dx1 * (1.0 + mod_s[1, pl.ds(img, 1), :])) + dx_s[img] * own
            late_ref[L_PATCH_B : L_PATCH_B + 1, :] += col_sum(dtok)
            hi, lo = parts(dtok, 2)
            late_ref[L_PATCH : L_PATCH + 16, :] += nn(pt_s[t], hi) + nn(pt_s[t], lo)
            edge_s[slot, img] = nt(wp_s[...], hi) + nt(wp_s[...], lo)
            dx1_s[...] = ahead
            return carry

        lax.fori_loop(0, slots * 4, tokens_back, 0)

    pl.run_scoped(
        closing,
        pltpu.VMEM((slots * HEADS, 128, toks), BF16),
        pltpu.VMEM((slots * HEADS, toks, 128), BF16),
        pltpu.VMEM((slots * pairs, toks, 128), BF16),
        pltpu.VMEM((slots, toks, d), F32),
        pltpu.VMEM((d, d), F32),
        pltpu.VMEM((toks, d), F32),
    )

    advance(LATE, 0)
    for i in range(slots):
        lat = shift_out([edge_s[s, i] for s in range(4)], masks)
        for s in range(4):
            edge_l[s, i * 16 : (i + 1) * 16, :] = lat[s].astype(BF16)
    advance(EDGE_L, 0)
    advance(LATE, 1)
    advance(EDGE_L, 1)
    advance(LATE, 2)
    for stages in groups:
        for stage in stages:
            stage.drain()
    assert len(net.known) <= count


def step(images, smalls, bigs):
    time_bin, latents = smalls[0], smalls[3]
    qkv_weight, fc1_weight = bigs[4], bigs[6]
    d, ff = qkv_weight.shape[0], fc1_weight.shape[1]
    slots, chans, side, _ = latents.shape
    toks = side * side // 4
    planes = slots * chans * 4
    pairs = HEADS // 2
    heads = slots * HEADS
    out_shape = (
        jax.ShapeDtypeStruct((2 * ff + 4 * d, d), BF16),
        jax.ShapeDtypeStruct((images, E_ROWS, d), BF16),
        jax.ShapeDtypeStruct((images, L_ROWS, d), BF16),
        jax.ShapeDtypeStruct((2, planes, toks), F32),
    )
    scratch = [(w.shape, w.dtype) for w in bigs[4:]] + [
        ((4, 2, planes, toks), BF16), ((8, 8, d), F32), ((slots * 4, 16, toks), BF16),
        ((slots, 16, toks), BF16), ((16, d), BF16), ((16, d), BF16), ((toks, d), BF16), ((slots * 4, d, toks), BF16),
        ((slots * 4, toks, d), F32), ((toks, 128), F32), ((slots * pairs, 4, toks, 128), BF16),
        ((slots * pairs, 4, toks, 128), BF16), ((heads, toks, 128), BF16), ((heads, 4, toks, toks), BF16),
        ((8, toks, 128), F32), ((8, toks, 128), F32), ((2, 1, toks), F32), ((heads, 1, toks), F32), ((heads, 1, toks), F32),
        ((heads, 64, toks), F32), ((slots * 12, toks, 128), BF16), ((slots * 12, toks, 128), BF16),
        ((slots, toks, d), BF16), ((slots, d, toks), BF16), ((slots, toks, d), BF16),
        ((slots, toks, d), F32), ((5, slots, 16, toks), F32),
        ((2 * ff + 4 * d, d), BF16), ((E_ROWS, d), F32), ((L_ROWS, d), F32), ((4, planes, toks), BF16), ((4, planes, toks), BF16),
        ((3, E_ROWS, d), F32), ((E_ROWS, d), BF16), ((3, L_ROWS, d), F32), ((L_ROWS, d), BF16), ((3, planes, toks), BF16),
        ((3, planes, toks), BF16),
    ]
    dma = pltpu.SemaphoreType.DMA
    parts_of = group_list(d, ff)
    count = sum(group_copies(images, plan) for _, _, plan in parts_of) + 2 * (3 + images - 1) + 6
    moved = [(s, BF16) for _, rows, plan in parts_of for s in group_shapes(images, rows, plan)]
    return pl.pallas_call(
        functools.partial(step_kernel, images, count),
        out_shape=out_shape,
        in_specs=[SMEM] * 3 + [VMEM] * (len(smalls) - 3) + [ANY] * len(bigs),
        out_specs=(VMEM,) * 4,
        scratch_shapes=[pltpu.VMEM(shape, kind) for shape, kind in scratch]
        + [dma((len(bigs),)), dma((3,)), dma((3,)), dma((count,)), dma((count,))]
        + [pltpu.VMEM(shape, kind) for shape, kind in moved],
        compiler_params=pltpu.CompilerParams(
            collective_id=0, has_side_effects=True, vmem_limit_bytes=64 * 1024 * 1024 - 65536
        ),
        name="step",
    )(*smalls, *bigs)


def finish_kernel(
    bins, classes, grads_hbm, early_ref, late_ref, planes_ref, ada_hbm, fada_hbm,
    out_ref, lat_ref, time_ref, class_hbm, patch_ref, patch_b_ref, ada_g_hbm, ada_b_ref, qkv_g_hbm, qv_b_ref, proj_g_ref,
    proj_b_ref, fc1_g_hbm, fc1_b_ref, fc2_g_hbm, fc2_b_ref, fada_g_hbm, fada_b_ref, out_gt_ref, out_b_ref,
    grads_ref, ada_ref, fada_ref, class_ref, ada_g_ref, qkv_g_ref, fc1_g_ref, fc2_g_ref, fada_g_ref, in_sem, out_sem,
):
    d = ada_ref.shape[0]
    ff = fc1_g_ref.shape[1]
    blocks = ff // d
    pairs = HEADS // 2
    slots, chans, side, _ = lat_ref.shape
    groups = early_ref.shape[0]
    images = groups * slots
    held = -(-images // 32) * 32

    bounds = [0, ff, 2 * ff, 2 * ff + 4 * d]
    loads = [
        pltpu.make_async_copy(grads_hbm.at[a:b, :], grads_ref.at[a:b, :], in_sem.at[i])
        for i, (a, b) in enumerate(zip(bounds[:-1], bounds[1:]))
    ]
    loads += [pltpu.make_async_copy(ada_hbm, ada_ref, in_sem.at[3]), pltpu.make_async_copy(fada_hbm, fada_ref, in_sem.at[4])]
    for c in loads:
        c.start()
    stores = []

    def send(src, dst):
        c = pltpu.make_async_copy(src, dst, out_sem.at[len(stores)])
        c.start()
        stores.append(c)

    loads[0].wait()
    fc2_g_ref[...] = grads_ref[0:ff, :].astype(F32)
    send(fc2_g_ref, fc2_g_hbm)
    loads[1].wait()
    for b in range(blocks):
        fc1_g_ref[:, b * d : (b + 1) * d] = grads_ref[ff + b * d : ff + (b + 1) * d, :].astype(F32)
    send(fc1_g_ref, fc1_g_hbm)
    loads[2].wait()
    third = d // 3
    for p in range(pairs):
        at = 2 * ff + p * (d + third)
        proj_g_ref[p * third : (p + 1) * third, :] = grads_ref[at + d : at + d + third, :].astype(F32)
        for k in range(3):
            lanes = slice(k * d + p * 128, k * d + (p + 1) * 128)
            qkv_g_ref[:, lanes] = grads_ref[at : at + d, k * 128 : (k + 1) * 128].astype(F32)
    send(qkv_g_ref, qkv_g_hbm)

    all_early = early_ref[...].reshape(groups * E_ROWS, d)
    all_late = late_ref[...].reshape(groups * L_ROWS, d)

    def chosen(block, rows, at):
        out_row, src = iota((held, groups * rows), 0), iota((held, groups * rows), 1)
        sel = (out_row < images) & (src // rows == out_row // slots) & (src % rows == at(out_row % slots))
        return nn(flag(sel).astype(BF16), block)

    cond = chosen(all_early, E_ROWS, lambda i: E_COND + i) + chosen(all_early, E_ROWS, lambda i: E_COND + slots + i)
    ids = chosen(all_early, E_ROWS, lambda i: E_IDS)
    img_row, lane = iota((held, d), 0), iota((held, d), 1)

    def id_part(k):
        return jnp.sum(jnp.where(lane == k * slots + img_row % slots, ids, 0.0), axis=1, keepdims=True)

    time_id, class_id = id_part(0), 256.0 * id_part(1) + id_part(2)

    a1, a2, a3 = parts(swish(cond), 3)
    left = jnp.concatenate([a1, a2, a3], axis=0).T
    loads[3].wait()
    loads[4].wait()
    dact = jnp.zeros((held, d), F32)
    bias_rows = []
    for p in range(8):
        if p < 2:
            dmod = chosen(all_late, L_ROWS, lambda i: L_MOD + p * slots + i)
        else:
            dmod = chosen(all_early, E_ROWS, lambda i: E_MOD + (p - 2) * slots + i)
        dmod16 = dmod.astype(BF16)
        grad = nn(left, jnp.concatenate([dmod16] * 3, axis=0))
        if p < 6:
            ada_g_ref[:, p * d : (p + 1) * d] = grad
            w = ada_ref[:, p * d : (p + 1) * d]
        else:
            fada_g_ref[:, (p - 6) * d : (p - 5) * d] = grad
            w = fada_ref[:, (p - 6) * d : (p - 5) * d]
        bias_rows.append(col_sum(dmod))
        dact = dact + nt(dmod16, w)
        if p == 5:
            send(ada_g_ref, ada_g_hbm)
    send(fada_g_ref, fada_g_hbm)
    ada_b_ref[...] = jnp.concatenate(bias_rows[:6], axis=1).reshape(6 * d)
    fada_b_ref[...] = jnp.concatenate(bias_rows[6:], axis=1).reshape(2 * d)
    sig = 1.0 / (1.0 + jnp.exp(-cond))
    dcond = dact * (sig * (1.0 + cond * (1.0 - sig)))
    stack = jnp.concatenate(parts(dcond, 3), axis=0)
    for ref, ids_col, many in ((class_ref, class_id, classes), (time_ref, time_id, bins)):
        wide = -(-many // 128) * 128
        at = iota((held, wide), 1).astype(F32)
        hit = flag((at == ids_col) & (iota((held, wide), 0) < images)).astype(BF16)
        ref[...] = tn(jnp.concatenate([hit, hit, hit], axis=0), stack)[:many]
        if many == classes:
            send(class_ref, class_hbm)

    early, late = jnp.sum(early_ref[...].astype(F32), axis=0), jnp.sum(late_ref[...].astype(F32), axis=0)
    swap = flag(iota((16, 16), 0) == (iota((16, 16), 1) ^ 3)).astype(BF16)

    def swapped(v):
        return tree([nn(swap, p) for p in parts(v, 2)] + [nn(swap, parts(v, 3)[2]), jnp.zeros_like(v)])

    patch_ref[...] = swapped(late[L_PATCH : L_PATCH + 16])
    out_gt_ref[...] = swapped(early[E_OUT : E_OUT + 16])

    def line(v, row):
        return v[row : row + 1, :]

    patch_b_ref[...] = line(late, L_PATCH_B).reshape(d)
    qv_b_ref[...] = jnp.concatenate([line(early, E_Q_B), line(early, E_V_B)], axis=1).reshape(2 * d)
    proj_b_ref[...] = line(early, E_PROJ_B).reshape(d)
    fc1_b_ref[...] = jnp.concatenate([line(early, E_FC1_B + b) for b in range(blocks)], axis=1).reshape(ff)
    fc2_b_ref[...] = line(early, E_FC2_B).reshape(d)
    tail = jnp.broadcast_to(line(early, E_OUT_B)[:, 0:16], (16, 16))
    pick = flag(iota((16, 16), 1) == (iota((16, 16), 0) ^ 3))
    column = jnp.sum(tail * pick, axis=1, keepdims=True)
    out_b_ref[...] = col_sum(jnp.where(iota((16, 16), 0) == iota((16, 16), 1), column, 0.0)).reshape(16)

    half = side // 2
    keep, spread, pick = plane_maps(slots, chans, side, half)
    for k, ref in ((0, lat_ref), (1, out_ref)):
        total = None
        for piece in parts(planes_ref[k], 3 if k == 0 else 1):
            for j in range(2):
                wide = (tn(pick[j], piece) * keep).astype(BF16)
                term = nt(wide, spread[j])
                total = term if total is None else total + term
        ref[...] = total.reshape(ref.shape).astype(ref.dtype)
    for c in stores:
        c.wait()


def finish(bins, classes, latents, grads, early, late, planes, ada_weight, fada_weight, ff):
    d = ada_weight.shape[0]
    f = lambda *shape: jax.ShapeDtypeStruct(shape, F32)
    out_shape = (
        jax.ShapeDtypeStruct(latents.shape, BF16), f(*latents.shape), f(bins, d), f(classes, d), f(16, d), f(d),
        f(d, 6 * d), f(6 * d), f(d, 3 * d), f(2 * d), f(d, d), f(d), f(d, ff), f(ff), f(ff, d), f(d), f(d, 2 * d), f(2 * d),
        f(16, d), f(16),
    )
    large = (3, 6, 8, 12, 14, 16)
    dma = pltpu.SemaphoreType.DMA
    return pl.pallas_call(
        functools.partial(finish_kernel, bins, classes),
        out_shape=out_shape,
        in_specs=[ANY] + [VMEM] * 3 + [ANY] * 2,
        out_specs=tuple(ANY if i in large else VMEM for i in range(len(out_shape))),
        scratch_shapes=[pltpu.VMEM(x.shape, x.dtype) for x in (grads, ada_weight, fada_weight)]
        + [pltpu.VMEM(out_shape[i].shape, F32) for i in large]
        + [dma((5,)), dma((len(large),))],
        compiler_params=pltpu.CompilerParams(vmem_limit_bytes=60 * 1024 * 1024),
        name="finish",
    )(grads, early, late, planes, ada_weight, fada_weight)


def local(
    images, latents, time_bin, class_label, live, time_table, class_table, patch_weight, patch_bias, ada_weight, ada_bias,
    qkv_weight, qv_bias, proj_weight, proj_bias, fc1_weight, fc1_bias, fc2_weight, fc2_bias, final_ada_weight,
    final_ada_bias, out_weight, out_bias, cotangent,
):
    d, ff = qkv_weight.shape[0], fc1_weight.shape[1]
    pos_a, pos_b = position_tables(LATENT // 2, d)
    smalls = (
        time_bin, class_label, live, latents, cotangent, patch_bias, ada_bias, qv_bias, proj_bias, fc1_bias, fc2_bias,
        final_ada_bias, out_bias, jnp.asarray(pos_a), jnp.asarray(pos_b), patch_weight, out_weight.T,
    )
    bigs = (time_table, class_table, ada_weight, final_ada_weight, qkv_weight, proj_weight, fc1_weight, fc2_weight)
    grads, early, late, planes = step(images, smalls, bigs)
    outs = list(
        finish(
            time_table.shape[0], class_table.shape[0], latents, grads, early, late, planes, ada_weight, final_ada_weight, ff
        )
    )
    outs[18] = outs[18].T
    return tuple(outs)


def solution(mesh):
    assert mesh.shape["row"] == 2 and mesh.shape["col"] == 2
    tiles = P("img", None, "row", "col")
    return jax.shard_map(
        functools.partial(local, mesh.shape["img"]),
        mesh=mesh,
        in_specs=(tiles,) + (P("img"),) * 3 + (P(),) * 18 + (tiles,),
        out_specs=(tiles, tiles) + (P(),) * 18,
        check_vma=False,
    )
```

```python
import functools

import jax
import jax.numpy as jnp
import numpy as np
from jax import lax
from jax.experimental import pallas as pl
from jax.experimental.pallas import tpu as pltpu
from jax.sharding import PartitionSpec as P

F32 = jnp.float32
BF16 = jnp.bfloat16
HEADS = 6
LATENT = 64
MESH = pl.DeviceIdType.MESH
VMEM = pl.BlockSpec(memory_space=pltpu.VMEM)
SMEM = pl.BlockSpec(memory_space=pltpu.SMEM)
ANY = pl.BlockSpec(memory_space=pl.ANY)


def nn(a, b):
    return lax.dot_general(a, b, (((1,), (0,)), ((), ())), preferred_element_type=F32)


def nt(a, b):
    return lax.dot_general(a, b, (((1,), (1,)), ((), ())), preferred_element_type=F32)


def tn(a, b):
    return lax.dot_general(a, b, (((0,), (0,)), ((), ())), preferred_element_type=F32)


def parts(v, many):
    out = []
    for _ in range(many):
        piece = v.astype(BF16)
        out.append(piece)
        v = v - piece.astype(F32)
    return out


def iota(shape, dim):
    return lax.broadcasted_iota(jnp.int32, shape, dim)


def flag(cond):
    return jnp.where(cond, 1.0, 0.0)


def swish(v):
    return v / (1.0 + jnp.exp(-v))


def position_tables(grid, width):
    quarter = width // 4
    omega = np.float32(1.0) / np.power(
        np.float32(10000.0), np.arange(quarter, dtype=np.float32) / np.float32(quarter)
    )
    angles = np.arange(grid, dtype=np.float32)[:, None] * omega[None, :].astype(np.float32)
    single = np.concatenate([np.sin(angles), np.cos(angles)], axis=1).astype(np.float32)
    blank = np.zeros_like(single)
    return np.concatenate([single, blank], axis=1), np.concatenate([blank, single], axis=1)


def plane_maps(slots, chans, side, halves):
    rows = slots * chans * side
    lanes = halves * halves
    spread = []
    keep = flag(iota((rows, lanes), 0) % side // 2 == iota((rows, lanes), 1) // halves)
    pick = []
    for j in range(2):
        col = iota((side, lanes), 0)
        spread.append(flag(col == iota((side, lanes), 1) % halves * 2 + j).astype(BF16))
        many = slots * chans * 4
        out, src = iota((many, rows), 0), iota((many, rows), 1)
        same = (out // 4 == src // side) & (out % 4 // 2 == src % 2) & (out % 2 == j)
        pick.append(flag(same).astype(BF16))
    return keep, spread, pick


def shift_masks(halves):
    row, lane = iota((16, halves * halves), 0), iota((16, halves * halves), 1)
    return row % 4 >= 2, row % 2 == 1, lane, halves


def shift_in(planes, masks):
    odd_row, odd_col, lane, side = masks
    full = side * side
    down = [
        jnp.where(
            odd_row,
            jnp.where(lane < side, pltpu.roll(planes[s ^ 2], side, 1), pltpu.roll(planes[s], side, 1)),
            planes[s],
        )
        for s in range(4)
    ]
    return [
        jnp.where(
            odd_col,
            jnp.where(
                lane % side == 0, pltpu.roll(down[s ^ 1], full - side + 1, 1), pltpu.roll(down[s], 1, 1)
            ),
            down[s],
        )
        for s in range(4)
    ]


def shift_out(planes, masks):
    odd_row, odd_col, lane, side = masks
    full = side * side
    up = [
        jnp.where(
            odd_row,
            jnp.where(
                lane >= full - side,
                pltpu.roll(planes[s ^ 2], full - side, 1),
                pltpu.roll(planes[s], full - side, 1),
            ),
            planes[s],
        )
        for s in range(4)
    ]
    return [
        jnp.where(
            odd_col,
            jnp.where(
                lane % side == side - 1, pltpu.roll(up[s ^ 1], side - 1, 1), pltpu.roll(up[s], full - 1, 1)
            ),
            up[s],
        )
        for s in range(4)
    ]


def mate(slot):
    row, col = lax.axis_index("row"), lax.axis_index("col")
    return {"row": row ^ (slot >> 1), "col": col ^ (slot & 1)}


def greet(devices):
    barrier = pltpu.get_barrier_semaphore()
    for device in devices:
        pl.semaphore_signal(barrier, inc=1, device_id=device, device_id_type=MESH)
    pl.semaphore_wait(barrier, len(devices))


def norm(v):
    share = 1.0 / v.shape[-1]
    centred = v - jnp.sum(v, axis=-1, keepdims=True) * share
    spread = jnp.sum(centred * centred, axis=-1, keepdims=True) * share
    inv = lax.rsqrt(spread + 1e-06)
    return centred * inv, inv


def norm_back(hat, inv, grad):
    share = 1.0 / hat.shape[-1]
    first = jnp.sum(grad, axis=-1, keepdims=True) * share
    second = jnp.sum(grad * hat, axis=-1, keepdims=True) * share
    return inv * (grad - first - hat * second)


def col_sum(v):
    return jnp.sum(v, axis=0, keepdims=True)


E_OUT, E_PROJ_B, E_FC2_B, E_FC1_B, E_OUT_B, E_MOD, E_COND, E_IDS, E_ROWS = 0, 16, 17, 18, 22, 23, 41, 47, 48
L_PATCH, L_PATCH_B, L_MOD, L_Q_B, L_V_B, L_ROWS = 0, 16, 17, 23, 24, 32


def tree(terms):
    while len(terms) > 1:
        terms = [terms[i] + terms[i + 1] for i in range(0, len(terms), 2)]
    return terms[0]


class Copies:
    def __init__(self, send_sem, recv_sem):
        self.send_sem, self.recv_sem, self.known = send_sem, recv_sem, {}

    def make(self, key, src, dst, device):
        at = self.known.setdefault(key, len(self.known))
        return pltpu.make_async_remote_copy(
            src_ref=src, dst_ref=dst, send_sem=self.send_sem.at[at], recv_sem=self.recv_sem.at[at],
            device_id=device, device_id_type=MESH,
        )


class Stage:
    def __init__(self, copies, reduce=None):
        self.copies, self.reduce = copies, reduce

    def start(self):
        for c in self.copies():
            c.start()

    def finish(self):
        for c in self.copies():
            c.wait_recv()
        if self.reduce is not None:
            self.reduce()

    def drain(self):
        for c in self.copies():
            c.wait_send()


def far(distance):
    return {"img": lax.axis_index("img") ^ distance}


def rows_at(start, many):
    return pl.ds(pl.multiple_of(start, 16), many)


def ways(images, plan):
    bits = images.bit_length() - 1
    kept = ["".join(x for x in way if not x.isdigit() or int(x) < bits) for way in plan]
    return [way for way in kept if way]


def shared_bits(images, plan):
    return max([int(x) + 1 for way in ways(images, plan) for x in way if x.isdigit()] + [0])


def members(way):
    return 1 << len(way)


def position(way):
    total = 0
    for x in way:
        if x.isdigit():
            side = (lax.axis_index("img") >> int(x)) & 1
        else:
            side = lax.axis_index({"c": "col", "r": "row"}[x])
        total = 2 * total + side
    return total


def partner(way, delta):
    device, flips = {}, 0
    for k, x in enumerate(reversed(way)):
        if delta >> k & 1:
            if x.isdigit():
                flips |= 1 << int(x)
            else:
                name = {"c": "col", "r": "row"}[x]
                device[name] = 1 - lax.axis_index(name)
    if flips:
        device["img"] = lax.axis_index("img") ^ flips
    return device


def group_shapes(images, rows, plan):
    d, shapes = 384, []
    for way in ways(images, plan):
        many = members(way)
        rows //= many
        shapes += [(many - 1, rows, d), (rows, d)]
    high = images >> shared_bits(images, plan)
    if high > 1:
        shapes += [(high - 1, rows, d), (rows, d)]
    return shapes


def group_copies(images, plan):
    return 2 * sum(members(way) - 1 for way in ways(images, plan)) + (images >> shared_bits(images, plan)) - 1


def group_stages(name, images, base, rows, plan, grads, out, bufs, net):
    bufs = list(bufs)
    known = ways(images, plan)
    shared = shared_bits(images, plan)
    high = images >> shared

    def add(*refs):
        return tree([r.astype(F32) for r in refs]).astype(BF16)

    def scatter(k, way, held, many, got, total, last):
        count = members(way)

        def copies():
            return [
                net.make(f"{name}s{k}.{e}", held((position(way) ^ e) * many, many), got.at[e - 1], partner(way, e))
                for e in range(1, count)
            ]

        def reduce():
            total[...] = add(held(position(way) * many, many)[...], *[got[e] for e in range(count - 1)])
            if last:
                out[rows_at(base + start(len(known)), many), :] = total[...]

        return Stage(copies, reduce)

    sizes = [rows]
    for way in known:
        sizes.append(sizes[-1] // members(way))

    def start(level):
        total = 0
        for k in range(level):
            total = total + position(known[k]) * sizes[k + 1]
        return total

    stages = []

    def held(at, many):
        return grads.at[rows_at(base + at, many), :]

    for k, way in enumerate(known):
        got, total = bufs[:2]
        del bufs[:2]
        stages.append(scatter(k, way, held, sizes[k + 1], got, total, high == 1 and k == len(known) - 1))

        def held(at, many, total=total):
            return total.at[rows_at(at, many), :]

    if high > 1:
        got, final = bufs[:2]
        summed, many = total, sizes[-1]

        def copies():
            return [net.make(f"{name}h{e}", summed, got.at[e - 1], far(e << shared)) for e in range(1, high)]

        def reduce():
            final[...] = add(summed[...], *[got[e] for e in range(high - 1)])
            out[rows_at(base + start(len(known)), many), :] = final[...]

        stages.append(Stage(copies, reduce))

    def gather(k, way):
        def copies():
            at = out.at[rows_at(base + start(k + 1), sizes[k + 1]), :]
            return [net.make(f"{name}g{k}.{e}", at, at, partner(way, e)) for e in range(1, members(way))]

        return Stage(copies)

    for k in reversed(range(len(known))):
        stages.append(gather(k, known[k]))
    return stages


def sum_stages(name, images, block, got, total, out, net):
    def c0():
        return [net.make(name + "m" + str(s), block, got.at[s - 1], mate(s)) for s in (1, 2, 3)]

    def r0():
        t = tree([r.astype(F32) for r in (block[...], got[0], got[1], got[2])]).astype(BF16)
        total[...] = t
        out[lax.axis_index("img")] = t

    def c1():
        at = out.at[lax.axis_index("img")]
        return [net.make(name + "i" + str(d), total, at, far(d)) for d in range(1, images)]

    return [Stage(c0, r0), Stage(c1)]


def edge_stages(name, edge, got, out, k, net):
    def c0():
        return [net.make(name + str(s), edge.at[s], got.at[s - 1], mate(s)) for s in (1, 2, 3)]

    def r0():
        out[k] = tree([r.astype(F32) for r in (edge[0], got[1], got[0], got[2])])

    return [Stage(c0, r0)]


PLANS = (("c", "r0", "12"), ("c", "01", "r2"), ("c", "r1", "02"))
FC, PAIR, EARLY, LATE, EDGE_Y, EDGE_L = 0, 6, 9, 10, 11, 12
IMAGE_EVENTS = ((1, 0, 1), (1, 1, 1), (2, 2, 1))
GRAD_EVENTS = ((1, 0, 2), (2, 1, 2), (3, 2, 2))
BACK_EVENTS = (
    (1, 3, 1), (1, 4, 1), (1, 5, 1), (2, 0, 3), (2, 1, 3), (2, 2, 3), (2, EDGE_Y, 1), (3, 3, 2), (3, 4, 2), (3, 5, 2),
    (4, 0, 4), (4, 1, 4), (4, 2, 4), (4, PAIR, 1), (5, 3, 3), (5, 4, 3), (5, 5, 3), (5, EARLY, 1), (6, 0, 5), (6, 1, 5), (6, 2, 5),
    (6, PAIR, 2), (7, 3, 4), (7, 4, 4), (7, 5, 4), (7, PAIR + 1, 1), (8, 0, 6), (8, 1, 6), (8, 2, 6), (8, PAIR, 3),
)
TAIL_EVENTS = (
    (0, 3, 5), (0, 4, 5), (0, 5, 5), (1, EARLY, 2), (2, PAIR + 1, 2), (3, PAIR, 4), (4, PAIR + 2, 1), (5, 3, 6), (5, 4, 6), (5, 5, 6),
    (7, PAIR + 1, 3), (8, PAIR, 5), (10, PAIR + 2, 2), (11, PAIR + 1, 4), (11, PAIR, 6),
)
END_EVENTS = ((PAIR + 2, 3), (PAIR + 1, 5), (PAIR + 2, 4), (PAIR + 1, 6))

def group_list(d, ff):
    rows = d + d // 3
    return [(k * rows, rows, PLANS[k % 3]) for k in range((2 * ff + 4 * d) // rows)]


def step_kernel(images, count, *refs):
    refs = list(refs)

    def take(n):
        out = refs[:n]
        del refs[:n]
        return out

    (time_ref, class_ref, live_ref, lat_ref, cot_ref, patch_b_ref, ada_b_ref, qv_b_ref, proj_b_ref, fc1_b_ref, fc2_b_ref,
     fada_b_ref, out_b_ref, pos_a_ref, pos_b_ref, patch_w_ref, out_wt_ref) = take(17)
    hbm = take(8)
    out_ref, early_out, late_out, planes_out = take(4)
    held = take(4)
    qkv_ref, proj_ref, fc1_ref, fc2_ref = held
    (planes_ref, mod_s, pt_s, gy_s, wp_s, wo_s, x1_s, x1t_s, hat_s, inv_s, k_s, v_s, q_s, e_s, sa_s, sb_s, top_s,
     linv_s, delta_s, of_s, a_s, b_s, dm_s, x2t_s, da_s, dx_s, edge_s,
     grads_ref, early_ref, late_ref, early_16, late_16, edge_y, edge_l, early_got, early_sum, late_got, late_sum, edge_y_got, edge_l_got) = take(40)
    load_sem, gather_send, gather_recv, send_sem, recv_sem = take(5)
    bufs = refs

    d = qkv_ref.shape[0]
    slots, chans, side, _ = lat_ref.shape
    toks = x1_s.shape[0]
    pairs = HEADS // 2
    ff = fc1_ref.shape[1]
    blocks = ff // d
    half = side // 2
    bins, classes = hbm[0].shape[0], hbm[1].shape[0]

    loads = [pltpu.make_async_copy(a, b, load_sem.at[4 + i]) for i, (a, b) in enumerate(zip(hbm[4:], held))]
    net = Copies(send_sem, recv_sem)
    groups = []
    for g, (base, rows, plan) in enumerate(group_list(d, ff)):
        n = len(group_shapes(images, rows, plan))
        groups.append(group_stages("g" + str(g), images, base, rows, plan, grads_ref, out_ref, bufs[:n], net))
        del bufs[:n]
    groups.append(sum_stages("e", images, early_16, early_got, early_sum, early_out, net))
    groups.append(sum_stages("l", images, late_16, late_got, late_sum, late_out, net))
    groups.append(edge_stages("y", edge_y, edge_y_got, planes_out, 1, net))
    groups.append(edge_stages("x", edge_l, edge_l_got, planes_out, 0, net))
    def advance(g, k):
        if k > 0:
            groups[g][k - 1].finish()
        if k < len(groups[g]):
            groups[g][k].start()

    def row_of(ref, start, many):
        return ref[...].astype(F32).reshape(1, ref.shape[0])[:, start : start + many]

    early_ref[...] = jnp.zeros_like(early_ref)
    late_ref[...] = jnp.zeros_like(late_ref)

    swap = flag(iota((16, 16), 0) == (iota((16, 16), 1) ^ 3)).astype(BF16)
    wp_s[...] = nn(swap, patch_w_ref[...]).astype(BF16)
    wo_s[...] = nn(swap, out_wt_ref[...]).astype(BF16)
    out_bias = jnp.sum(
        flag(iota((16, 16), 1) == (iota((16, 16), 0) ^ 3)) * row_of(out_b_ref, 0, 16), axis=1, keepdims=True
    )

    inv_lane = iota((toks, 128), 1)

    def opening(time_table_ref, class_table_ref, ada_ref, fada_ref, pos_s):
        tables = [
            pltpu.make_async_copy(a, b, load_sem.at[i])
            for i, (a, b) in enumerate(zip(hbm[:4], (time_table_ref, class_table_ref, ada_ref, fada_ref)))
        ]
        for c in tables + loads:
            c.start()
        greet([mate(s) for s in (1, 2, 3)] + [far(k) for k in range(1, images)])
        keep, spread, pick = plane_maps(slots, chans, side, half)
        for k, ref in enumerate((lat_ref, cot_ref)):
            tile = ref[...].reshape(slots * chans * side, side)
            total = None
            for j in range(2):
                wide = (nn(tile, spread[j]) * keep).astype(BF16)
                term = nn(pick[j], wide)
                total = term if total is None else total + term
            planes_ref[0, k] = total.astype(BF16)
        gathers = []
        for s in (1, 2, 3):
            c = pltpu.make_async_remote_copy(
                src_ref=planes_ref.at[0], dst_ref=planes_ref.at[s], send_sem=gather_send.at[s - 1], recv_sem=gather_recv.at[s - 1],
                device_id=mate(s), device_id_type=MESH,
            )
            c.start()
            gathers.append(c)

        my_row, my_col = lax.axis_index("row"), lax.axis_index("col")
        patch_b = row_of(patch_b_ref, 0, d)
        for s in range(4):
            ta = pos_a_ref[pl.ds(pl.multiple_of((my_row ^ (s >> 1)) * half, half), half), :]
            tb = pos_b_ref[pl.ds(pl.multiple_of((my_col ^ (s & 1)) * half, half), half), :] + patch_b
            for a in range(half):
                pos_s[s, a * half : (a + 1) * half, :] = ta[a : a + 1, :] + tb

        def onehot(ids_ref, many):
            row, lane = iota((16, many), 0), iota((16, many), 1)
            hit = jnp.zeros((16, many), F32)
            for i in range(slots):
                hit = hit + flag((row == i) & (lane == ids_ref[i]))
            return hit.astype(BF16)

        for c in tables:
            c.wait()
        cond = nn(onehot(time_ref, bins), time_table_ref[...]) + nn(onehot(class_ref, classes), class_table_ref[...])
        cond = cond[:8]
        act = parts(swish(cond), 3)
        act = jnp.concatenate([p.astype(F32) for p in act] + [jnp.zeros((8, d), F32)], axis=0).astype(BF16)
        for p in range(8):
            w = ada_ref[:, p * d : (p + 1) * d] if p < 6 else fada_ref[:, (p - 6) * d : (p - 5) * d]
            m = nn(act, w)
            b = row_of(ada_b_ref, p * d, d) if p < 6 else row_of(fada_b_ref, (p - 6) * d, d)
            mod_s[p] = m[0:8] + m[8:16] + m[16:24] + b
        row, lane = iota((8, d), 0), iota((8, d), 1)
        ids = jnp.zeros((8, d), F32)
        for i in range(slots):
            for k, v in enumerate((time_ref[i], class_ref[i] // 256, class_ref[i] % 256)):
                ids = ids + jnp.where((row == 0) & (lane == k * slots + i), 0.25 * v.astype(F32), 0.0)
        high = cond.astype(BF16).astype(F32)
        early_ref[E_COND : E_COND + slots, :] = 0.25 * high[:slots]
        early_ref[E_COND + slots : E_COND + 2 * slots, :] = 0.25 * (cond - high)[:slots]
        early_ref[E_IDS : E_IDS + 1, :] = ids[0:1]

        for c in gathers:
            c.wait_recv()
        masks = shift_masks(half)
        live = [live_ref[i].astype(F32) for i in range(slots)]
        for i in range(slots):
            lat = shift_in([planes_ref[s, 0, i * 16 : (i + 1) * 16, :].astype(F32) for s in range(4)], masks)
            cot = shift_in([planes_ref[s, 1, i * 16 : (i + 1) * 16, :].astype(F32) for s in range(4)], masks)
            for s in range(4):
                pt_s[i * 4 + s] = lat[s].astype(BF16)
            gy_s[i] = (cot[0] * live[i]).astype(BF16)

        v_bias = row_of(qv_b_ref, d, d)

        def token_norm(t):
            img, slot = t // 4, t % 4
            tok = tn(pt_s[t], wp_s[...]) + pos_s[slot]
            dx_s[img] = tok
            hat, inv = norm(tok)
            hat_s[t] = hat
            inv_s[...] = jnp.where(inv_lane == t, inv, inv_s[...])
            x1_s[...] = (hat * (1.0 + mod_s[1, pl.ds(img, 1), :]) + mod_s[0, pl.ds(img, 1), :]).astype(BF16)

        token_norm(jnp.int32(3))
        loads[0].wait()

        def reverse(n):
            return n // 4 * 4 + 3 - n % 4

        def tokens(n, carry):
            t = reverse(n)
            img, slot = t // 4, t % 4
            x1 = x1_s[...]
            x1t_s[t] = x1.T
            keys = nn(x1, qkv_ref[:, d : 2 * d]).astype(BF16)
            vals = (nn(x1, qkv_ref[:, 2 * d :]) + v_bias).astype(BF16)
            for p in range(pairs):
                k_s[img * pairs + p, slot] = keys[:, p * 128 : (p + 1) * 128]
                v_s[img * pairs + p, slot] = vals[:, p * 128 : (p + 1) * 128]
            token_norm(reverse(jnp.minimum(n + 1, slots * 4 - 1)))
            return carry

        lax.fori_loop(0, slots * 4, tokens, 0)

        for c in gathers:
            c.wait_send()

    pl.run_scoped(
        opening,
        *[pltpu.VMEM(hbm[i].shape, BF16) for i in range(4)],
        pltpu.VMEM((4, toks, d), F32),
    )
    masks = shift_masks(half)

    lane128 = iota((1, 128), 1) // 64
    head_mask = [flag(lane128 == h) for h in range(2)]

    q_bias = row_of(qv_b_ref, 0, d)

    def queries(img, carry):
        query = tn(x1t_s[img * 4], qkv_ref[:, :d]) + q_bias
        query = query.astype(BF16).astype(F32) * 0.125
        for p in range(pairs):
            for h in range(2):
                q_s[img * HEADS + p * 2 + h] = (query[:, p * 128 : (p + 1) * 128] * head_mask[h]).astype(BF16)
        return carry

    lax.fori_loop(0, slots, queries, 0)

    def scores(idx, h, buf):
        top = None
        for c in range(4):
            s = nt(k_s[idx, c], q_s[idx * 2 + h])
            buf[2 * c] = s[:, :128]
            buf[2 * c + 1] = s[:, 128:]
            m = jnp.max(s, axis=0, keepdims=True)
            top = m if top is None else jnp.maximum(top, m)
        top_s[h] = top

    def softmax(idx, h, buf, vt):
        head = idx * 2 + h
        top, total, acc = top_s[h], None, None
        for c in range(4):
            e = jnp.exp(jnp.concatenate([buf[2 * c], buf[2 * c + 1]], axis=1) - top)
            l = col_sum(e)
            total = l if total is None else total + l
            eb = e.astype(BF16)
            e_s[head, c] = eb
            o = nn(vt[c][h * 64 : (h + 1) * 64], eb)
            acc = o if acc is None else acc + o
        linv = 1.0 / total
        linv_s[head] = linv
        of_s[head] = acc * linv

    scores(jnp.int32(0), 0, sa_s)

    def attend(idx, carry):
        vt = [v_s[idx, c].T for c in range(4)]
        scores(idx, 1, sb_s)
        softmax(idx, 0, sa_s, vt)
        scores(jnp.minimum(idx + 1, slots * pairs - 1), 0, sa_s)
        softmax(idx, 1, sb_s, vt)
        return carry

    lax.fori_loop(0, slots * pairs, attend, 0)
    for c in loads[1:]:
        c.wait()
    proj_b, fc1_b, fc2_b = row_of(proj_b_ref, 0, d), row_of(fc1_b_ref, 0, ff), row_of(fc2_b_ref, 0, d)

    def closing(hat2_s, dot_s, dom_s, dq_s, dxq_s, acc_s, dx1_s):
        def pair_row(k):
            return 2 * ff + k * (d + d // 3)

        def wide(ref, img, b):
            return jnp.concatenate([ref[img * 12 + b * 3 + j] for j in range(3)], axis=1)

        def fc2_grad(b, carry):
            total = tree([tn(wide(a_s, img, b), dm_s[img]) for img in range(2)])
            for img in range(2, slots):
                total = total + tn(wide(a_s, img, b), dm_s[img])
            grads_ref[rows_at(b * d, d), :] = total.astype(BF16)
            started(b, FC)
            return carry

        def started(b, first):
            for k in range(1, blocks):

                @pl.when(b == k)
                def _():
                    advance(first + k - 1, 0)

        def when_at(i, plan):
            for at, events in plan.items():

                @pl.when(i == at)
                def _():
                    for g, k in events:
                        advance(g, k)

        image_plan, grad_plan, back_plan, tail_plan = {}, {}, {}, {}
        for plan, events in ((image_plan, IMAGE_EVENTS), (grad_plan, GRAD_EVENTS), (back_plan, BACK_EVENTS), (tail_plan, TAIL_EVENTS)):
            for at, g, k in events:
                if k <= len(groups[g]):
                    plan.setdefault(at, []).append((g, k))

        def inv_at(t):
            return jnp.sum(jnp.where(inv_lane == t, inv_s[...], 0.0), axis=1, keepdims=True)

        def image(img, carry):
            def mod_row(p):
                return mod_s[p, pl.ds(img, 1), :]

            ot = jnp.concatenate([of_s[img * HEADS + h] for h in range(HEADS)], axis=0).astype(BF16)
            branch = tn(ot, proj_ref[...]) + proj_b
            g1 = mod_row(2)
            resid = dx_s[img] + g1 * branch
            hat2, inv2 = norm(resid)
            hat2_s[img] = hat2
            inv_s[...] = jnp.where(inv_lane == slots * 4 + img, inv2, inv_s[...])
            x2 = (hat2 * (1.0 + mod_row(4)) + mod_row(3)).astype(BF16)
            x2t_s[img] = x2.T
            mlp = jnp.zeros((toks, d), F32)
            k0, k1 = 0.7978845608028654, 0.044715
            for b in range(blocks):
                at_b = slice(b * d, (b + 1) * d)
                u = nn(x2, fc1_ref[:, at_b]) + fc1_b[:, at_b]
                sq = u * u
                cdf = 0.5 + 0.5 * jnp.tanh(u * (k0 + (k0 * k1) * sq))
                hidden = u * cdf
                slope = cdf + hidden * (1.0 - cdf) * ((2.0 * k0) + (6.0 * k0 * k1) * sq)
                slope = slope.astype(BF16)
                for j in range(3):
                    b_s[img * 12 + b * 3 + j] = slope[:, j * 128 : (j + 1) * 128]
                hidden = hidden.astype(BF16)
                for j in range(3):
                    a_s[img * 12 + b * 3 + j] = hidden[:, j * 128 : (j + 1) * 128]
                mlp = mlp + nn(hidden, fc2_ref[at_b, :])
            mlp = mlp + fc2_b
            g2 = mod_row(5)
            x3 = resid + g2 * mlp
            hatf, invf = norm(x3)
            scf = 1.0 + mod_row(7)
            xf = (hatf * scf + mod_row(6)).astype(BF16)
            edge_s[4, img] = (nt(wo_s[...], xf) + out_bias) * live_ref[img].astype(F32)
            gy = gy_s[img]
            early_ref[E_OUT : E_OUT + 16, :] += nn(gy, xf)
            early_ref[E_OUT_B : E_OUT_B + 1, 0:16] += nt(jnp.ones((8, toks), BF16), gy)[0:1]
            dxf = tn(gy, wo_s[...])

            def put_mod(p, v):
                early_ref[pl.ds(E_MOD + (p - 2) * slots + img, 1), :] = v

            put_mod(6, col_sum(dxf))
            put_mod(7, col_sum(dxf * hatf))
            dx3 = norm_back(hatf, invf, dxf * scf)
            dm = (g2 * dx3).astype(BF16)
            dm_s[img] = dm
            put_mod(5, col_sum(mlp * dx3))
            early_ref[E_FC2_B : E_FC2_B + 1, :] += col_sum(dm.astype(F32))
            dx_s[img] = dx3
            return carry

        lax.fori_loop(0, slots, image, 0)
        lax.fori_loop(0, blocks, fc2_grad, 0)

        def image_back(img, carry):
            when_at(img, image_plan)

            def mod_row(p):
                return mod_s[p, pl.ds(img, 1), :]

            def put_mod(p, v):
                early_ref[pl.ds(E_MOD + (p - 2) * slots + img, 1), :] = v

            g1, dm, hat2 = mod_row(2), dm_s[img], hat2_s[img]
            inv2 = inv_at(slots * 4 + img)
            dx2 = jnp.zeros((toks, d), F32)
            for b in range(blocks):
                at_b = slice(b * d, (b + 1) * d)
                slope = jnp.concatenate([b_s[img * 12 + b * 3 + j] for j in range(3)], axis=1).astype(F32)
                du = (nt(dm, fc2_ref[at_b, :]) * slope).astype(BF16)
                for j in range(3):
                    b_s[img * 12 + b * 3 + j] = du[:, j * 128 : (j + 1) * 128]
                early_ref[E_FC1_B + b : E_FC1_B + b + 1, :] += col_sum(du.astype(F32))
                dx2 = dx2 + nt(du, fc1_ref[:, at_b])
            put_mod(3, col_sum(dx2))
            put_mod(4, col_sum(dx2 * hat2))
            dx = dx_s[img] + norm_back(hat2, inv2, dx2 * (1.0 + mod_row(4)))
            dx_s[img] = dx
            ot = jnp.concatenate([of_s[img * HEADS + h] for h in range(HEADS)], axis=0).astype(BF16)
            branch = tn(ot, proj_ref[...]) + proj_b
            put_mod(2, col_sum(branch * dx))
            da = (g1 * dx).astype(BF16)
            da_s[img] = da
            early_ref[E_PROJ_B : E_PROJ_B + 1, :] += col_sum(da.astype(F32))
            dot = nt(proj_ref[...], da)
            blank = jnp.zeros((64, toks), F32)
            for hd in range(HEADS):
                head = img * HEADS + hd
                piece = dot[hd * 64 : (hd + 1) * 64]
                linv = linv_s[head]
                delta_s[head] = col_sum(piece * of_s[head]) * linv
                piece = piece * linv
                wide = jnp.concatenate([piece, blank] if hd % 2 == 0 else [blank, piece], axis=0).astype(BF16)
                dot_s[head] = wide
                dom_s[head] = wide.T
            return carry

        lax.fori_loop(0, slots, image_back, 0)

        def fc1_grad(b, carry):
            when_at(b, grad_plan)
            total = tree([nn(x2t_s[img], wide(b_s, img, b)) for img in range(2)])
            for img in range(2, slots):
                total = total + nn(x2t_s[img], wide(b_s, img, b))
            grads_ref[rows_at(ff + b * d, d), :] = total.astype(BF16)
            started(b, FC + blocks - 1)
            return carry

        lax.fori_loop(0, blocks, fc1_grad, 0)
        total = None
        for img in range(slots):
            ot = jnp.concatenate([of_s[img * HEADS + h] for h in range(HEADS)], axis=0).astype(BF16)
            term = nn(ot, da_s[img])
            total = term if total is None else total + term
        for k in range(pairs):
            grads_ref[pair_row(k) + d : pair_row(k + 1), :] = total[k * (d // 3) : (k + 1) * (d // 3)].astype(BF16)
        blank = jnp.zeros((16, toks), F32)
        for i in range(slots):
            out = shift_out([edge_s[4, i], blank, blank, blank], masks)
            for s in range(4):
                edge_y[s, i * 16 : (i + 1) * 16, :] = out[s].astype(BF16)
        early_16[...] = early_ref[...].astype(BF16)
        advance(EDGE_Y, 0)
        advance(EARLY, 0)

        acc_s[...] = jnp.zeros_like(acc_s)

        def attend_back(it, carry):
            when_at(it, back_plan)
            p, img = it // slots, it % slots
            idx = img * pairs + p
            dqt = [None, None]
            jobs = [(c, h) for c in range(4) for h in range(2)]

            def product(job):
                return nn(v_s[idx, job[0]], dot_s[idx * 2 + job[1]])

            dp = product(jobs[0])
            gathered = None
            sum_v = None
            for n, (c, h) in enumerate(jobs):
                head = idx * 2 + h
                ahead = product(jobs[n + 1]) if n + 1 < len(jobs) else None
                if h == 0:
                    kt = k_s[idx, c].T
                    dk, dv = None, None
                e = e_s[head, c]
                ds = (e.astype(F32) * (dp - delta_s[head])).astype(BF16)
                dk_h, dv_h = nn(ds, q_s[head]), nn(e, dom_s[head])
                dk = dk_h if dk is None else dk + dk_h
                dv = dv_h if dv is None else dv + dv_h
                dq_h = nn(kt[h * 64 : (h + 1) * 64], ds)
                dqt[h] = dq_h if dqt[h] is None else dqt[h] + dq_h
                dp = ahead
                if h == 1:
                    dk, dv = dk.astype(BF16), dv.astype(BF16)
                    a_s[idx * 4 + c] = dk
                    b_s[idx * 4 + c] = dv
                    sv = col_sum(dv.astype(F32))
                    sum_v = sv if sum_v is None else sum_v + sv
                    term = nn(x1t_s[img * 4 + c], jnp.concatenate([dk, dv], axis=1))
                    gathered = term if gathered is None else gathered + term
            dq = (jnp.concatenate(dqt, axis=0) * 0.125).T.astype(BF16)
            dq_s[idx] = dq
            lanes = pl.ds(pl.multiple_of(p * 128, 128), 128)
            late_ref[L_V_B : L_V_B + 1, lanes] += sum_v
            late_ref[L_Q_B : L_Q_B + 1, lanes] += col_sum(dq.astype(F32))
            acc_s[:, 128:] += gathered
            acc_s[:, :128] += nn(x1t_s[img * 4], dq)

            for pair in range(pairs):

                @pl.when(it == pair * slots + slots - 1)
                def _():
                    at = pair_row(pair)
                    grads_ref[at : at + d, :] = acc_s[...].astype(BF16)
                    acc_s[...] = jnp.zeros_like(acc_s)
                    advance(PAIR + pair, 0)

            return carry

        lax.fori_loop(0, slots * pairs, attend_back, 0)

        def joined(ref, img, slot):
            return [ref[(img * pairs + p) * 4 + slot] for p in range(pairs)]

        def query_back(img, carry):
            dq = jnp.concatenate([dq_s[img * pairs + p] for p in range(pairs)], axis=1)
            dxq_s[img] = nt(dq, qkv_ref[:, :d])
            return carry

        lax.fori_loop(0, slots, query_back, 0)

        def product_back(t):
            img, slot = t // 4, t % 4
            dkv = jnp.concatenate(joined(a_s, img, slot) + joined(b_s, img, slot), axis=1)
            own = jnp.where(slot == 0, 1.0, 0.0)
            return nt(dkv, qkv_ref[:, d:]) + dxq_s[img] * own

        dx1_s[...] = product_back(jnp.int32(0))
        def tokens_back(t, carry):
            when_at(t, tail_plan)
            img, slot = t // 4, t % 4
            dx1 = dx1_s[...]
            ahead = product_back(jnp.minimum(t + 1, slots * 4 - 1))
            hat = hat_s[t]
            late_ref[pl.ds(L_MOD + img, 1), :] += col_sum(dx1)
            late_ref[pl.ds(L_MOD + slots + img, 1), :] += col_sum(dx1 * hat)
            own = jnp.where(slot == 0, 1.0, 0.0)
            dtok = norm_back(hat, inv_at(t), dx1 * (1.0 + mod_s[1, pl.ds(img, 1), :])) + dx_s[img] * own
            late_ref[L_PATCH_B : L_PATCH_B + 1, :] += col_sum(dtok)
            hi, lo = parts(dtok, 2)
            late_ref[L_PATCH : L_PATCH + 16, :] += nn(pt_s[t], hi) + nn(pt_s[t], lo)
            edge_s[slot, img] = nt(wp_s[...], hi) + nt(wp_s[...], lo)
            dx1_s[...] = ahead
            return carry

        lax.fori_loop(0, slots * 4, tokens_back, 0)

    pl.run_scoped(
        closing,
        pltpu.VMEM((slots, toks, d), F32),
        pltpu.VMEM((slots * HEADS, 128, toks), BF16),
        pltpu.VMEM((slots * HEADS, toks, 128), BF16),
        pltpu.VMEM((slots * pairs, toks, 128), BF16),
        pltpu.VMEM((slots, toks, d), F32),
        pltpu.VMEM((d, d), F32),
        pltpu.VMEM((toks, d), F32),
    )

    late_16[...] = late_ref[...].astype(BF16)
    advance(LATE, 0)
    for i in range(slots):
        lat = shift_out([edge_s[s, i] for s in range(4)], masks)
        for s in range(4):
            edge_l[s, i * 16 : (i + 1) * 16, :] = lat[s].astype(BF16)
    advance(EDGE_L, 0)
    state = {g: 1 for g in (LATE, EDGE_L)}
    for g in (*range(FC, PAIR + 3), EARLY, EDGE_Y):
        done = [k for events in (IMAGE_EVENTS, GRAD_EVENTS, BACK_EVENTS, TAIL_EVENTS) for _, h, k in events if h == g]
        assert done == list(range(1, len(done) + 1))
        state[g] = len(done) + 1
    order = [LATE, EDGE_L, LATE] + [g for g, _ in END_EVENTS]
    order += [g for g in state for _ in range(len(groups[g]))]
    for g in order:
        if state[g] <= len(groups[g]):
            advance(g, state[g])
            state[g] += 1
    for stages in groups:
        for stage in stages:
            stage.drain()
    assert len(net.known) <= count


def step(images, smalls, bigs):
    time_bin, latents = smalls[0], smalls[3]
    qkv_weight, fc1_weight = bigs[4], bigs[6]
    d, ff = qkv_weight.shape[0], fc1_weight.shape[1]
    slots, chans, side, _ = latents.shape
    toks = side * side // 4
    planes = slots * chans * 4
    pairs = HEADS // 2
    heads = slots * HEADS
    out_shape = (
        jax.ShapeDtypeStruct((2 * ff + 4 * d, d), BF16),
        jax.ShapeDtypeStruct((images, E_ROWS, d), BF16),
        jax.ShapeDtypeStruct((images, L_ROWS, d), BF16),
        jax.ShapeDtypeStruct((2, planes, toks), F32),
    )
    scratch = [(w.shape, w.dtype) for w in bigs[4:]] + [
        ((4, 2, planes, toks), BF16), ((8, 8, d), F32), ((slots * 4, 16, toks), BF16),
        ((slots, 16, toks), BF16), ((16, d), BF16), ((16, d), BF16), ((toks, d), BF16), ((slots * 4, d, toks), BF16),
        ((slots * 4, toks, d), F32), ((toks, 128), F32), ((slots * pairs, 4, toks, 128), BF16),
        ((slots * pairs, 4, toks, 128), BF16), ((heads, toks, 128), BF16), ((heads, 4, toks, toks), BF16),
        ((8, toks, 128), F32), ((8, toks, 128), F32), ((2, 1, toks), F32), ((heads, 1, toks), F32), ((heads, 1, toks), F32),
        ((heads, 64, toks), F32), ((slots * 12, toks, 128), BF16), ((slots * 12, toks, 128), BF16),
        ((slots, toks, d), BF16), ((slots, d, toks), BF16), ((slots, toks, d), BF16),
        ((slots, toks, d), F32), ((5, slots, 16, toks), F32),
        ((2 * ff + 4 * d, d), BF16), ((E_ROWS, d), F32), ((L_ROWS, d), F32), ((E_ROWS, d), BF16), ((L_ROWS, d), BF16), ((4, planes, toks), BF16), ((4, planes, toks), BF16),
        ((3, E_ROWS, d), BF16), ((E_ROWS, d), BF16), ((3, L_ROWS, d), BF16), ((L_ROWS, d), BF16), ((3, planes, toks), BF16),
        ((3, planes, toks), BF16),
    ]
    dma = pltpu.SemaphoreType.DMA
    parts_of = group_list(d, ff)
    count = sum(group_copies(images, plan) for _, _, plan in parts_of) + 2 * (3 + images - 1) + 6
    moved = [(s, BF16) for _, rows, plan in parts_of for s in group_shapes(images, rows, plan)]
    return pl.pallas_call(
        functools.partial(step_kernel, images, count),
        out_shape=out_shape,
        in_specs=[SMEM] * 3 + [VMEM] * (len(smalls) - 3) + [ANY] * len(bigs),
        out_specs=(VMEM,) * 4,
        scratch_shapes=[pltpu.VMEM(shape, kind) for shape, kind in scratch]
        + [dma((len(bigs),)), dma((3,)), dma((3,)), dma((count,)), dma((count,))]
        + [pltpu.VMEM(shape, kind) for shape, kind in moved],
        compiler_params=pltpu.CompilerParams(
            collective_id=0, has_side_effects=True, vmem_limit_bytes=64 * 1024 * 1024 - 65536
        ),
        name="step",
    )(*smalls, *bigs)


def finish_kernel(
    bins, classes, grads_hbm, early_ref, late_ref, planes_ref, ada_hbm, fada_hbm,
    out_ref, lat_ref, time_ref, class_hbm, patch_ref, patch_b_ref, ada_g_hbm, ada_b_ref, qkv_g_hbm, qv_b_ref, proj_g_ref,
    proj_b_ref, fc1_g_hbm, fc1_b_ref, fc2_g_hbm, fc2_b_ref, fada_g_hbm, fada_b_ref, out_gt_ref, out_b_ref,
    grads_ref, ada_ref, fada_ref, class_ref, ada_g_ref, qkv_g_ref, fc1_g_ref, fc2_g_ref, fada_g_ref, in_sem, out_sem,
):
    d = ada_ref.shape[0]
    ff = fc1_g_ref.shape[1]
    blocks = ff // d
    pairs = HEADS // 2
    slots, chans, side, _ = lat_ref.shape
    groups = early_ref.shape[0]
    images = groups * slots
    held = -(-images // 32) * 32

    bounds = [0, ff, 2 * ff, 2 * ff + 4 * d]
    loads = [
        pltpu.make_async_copy(grads_hbm.at[a:b, :], grads_ref.at[a:b, :], in_sem.at[i])
        for i, (a, b) in enumerate(zip(bounds[:-1], bounds[1:]))
    ]
    loads += [pltpu.make_async_copy(ada_hbm, ada_ref, in_sem.at[3]), pltpu.make_async_copy(fada_hbm, fada_ref, in_sem.at[4])]
    for c in loads:
        c.start()
    stores = []

    def send(src, dst):
        c = pltpu.make_async_copy(src, dst, out_sem.at[len(stores)])
        c.start()
        stores.append(c)

    loads[0].wait()
    fc2_g_ref[...] = grads_ref[0:ff, :].astype(F32)
    send(fc2_g_ref, fc2_g_hbm)
    loads[1].wait()
    for b in range(blocks):
        fc1_g_ref[:, b * d : (b + 1) * d] = grads_ref[ff + b * d : ff + (b + 1) * d, :].astype(F32)
    send(fc1_g_ref, fc1_g_hbm)
    loads[2].wait()
    third = d // 3
    for p in range(pairs):
        at = 2 * ff + p * (d + third)
        proj_g_ref[p * third : (p + 1) * third, :] = grads_ref[at + d : at + d + third, :].astype(F32)
        for k in range(3):
            lanes = slice(k * d + p * 128, k * d + (p + 1) * 128)
            qkv_g_ref[:, lanes] = grads_ref[at : at + d, k * 128 : (k + 1) * 128].astype(F32)
    send(qkv_g_ref, qkv_g_hbm)

    all_early = early_ref[...].reshape(groups * E_ROWS, d)
    all_late = late_ref[...].reshape(groups * L_ROWS, d)

    def chosen(block, rows, at):
        out_row, src = iota((held, groups * rows), 0), iota((held, groups * rows), 1)
        sel = (out_row < images) & (src // rows == out_row // slots) & (src % rows == at(out_row % slots))
        return nn(flag(sel).astype(BF16), block)

    cond = chosen(all_early, E_ROWS, lambda i: E_COND + i) + chosen(all_early, E_ROWS, lambda i: E_COND + slots + i)
    ids = chosen(all_early, E_ROWS, lambda i: E_IDS)
    img_row, lane = iota((held, d), 0), iota((held, d), 1)

    def id_part(k):
        return jnp.sum(jnp.where(lane == k * slots + img_row % slots, ids, 0.0), axis=1, keepdims=True)

    time_id, class_id = id_part(0), 256.0 * id_part(1) + id_part(2)

    a1, a2, a3 = parts(swish(cond), 3)
    left = jnp.concatenate([a1, a2, a3], axis=0).T
    loads[3].wait()
    loads[4].wait()
    dact = jnp.zeros((held, d), F32)
    bias_rows = []
    for p in range(8):
        if p < 2:
            dmod = chosen(all_late, L_ROWS, lambda i: L_MOD + p * slots + i)
        else:
            dmod = chosen(all_early, E_ROWS, lambda i: E_MOD + (p - 2) * slots + i)
        dmod16 = dmod.astype(BF16)
        grad = nn(left, jnp.concatenate([dmod16] * 3, axis=0))
        if p < 6:
            ada_g_ref[:, p * d : (p + 1) * d] = grad
            w = ada_ref[:, p * d : (p + 1) * d]
        else:
            fada_g_ref[:, (p - 6) * d : (p - 5) * d] = grad
            w = fada_ref[:, (p - 6) * d : (p - 5) * d]
        bias_rows.append(col_sum(dmod))
        dact = dact + nt(dmod16, w)
        if p == 5:
            send(ada_g_ref, ada_g_hbm)
    send(fada_g_ref, fada_g_hbm)
    ada_b_ref[...] = jnp.concatenate(bias_rows[:6], axis=1).reshape(6 * d)
    fada_b_ref[...] = jnp.concatenate(bias_rows[6:], axis=1).reshape(2 * d)
    sig = 1.0 / (1.0 + jnp.exp(-cond))
    dcond = dact * (sig * (1.0 + cond * (1.0 - sig)))
    stack = jnp.concatenate(parts(dcond, 3), axis=0)
    for ref, ids_col, many in ((class_ref, class_id, classes), (time_ref, time_id, bins)):
        wide = -(-many // 128) * 128
        at = iota((held, wide), 1).astype(F32)
        hit = flag((at == ids_col) & (iota((held, wide), 0) < images)).astype(BF16)
        ref[...] = tn(jnp.concatenate([hit, hit, hit], axis=0), stack)[:many]
        if many == classes:
            send(class_ref, class_hbm)

    early, late = jnp.sum(early_ref[...].astype(F32), axis=0), jnp.sum(late_ref[...].astype(F32), axis=0)
    swap = flag(iota((16, 16), 0) == (iota((16, 16), 1) ^ 3)).astype(BF16)

    def swapped(v):
        return tree([nn(swap, p) for p in parts(v, 2)] + [nn(swap, parts(v, 3)[2]), jnp.zeros_like(v)])

    patch_ref[...] = swapped(late[L_PATCH : L_PATCH + 16])
    out_gt_ref[...] = swapped(early[E_OUT : E_OUT + 16])

    def line(v, row):
        return v[row : row + 1, :]

    patch_b_ref[...] = line(late, L_PATCH_B).reshape(d)
    qv_b_ref[...] = jnp.concatenate([line(late, L_Q_B), line(late, L_V_B)], axis=1).reshape(2 * d)
    proj_b_ref[...] = line(early, E_PROJ_B).reshape(d)
    fc1_b_ref[...] = jnp.concatenate([line(early, E_FC1_B + b) for b in range(blocks)], axis=1).reshape(ff)
    fc2_b_ref[...] = line(early, E_FC2_B).reshape(d)
    tail = jnp.broadcast_to(line(early, E_OUT_B)[:, 0:16], (16, 16))
    pick = flag(iota((16, 16), 1) == (iota((16, 16), 0) ^ 3))
    column = jnp.sum(tail * pick, axis=1, keepdims=True)
    out_b_ref[...] = col_sum(jnp.where(iota((16, 16), 0) == iota((16, 16), 1), column, 0.0)).reshape(16)

    half = side // 2
    keep, spread, pick = plane_maps(slots, chans, side, half)
    for k, ref in ((0, lat_ref), (1, out_ref)):
        total = None
        for piece in parts(planes_ref[k], 3 if k == 0 else 1):
            for j in range(2):
                wide = (tn(pick[j], piece) * keep).astype(BF16)
                term = nt(wide, spread[j])
                total = term if total is None else total + term
        ref[...] = total.reshape(ref.shape).astype(ref.dtype)
    for c in stores:
        c.wait()


def finish(bins, classes, latents, grads, early, late, planes, ada_weight, fada_weight, ff):
    d = ada_weight.shape[0]
    f = lambda *shape: jax.ShapeDtypeStruct(shape, F32)
    out_shape = (
        jax.ShapeDtypeStruct(latents.shape, BF16), f(*latents.shape), f(bins, d), f(classes, d), f(16, d), f(d),
        f(d, 6 * d), f(6 * d), f(d, 3 * d), f(2 * d), f(d, d), f(d), f(d, ff), f(ff), f(ff, d), f(d), f(d, 2 * d), f(2 * d),
        f(16, d), f(16),
    )
    large = (3, 6, 8, 12, 14, 16)
    dma = pltpu.SemaphoreType.DMA
    return pl.pallas_call(
        functools.partial(finish_kernel, bins, classes),
        out_shape=out_shape,
        in_specs=[ANY] + [VMEM] * 3 + [ANY] * 2,
        out_specs=tuple(ANY if i in large else VMEM for i in range(len(out_shape))),
        scratch_shapes=[pltpu.VMEM(x.shape, x.dtype) for x in (grads, ada_weight, fada_weight)]
        + [pltpu.VMEM(out_shape[i].shape, F32) for i in large]
        + [dma((5,)), dma((len(large),))],
        compiler_params=pltpu.CompilerParams(vmem_limit_bytes=60 * 1024 * 1024),
        name="finish",
    )(grads, early, late, planes, ada_weight, fada_weight)


def local(
    images, latents, time_bin, class_label, live, time_table, class_table, patch_weight, patch_bias, ada_weight, ada_bias,
    qkv_weight, qv_bias, proj_weight, proj_bias, fc1_weight, fc1_bias, fc2_weight, fc2_bias, final_ada_weight,
    final_ada_bias, out_weight, out_bias, cotangent,
):
    d, ff = qkv_weight.shape[0], fc1_weight.shape[1]
    pos_a, pos_b = position_tables(LATENT // 2, d)
    smalls = (
        time_bin, class_label, live, latents, cotangent, patch_bias, ada_bias, qv_bias, proj_bias, fc1_bias, fc2_bias,
        final_ada_bias, out_bias, jnp.asarray(pos_a), jnp.asarray(pos_b), patch_weight, out_weight.T,
    )
    bigs = (time_table, class_table, ada_weight, final_ada_weight, qkv_weight, proj_weight, fc1_weight, fc2_weight)
    grads, early, late, planes = step(images, smalls, bigs)
    outs = list(
        finish(
            time_table.shape[0], class_table.shape[0], latents, grads, early, late, planes, ada_weight, final_ada_weight, ff
        )
    )
    outs[18] = outs[18].T
    return tuple(outs)


def solution(mesh):
    assert mesh.shape["row"] == 2 and mesh.shape["col"] == 2
    tiles = P("img", None, "row", "col")
    return jax.shard_map(
        functools.partial(local, mesh.shape["img"]),
        mesh=mesh,
        in_specs=(tiles,) + (P("img"),) * 3 + (P(),) * 18 + (tiles,),
        out_specs=(tiles, tiles) + (P(),) * 18,
        check_vma=False,
    )
```

```python
import functools

import jax
import jax.numpy as jnp
import numpy as np
from jax import lax
from jax.experimental import pallas as pl
from jax.experimental.pallas import tpu as pltpu
from jax.sharding import PartitionSpec as P

F32 = jnp.float32
BF16 = jnp.bfloat16
HEADS = 6
LATENT = 64
MESH = pl.DeviceIdType.MESH
VMEM = pl.BlockSpec(memory_space=pltpu.VMEM)
SMEM = pl.BlockSpec(memory_space=pltpu.SMEM)
ANY = pl.BlockSpec(memory_space=pl.ANY)


def nn(a, b):
    return lax.dot_general(a, b, (((1,), (0,)), ((), ())), preferred_element_type=F32)


def nt(a, b):
    return lax.dot_general(a, b, (((1,), (1,)), ((), ())), preferred_element_type=F32)


def tn(a, b):
    return lax.dot_general(a, b, (((0,), (0,)), ((), ())), preferred_element_type=F32)


def parts(v, many):
    out = []
    for _ in range(many):
        piece = v.astype(BF16)
        out.append(piece)
        v = v - piece.astype(F32)
    return out


def iota(shape, dim):
    return lax.broadcasted_iota(jnp.int32, shape, dim)


def flag(cond):
    return jnp.where(cond, 1.0, 0.0)


def swish(v):
    return v / (1.0 + jnp.exp(-v))


def position_tables(grid, width):
    quarter = width // 4
    omega = np.float32(1.0) / np.power(
        np.float32(10000.0), np.arange(quarter, dtype=np.float32) / np.float32(quarter)
    )
    angles = np.arange(grid, dtype=np.float32)[:, None] * omega[None, :].astype(np.float32)
    single = np.concatenate([np.sin(angles), np.cos(angles)], axis=1).astype(np.float32)
    blank = np.zeros_like(single)
    return np.concatenate([single, blank], axis=1), np.concatenate([blank, single], axis=1)


def plane_maps(slots, chans, side, halves):
    rows = slots * chans * side
    lanes = halves * halves
    spread = []
    keep = flag(iota((rows, lanes), 0) % side // 2 == iota((rows, lanes), 1) // halves)
    pick = []
    for j in range(2):
        col = iota((side, lanes), 0)
        spread.append(flag(col == iota((side, lanes), 1) % halves * 2 + j).astype(BF16))
        many = slots * chans * 4
        out, src = iota((many, rows), 0), iota((many, rows), 1)
        same = (out // 4 == src // side) & (out % 4 // 2 == src % 2) & (out % 2 == j)
        pick.append(flag(same).astype(BF16))
    return keep, spread, pick


def shift_masks(halves):
    row, lane = iota((16, halves * halves), 0), iota((16, halves * halves), 1)
    return row % 4 >= 2, row % 2 == 1, lane, halves


def shift_in(planes, masks):
    odd_row, odd_col, lane, side = masks
    full = side * side
    down = [
        jnp.where(
            odd_row,
            jnp.where(lane < side, pltpu.roll(planes[s ^ 2], side, 1), pltpu.roll(planes[s], side, 1)),
            planes[s],
        )
        for s in range(4)
    ]
    return [
        jnp.where(
            odd_col,
            jnp.where(
                lane % side == 0, pltpu.roll(down[s ^ 1], full - side + 1, 1), pltpu.roll(down[s], 1, 1)
            ),
            down[s],
        )
        for s in range(4)
    ]


def shift_out(planes, masks):
    odd_row, odd_col, lane, side = masks
    full = side * side
    up = [
        jnp.where(
            odd_row,
            jnp.where(
                lane >= full - side,
                pltpu.roll(planes[s ^ 2], full - side, 1),
                pltpu.roll(planes[s], full - side, 1),
            ),
            planes[s],
        )
        for s in range(4)
    ]
    return [
        jnp.where(
            odd_col,
            jnp.where(
                lane % side == side - 1, pltpu.roll(up[s ^ 1], side - 1, 1), pltpu.roll(up[s], full - 1, 1)
            ),
            up[s],
        )
        for s in range(4)
    ]


def mate(slot):
    row, col = lax.axis_index("row"), lax.axis_index("col")
    return {"row": row ^ (slot >> 1), "col": col ^ (slot & 1)}


def greet(devices):
    barrier = pltpu.get_barrier_semaphore()
    for device in devices:
        pl.semaphore_signal(barrier, inc=1, device_id=device, device_id_type=MESH)
    pl.semaphore_wait(barrier, len(devices))


def norm(v):
    share = 1.0 / v.shape[-1]
    centred = v - jnp.sum(v, axis=-1, keepdims=True) * share
    spread = jnp.sum(centred * centred, axis=-1, keepdims=True) * share
    inv = lax.rsqrt(spread + 1e-06)
    return centred * inv, inv


def norm_back(hat, inv, grad):
    share = 1.0 / hat.shape[-1]
    first = jnp.sum(grad, axis=-1, keepdims=True) * share
    second = jnp.sum(grad * hat, axis=-1, keepdims=True) * share
    return inv * (grad - first - hat * second)


def col_sum(v):
    return jnp.sum(v, axis=0, keepdims=True)


E_OUT, E_PROJ_B, E_FC2_B, E_FC1_B, E_OUT_B, E_MOD, E_COND, E_IDS, E_ROWS = 0, 16, 17, 18, 22, 23, 41, 47, 48
L_PATCH, L_PATCH_B, L_MOD, L_Q_B, L_V_B, L_ROWS = 0, 16, 17, 23, 24, 32


def tree(terms):
    while len(terms) > 1:
        terms = [terms[i] + terms[i + 1] for i in range(0, len(terms), 2)]
    return terms[0]


class Copies:
    def __init__(self, send_sem, recv_sem):
        self.send_sem, self.recv_sem, self.known = send_sem, recv_sem, {}

    def make(self, key, src, dst, device):
        at = self.known.setdefault(key, len(self.known))
        return pltpu.make_async_remote_copy(
            src_ref=src, dst_ref=dst, send_sem=self.send_sem.at[at], recv_sem=self.recv_sem.at[at],
            device_id=device, device_id_type=MESH,
        )


class Stage:
    def __init__(self, copies, reduce=None):
        self.copies, self.reduce = copies, reduce

    def start(self):
        for c in self.copies():
            c.start()

    def finish(self):
        for c in self.copies():
            c.wait_recv()
        if self.reduce is not None:
            self.reduce()

    def drain(self):
        for c in self.copies():
            c.wait_send()


def far(distance):
    return {"img": lax.axis_index("img") ^ distance}


def rows_at(start, many):
    return pl.ds(pl.multiple_of(start, 16), many)


def ways(images, plan):
    bits = images.bit_length() - 1
    kept = ["".join(x for x in way if not x.isdigit() or int(x) < bits) for way in plan]
    return [way for way in kept if way]


def shared_bits(images, plan):
    return max([int(x) + 1 for way in ways(images, plan) for x in way if x.isdigit()] + [0])


def members(way):
    return 1 << len(way)


def position(way):
    total = 0
    for x in way:
        if x.isdigit():
            side = (lax.axis_index("img") >> int(x)) & 1
        else:
            side = lax.axis_index({"c": "col", "r": "row"}[x])
        total = 2 * total + side
    return total


def partner(way, delta):
    device, flips = {}, 0
    for k, x in enumerate(reversed(way)):
        if delta >> k & 1:
            if x.isdigit():
                flips |= 1 << int(x)
            else:
                name = {"c": "col", "r": "row"}[x]
                device[name] = 1 - lax.axis_index(name)
    if flips:
        device["img"] = lax.axis_index("img") ^ flips
    return device


def group_shapes(images, rows, plan):
    d, shapes = 384, []
    for way in ways(images, plan):
        many = members(way)
        rows //= many
        shapes += [(many - 1, rows, d), (rows, d)]
    high = images >> shared_bits(images, plan)
    if high > 1:
        shapes += [(high - 1, rows, d), (rows, d)]
    return shapes


def group_copies(images, plan):
    return 2 * sum(members(way) - 1 for way in ways(images, plan)) + (images >> shared_bits(images, plan)) - 1


def group_stages(name, images, base, rows, plan, grads, out, bufs, net):
    bufs = list(bufs)
    known = ways(images, plan)
    shared = shared_bits(images, plan)
    high = images >> shared

    def add(*refs):
        return tree([r.astype(F32) for r in refs]).astype(BF16)

    def scatter(k, way, held, many, got, total, last):
        count = members(way)

        def copies():
            return [
                net.make(f"{name}s{k}.{e}", held((position(way) ^ e) * many, many), got.at[e - 1], partner(way, e))
                for e in range(1, count)
            ]

        def reduce():
            total[...] = add(held(position(way) * many, many)[...], *[got[e] for e in range(count - 1)])
            if last:
                out[rows_at(base + start(len(known)), many), :] = total[...]

        return Stage(copies, reduce)

    sizes = [rows]
    for way in known:
        sizes.append(sizes[-1] // members(way))

    def start(level):
        total = 0
        for k in range(level):
            total = total + position(known[k]) * sizes[k + 1]
        return total

    stages = []

    def held(at, many):
        return grads.at[rows_at(base + at, many), :]

    for k, way in enumerate(known):
        got, total = bufs[:2]
        del bufs[:2]
        stages.append(scatter(k, way, held, sizes[k + 1], got, total, high == 1 and k == len(known) - 1))

        def held(at, many, total=total):
            return total.at[rows_at(at, many), :]

    if high > 1:
        got, final = bufs[:2]
        summed, many = total, sizes[-1]

        def copies():
            return [net.make(f"{name}h{e}", summed, got.at[e - 1], far(e << shared)) for e in range(1, high)]

        def reduce():
            final[...] = add(summed[...], *[got[e] for e in range(high - 1)])
            out[rows_at(base + start(len(known)), many), :] = final[...]

        stages.append(Stage(copies, reduce))

    def gather(k, way):
        def copies():
            at = out.at[rows_at(base + start(k + 1), sizes[k + 1]), :]
            return [net.make(f"{name}g{k}.{e}", at, at, partner(way, e)) for e in range(1, members(way))]

        return Stage(copies)

    for k in reversed(range(len(known))):
        stages.append(gather(k, known[k]))
    return stages


def sum_stages(name, images, block, got, total, out, net):
    def c0():
        return [net.make(name + "m" + str(s), block, got.at[s - 1], mate(s)) for s in (1, 2, 3)]

    def r0():
        t = tree([r.astype(F32) for r in (block[...], got[0], got[1], got[2])]).astype(BF16)
        total[...] = t
        out[lax.axis_index("img")] = t

    def c1():
        at = out.at[lax.axis_index("img")]
        return [net.make(name + "i" + str(d), total, at, far(d)) for d in range(1, images)]

    return [Stage(c0, r0), Stage(c1)]


def edge_stages(name, edge, got, out, net):
    def c0():
        return [net.make(name + str(s), edge.at[s], got.at[s - 1], mate(s)) for s in (1, 2, 3)]

    def r0():
        out[...] = tree([r.astype(F32) for r in (edge[0], got[1], got[0], got[2])])

    return [Stage(c0, r0)]


SLOW = (("c", "r", "0", "12"), ("c", "0", "1", "r2"), ("c", "1", "r", "02"))
FAST = (("c", "r0", "12"), ("c", "01", "r2"), ("c", "r1", "02"))
FC, PAIR, EARLY, LATE, EDGE_L = 0, 3, 6, 7, 8
IMAGE_EVENTS = ((2, 0, 1),)
GRAD_EVENTS = ()
BACK_EVENTS = ((1, 0, 2), (1, 1, 1), (1, 2, 1), (3, 0, 3), (3, 6, 1), (4, 1, 2), (4, 2, 2), (5, 0, 4), (5, 3, 1), (6, 1, 3), (6, 2, 3), (7, 0, 5), (7, 3, 2), (8, 1, 4), (8, 2, 4), (8, 4, 1), (8, 6, 2))
TAIL_EVENTS = ((0, 0, 6), (0, 3, 3), (2, 1, 5), (2, 2, 5), (4, 5, 1), (8, 0, 7), (8, 1, 6), (8, 2, 6), (8, 3, 4), (8, 4, 2), (11, 0, 8), (11, 5, 2))
END_EVENTS = (4, 3, 5, 1, 2, 7, 8, 4, 3, 1, 2, 5, 7, 4, 5, 4, 5)


def group_list(d, ff):
    large, rows = 2 * ff // 3, d + d // 3
    out = [(k * large, large, SLOW[k]) for k in range(3)]
    return out + [(2 * ff + k * rows, rows, FAST[k]) for k in range(3)]


def step_kernel(images, count, *refs):
    refs = list(refs)

    def take(n):
        out = refs[:n]
        del refs[:n]
        return out

    (time_ref, class_ref, live_ref, lat_ref, cot_ref, patch_b_ref, ada_b_ref, qv_b_ref, proj_b_ref, fc1_b_ref, fc2_b_ref,
     fada_b_ref, out_b_ref, pos_a_ref, pos_b_ref, patch_w_ref, out_wt_ref) = take(17)
    hbm = take(8)
    out_ref, early_out, late_out, planes_out = take(4)
    held = take(4)
    qkv_ref, proj_ref, fc1_ref, fc2_ref = held
    (planes_ref, mod_s, pt_s, gy_s, wp_s, wo_s, x1_s, x1_b, x1t_s, hat_s, inv_s, k_s, v_s, q_s, e_s, sa_s, sb_s, top_s,
     linv_s, delta_s, of_s, a_s, b_s, dm_s, x2t_s, da_s, dx_s, edge_s,
     grads_ref, early_ref, late_ref, early_16, late_16, edge_l, early_got, early_sum, late_got, late_sum, edge_l_got) = take(39)
    load_sem, gather_send, gather_recv, send_sem, recv_sem = take(5)
    bufs = refs

    d = qkv_ref.shape[0]
    slots, chans, side, _ = lat_ref.shape
    toks = x1_s.shape[0]
    pairs = HEADS // 2
    ff = fc1_ref.shape[1]
    blocks = ff // d
    half = side // 2
    bins, classes = hbm[0].shape[0], hbm[1].shape[0]

    loads = [pltpu.make_async_copy(a, b, load_sem.at[4 + i]) for i, (a, b) in enumerate(zip(hbm[4:], held))]
    net = Copies(send_sem, recv_sem)
    groups = []
    for g, (base, rows, plan) in enumerate(group_list(d, ff)):
        n = len(group_shapes(images, rows, plan))
        groups.append(group_stages("g" + str(g), images, base, rows, plan, grads_ref, out_ref, bufs[:n], net))
        del bufs[:n]
    groups.append(sum_stages("e", images, early_16, early_got, early_sum, early_out, net))
    groups.append(sum_stages("l", images, late_16, late_got, late_sum, late_out, net))
    groups.append(edge_stages("x", edge_l, edge_l_got, planes_out, net))
    def advance(g, k):
        if k > 0:
            groups[g][k - 1].finish()
        if k < len(groups[g]):
            groups[g][k].start()

    def row_of(ref, start, many):
        return ref[...].astype(F32).reshape(1, ref.shape[0])[:, start : start + many]

    early_ref[...] = jnp.zeros_like(early_ref)
    late_ref[...] = jnp.zeros_like(late_ref)

    swap = flag(iota((16, 16), 0) == (iota((16, 16), 1) ^ 3)).astype(BF16)
    wp_s[...] = nn(swap, patch_w_ref[...]).astype(BF16)
    wo_s[...] = nn(swap, out_wt_ref[...]).astype(BF16)
    out_bias = jnp.sum(
        flag(iota((16, 16), 1) == (iota((16, 16), 0) ^ 3)) * row_of(out_b_ref, 0, 16), axis=1, keepdims=True
    )

    inv_lane = iota((toks, 128), 1)

    def opening(time_table_ref, class_table_ref, ada_ref, fada_ref, pos_s):
        tables = [
            pltpu.make_async_copy(a, b, load_sem.at[i])
            for i, (a, b) in enumerate(zip(hbm[:4], (time_table_ref, class_table_ref, ada_ref, fada_ref)))
        ]
        for c in tables + loads:
            c.start()
        greet([mate(s) for s in (1, 2, 3)] + [far(k) for k in range(1, images)])
        keep, spread, pick = plane_maps(slots, chans, side, half)
        for k, ref in enumerate((lat_ref, cot_ref)):
            tile = ref[...].reshape(slots * chans * side, side)
            total = None
            for j in range(2):
                wide = (nn(tile, spread[j]) * keep).astype(BF16)
                term = nn(pick[j], wide)
                total = term if total is None else total + term
            planes_ref[0, k] = total.astype(BF16)
        gathers = []
        for s in (1, 2, 3):
            c = pltpu.make_async_remote_copy(
                src_ref=planes_ref.at[0], dst_ref=planes_ref.at[s], send_sem=gather_send.at[s - 1], recv_sem=gather_recv.at[s - 1],
                device_id=mate(s), device_id_type=MESH,
            )
            c.start()
            gathers.append(c)

        my_row, my_col = lax.axis_index("row"), lax.axis_index("col")
        patch_b = row_of(patch_b_ref, 0, d)
        for s in range(4):
            ta = pos_a_ref[pl.ds(pl.multiple_of((my_row ^ (s >> 1)) * half, half), half), :]
            tb = pos_b_ref[pl.ds(pl.multiple_of((my_col ^ (s & 1)) * half, half), half), :] + patch_b
            for a in range(half):
                pos_s[s, a * half : (a + 1) * half, :] = ta[a : a + 1, :] + tb

        def onehot(ids_ref, many):
            row, lane = iota((16, many), 0), iota((16, many), 1)
            hit = jnp.zeros((16, many), F32)
            for i in range(slots):
                hit = hit + flag((row == i) & (lane == ids_ref[i]))
            return hit.astype(BF16)

        for c in tables:
            c.wait()
        cond = nn(onehot(time_ref, bins), time_table_ref[...]) + nn(onehot(class_ref, classes), class_table_ref[...])
        cond = cond[:8]
        act = parts(swish(cond), 3)
        act = jnp.concatenate([p.astype(F32) for p in act] + [jnp.zeros((8, d), F32)], axis=0).astype(BF16)
        for p in range(8):
            w = ada_ref[:, p * d : (p + 1) * d] if p < 6 else fada_ref[:, (p - 6) * d : (p - 5) * d]
            m = nn(act, w)
            b = row_of(ada_b_ref, p * d, d) if p < 6 else row_of(fada_b_ref, (p - 6) * d, d)
            mod_s[p] = m[0:8] + m[8:16] + m[16:24] + b
        row, lane = iota((8, d), 0), iota((8, d), 1)
        ids = jnp.zeros((8, d), F32)
        for i in range(slots):
            for k, v in enumerate((time_ref[i], class_ref[i] // 256, class_ref[i] % 256)):
                ids = ids + jnp.where((row == 0) & (lane == k * slots + i), 0.25 * v.astype(F32), 0.0)
        high = cond.astype(BF16).astype(F32)
        early_ref[E_COND : E_COND + slots, :] = 0.25 * high[:slots]
        early_ref[E_COND + slots : E_COND + 2 * slots, :] = 0.25 * (cond - high)[:slots]
        early_ref[E_IDS : E_IDS + 1, :] = ids[0:1]

        for c in gathers:
            c.wait_recv()
        masks = shift_masks(half)
        live = [live_ref[i].astype(F32) for i in range(slots)]
        for i in range(slots):
            lat = shift_in([planes_ref[s, 0, i * 16 : (i + 1) * 16, :].astype(F32) for s in range(4)], masks)
            cot = shift_in([planes_ref[s, 1, i * 16 : (i + 1) * 16, :].astype(F32) for s in range(4)], masks)
            for s in range(4):
                pt_s[i * 4 + s] = lat[s].astype(BF16)
            gy_s[i] = (cot[0] * live[i]).astype(BF16)

        v_bias = row_of(qv_b_ref, d, d)

        def token_norm(t, x1_buf):
            img, slot = t // 4, t % 4
            tok = tn(pt_s[t], wp_s[...]) + pos_s[slot]
            dx_s[img] = tok
            hat, inv = norm(tok)
            hat_s[t] = hat
            inv_s[...] = jnp.where(inv_lane == t, inv, inv_s[...])
            x1_buf[...] = (hat * (1.0 + mod_s[1, pl.ds(img, 1), :]) + mod_s[0, pl.ds(img, 1), :]).astype(BF16)

        def token_keys(t, x1_buf):
            img, slot = t // 4, t % 4
            x1 = x1_buf[...]
            keys = nn(x1, qkv_ref[:, d : 2 * d]).astype(BF16)
            vals = (nn(x1, qkv_ref[:, 2 * d :]) + v_bias).astype(BF16)
            for p in range(pairs):
                k_s[img * pairs + p, slot] = keys[:, p * 128 : (p + 1) * 128]
                v_s[img * pairs + p, slot] = vals[:, p * 128 : (p + 1) * 128]
            x1t_s[t] = x1.T

        def reverse(n):
            return n // 4 * 4 + 3 - n % 4

        token_norm(jnp.int32(3), x1_s)
        loads[0].wait()

        def tokens(n, carry):
            token_norm(reverse(2 * n + 1), x1_b)
            token_keys(reverse(2 * n), x1_s)
            token_norm(reverse(jnp.minimum(2 * n + 2, slots * 4 - 1)), x1_s)
            token_keys(reverse(2 * n + 1), x1_b)
            return carry

        lax.fori_loop(0, slots * 2, tokens, 0)

        for c in gathers:
            c.wait_send()

    pl.run_scoped(
        opening,
        *[pltpu.VMEM(hbm[i].shape, BF16) for i in range(4)],
        pltpu.VMEM((4, toks, d), F32),
    )
    masks = shift_masks(half)

    lane128 = iota((1, 128), 1) // 64
    head_mask = [flag(lane128 == h) for h in range(2)]

    q_bias = row_of(qv_b_ref, 0, d)

    def queries(img, carry):
        query = tn(x1t_s[img * 4], qkv_ref[:, :d]) + q_bias
        query = query.astype(BF16).astype(F32) * 0.125
        for p in range(pairs):
            for h in range(2):
                q_s[img * HEADS + p * 2 + h] = (query[:, p * 128 : (p + 1) * 128] * head_mask[h]).astype(BF16)
        return carry

    lax.fori_loop(0, slots, queries, 0)

    def scores(idx, h, buf):
        top = None
        for c in range(4):
            s = nt(k_s[idx, c], q_s[idx * 2 + h])
            buf[c] = s
            m = jnp.max(s, axis=0, keepdims=True)
            top = m if top is None else jnp.maximum(top, m)
        top_s[h] = top

    def softmax(idx, h, buf, vt):
        head = idx * 2 + h
        top, total, acc = top_s[h], None, None
        for c in range(4):
            e = jnp.exp(buf[c] - top)
            l = col_sum(e)
            total = l if total is None else total + l
            eb = e.astype(BF16)
            e_s[head, c] = eb
            o = nn(vt[c][h * 64 : (h + 1) * 64], eb)
            acc = o if acc is None else acc + o
        linv = 1.0 / total
        linv_s[head] = linv
        of_s[head] = acc * linv

    scores(jnp.int32(0), 0, sa_s)

    def attend(idx, carry):
        vt = [v_s[idx, c].T for c in range(4)]
        scores(idx, 1, sb_s)
        softmax(idx, 0, sa_s, vt)
        scores(jnp.minimum(idx + 1, slots * pairs - 1), 0, sa_s)
        softmax(idx, 1, sb_s, vt)
        return carry

    lax.fori_loop(0, slots * pairs, attend, 0)
    for c in loads[1:]:
        c.wait()
    proj_b, fc1_b, fc2_b = row_of(proj_b_ref, 0, d), row_of(fc1_b_ref, 0, ff), row_of(fc2_b_ref, 0, d)

    def closing(dot_s, dom_s, dq_s, dxq_s, acc_s, dx1_s):
        def pair_row(k):
            return 2 * ff + k * (d + d // 3)

        def wide(ref, img, b):
            return jnp.concatenate([ref[img * 12 + b * 3 + j] for j in range(3)], axis=1)

        def fc2_grad(b, carry):
            total = tree([tn(wide(a_s, img, b), dm_s[img]) for img in range(2)])
            for img in range(2, slots):
                total = total + tn(wide(a_s, img, b), dm_s[img])
            grads_ref[rows_at(b * d, d), :] = total.astype(BF16)
            started(b, 0)
            return carry

        def started(b, before):
            for g in range(FC, PAIR):
                last = -(-(g + 1) * (2 * ff // 3) // d) - 1 - before
                if 0 <= last < blocks:

                    @pl.when(b == last)
                    def _():
                        advance(g, 0)

        def when_at(i, plan):
            for at, events in plan.items():

                @pl.when(i == at)
                def _():
                    for g, k in events:
                        advance(g, k)

        image_plan, grad_plan, back_plan, tail_plan = {}, {}, {}, {}
        for plan, events in ((image_plan, IMAGE_EVENTS), (grad_plan, GRAD_EVENTS), (back_plan, BACK_EVENTS), (tail_plan, TAIL_EVENTS)):
            for at, g, k in events:
                if k <= len(groups[g]):
                    plan.setdefault(at, []).append((g, k))

        def inv_at(t):
            return jnp.sum(jnp.where(inv_lane == t, inv_s[...], 0.0), axis=1, keepdims=True)

        def image(img, carry):
            def mod_row(p):
                return mod_s[p, pl.ds(img, 1), :]

            ot = jnp.concatenate([of_s[img * HEADS + h] for h in range(HEADS)], axis=0).astype(BF16)
            branch = tn(ot, proj_ref[...]) + proj_b
            g1 = mod_row(2)
            resid = dx_s[img] + g1 * branch
            hat2, inv2 = norm(resid)
            sa_s[img] = hat2[:, :toks]
            sb_s[img, :, : d - toks] = hat2[:, toks:]
            inv_s[...] = jnp.where(inv_lane == slots * 4 + img, inv2, inv_s[...])
            x2 = (hat2 * (1.0 + mod_row(4)) + mod_row(3)).astype(BF16)
            x2t_s[img] = x2.T
            mlp = jnp.zeros((toks, d), F32)
            k0, k1 = 0.7978845608028654, 0.044715
            def first(b):
                return nn(x2, fc1_ref[:, b * d : (b + 1) * d])

            u = first(0)
            for b in range(blocks):
                at_b = slice(b * d, (b + 1) * d)
                ahead = first(b + 1) if b + 1 < blocks else None
                u = u + fc1_b[:, at_b]
                sq = u * u
                inner = k0 + (k0 * k1) * sq
                cdf = 0.5 + 0.5 * jnp.tanh(u * inner)
                hidden = u * cdf
                slope = cdf + (hidden - hidden * cdf) * (6.0 * inner - 4.0 * k0)
                hidden = hidden.astype(BF16)
                slope = slope.astype(BF16)
                for j in range(3):
                    a_s[img * 12 + b * 3 + j] = hidden[:, j * 128 : (j + 1) * 128]
                    b_s[img * 12 + b * 3 + j] = slope[:, j * 128 : (j + 1) * 128]
                mlp = mlp + nn(hidden, fc2_ref[at_b, :])
                u = ahead
            mlp = mlp + fc2_b
            g2 = mod_row(5)
            x3 = resid + g2 * mlp
            hatf, invf = norm(x3)
            scf = 1.0 + mod_row(7)
            xf = (hatf * scf + mod_row(6)).astype(BF16)
            edge_s[4, img] = (nt(wo_s[...], xf) + out_bias) * live_ref[img].astype(F32)
            gy = gy_s[img]
            early_ref[E_OUT : E_OUT + 16, :] += nn(gy, xf)
            early_ref[E_OUT_B : E_OUT_B + 1, 0:16] += nt(jnp.ones((8, toks), BF16), gy)[0:1]
            dxf = tn(gy, wo_s[...])

            def put_mod(p, v):
                early_ref[pl.ds(E_MOD + (p - 2) * slots + img, 1), :] = v

            put_mod(6, col_sum(dxf))
            put_mod(7, col_sum(dxf * hatf))
            dx3 = norm_back(hatf, invf, dxf * scf)
            dm = (g2 * dx3).astype(BF16)
            dm_s[img] = dm
            put_mod(5, col_sum(mlp * dx3))
            early_ref[E_FC2_B : E_FC2_B + 1, :] += col_sum(dm.astype(F32))
            dx_s[img] = dx3
            return carry

        lax.fori_loop(0, slots, image, 0)
        lax.fori_loop(0, blocks, fc2_grad, 0)

        def image_back(img, carry):
            when_at(img, image_plan)

            def mod_row(p):
                return mod_s[p, pl.ds(img, 1), :]

            def put_mod(p, v):
                early_ref[pl.ds(E_MOD + (p - 2) * slots + img, 1), :] = v

            g1, dm = mod_row(2), dm_s[img]
            hat2 = jnp.concatenate([sa_s[img], sb_s[img, :, : d - toks]], axis=1)
            inv2 = inv_at(slots * 4 + img)
            dx2 = jnp.zeros((toks, d), F32)
            def second(b):
                return nt(dm, fc2_ref[b * d : (b + 1) * d, :])

            dh = second(0)
            for b in range(blocks):
                ahead = second(b + 1) if b + 1 < blocks else None
                slope = jnp.concatenate([b_s[img * 12 + b * 3 + j] for j in range(3)], axis=1).astype(F32)
                du = (dh * slope).astype(BF16)
                for j in range(3):
                    b_s[img * 12 + b * 3 + j] = du[:, j * 128 : (j + 1) * 128]
                early_ref[E_FC1_B + b : E_FC1_B + b + 1, :] += col_sum(du.astype(F32))
                dx2 = dx2 + nt(du, fc1_ref[:, b * d : (b + 1) * d])
                dh = ahead
            put_mod(3, col_sum(dx2))
            put_mod(4, col_sum(dx2 * hat2))
            dx = dx_s[img] + norm_back(hat2, inv2, dx2 * (1.0 + mod_row(4)))
            dx_s[img] = dx
            ot = jnp.concatenate([of_s[img * HEADS + h] for h in range(HEADS)], axis=0).astype(BF16)
            branch = tn(ot, proj_ref[...]) + proj_b
            put_mod(2, col_sum(branch * dx))
            da = (g1 * dx).astype(BF16)
            da_s[img] = da
            early_ref[E_PROJ_B : E_PROJ_B + 1, :] += col_sum(da.astype(F32))
            dot = nt(proj_ref[...], da)
            blank = jnp.zeros((64, toks), F32)
            for hd in range(HEADS):
                head = img * HEADS + hd
                piece = dot[hd * 64 : (hd + 1) * 64]
                linv = linv_s[head]
                delta_s[head] = col_sum(piece * of_s[head]) * linv
                piece = piece * linv
                wide = jnp.concatenate([piece, blank] if hd % 2 == 0 else [blank, piece], axis=0).astype(BF16)
                dot_s[head] = wide
                dom_s[head] = wide.T
            return carry

        lax.fori_loop(0, slots, image_back, 0)

        def fc1_grad(b, carry):
            when_at(b, grad_plan)
            total = tree([nn(x2t_s[img], wide(b_s, img, b)) for img in range(2)])
            for img in range(2, slots):
                total = total + nn(x2t_s[img], wide(b_s, img, b))
            grads_ref[rows_at(ff + b * d, d), :] = total.astype(BF16)
            started(b, blocks)
            return carry

        lax.fori_loop(0, blocks, fc1_grad, 0)
        total = None
        for img in range(slots):
            ot = jnp.concatenate([of_s[img * HEADS + h] for h in range(HEADS)], axis=0).astype(BF16)
            term = nn(ot, da_s[img])
            total = term if total is None else total + term
        for k in range(pairs):
            grads_ref[pair_row(k) + d : pair_row(k + 1), :] = total[k * (d // 3) : (k + 1) * (d // 3)].astype(BF16)
        blank = jnp.zeros((16, toks), F32)
        for i in range(slots):
            out = shift_out([edge_s[4, i], blank, blank, blank], masks)
            for s in range(4):
                edge_l[s, 1, i * 16 : (i + 1) * 16, :] = out[s].astype(BF16)
        early_16[...] = early_ref[...].astype(BF16)
        advance(EARLY, 0)

        acc_s[...] = jnp.zeros_like(acc_s)

        def attend_back(it, carry):
            when_at(it, back_plan)
            p, img = it // slots, it % slots
            idx = img * pairs + p
            dqt = [None, None]
            jobs = [(c, h) for c in range(4) for h in range(2)]

            def product(job):
                return nn(v_s[idx, job[0]], dot_s[idx * 2 + job[1]])

            dp = product(jobs[0])
            gathered = None
            sum_v = None
            for n, (c, h) in enumerate(jobs):
                head = idx * 2 + h
                ahead = product(jobs[n + 1]) if n + 1 < len(jobs) else None
                if h == 0:
                    kt = k_s[idx, c].T
                    dk, dv = None, None
                e = e_s[head, c]
                ds = (e.astype(F32) * (dp - delta_s[head])).astype(BF16)
                dk_h, dv_h = nn(ds, q_s[head]), nn(e, dom_s[head])
                dk = dk_h if dk is None else dk + dk_h
                dv = dv_h if dv is None else dv + dv_h
                dq_h = nn(kt[h * 64 : (h + 1) * 64], ds)
                dqt[h] = dq_h if dqt[h] is None else dqt[h] + dq_h
                dp = ahead
                if h == 1:
                    dk, dv = dk.astype(BF16), dv.astype(BF16)
                    a_s[idx * 4 + c] = dk
                    b_s[idx * 4 + c] = dv
                    sv = col_sum(dv.astype(F32))
                    sum_v = sv if sum_v is None else sum_v + sv
                    term = nn(x1t_s[img * 4 + c], jnp.concatenate([dk, dv], axis=1))
                    gathered = term if gathered is None else gathered + term
            dq = (jnp.concatenate(dqt, axis=0) * 0.125).T.astype(BF16)
            dq_s[idx] = dq
            lanes = pl.ds(pl.multiple_of(p * 128, 128), 128)
            late_ref[L_V_B : L_V_B + 1, lanes] += sum_v
            late_ref[L_Q_B : L_Q_B + 1, lanes] += col_sum(dq.astype(F32))
            acc_s[:, 128:] += gathered
            acc_s[:, :128] += nn(x1t_s[img * 4], dq)

            for pair in range(pairs):

                @pl.when(it == pair * slots + slots - 1)
                def _():
                    at = pair_row(pair)
                    grads_ref[at : at + d, :] = acc_s[...].astype(BF16)
                    acc_s[...] = jnp.zeros_like(acc_s)
                    advance(PAIR + pair, 0)

            return carry

        lax.fori_loop(0, slots * pairs, attend_back, 0)

        def joined(ref, img, slot):
            return [ref[(img * pairs + p) * 4 + slot] for p in range(pairs)]

        def query_back(img, carry):
            dq = jnp.concatenate([dq_s[img * pairs + p] for p in range(pairs)], axis=1)
            dxq_s[img] = nt(dq, qkv_ref[:, :d])
            return carry

        lax.fori_loop(0, slots, query_back, 0)

        def product_back(t):
            img, slot = t // 4, t % 4
            dkv = jnp.concatenate(joined(a_s, img, slot) + joined(b_s, img, slot), axis=1)
            own = jnp.where(slot == 0, 1.0, 0.0)
            return nt(dkv, qkv_ref[:, d:]) + dxq_s[img] * own

        dx1_s[...] = product_back(jnp.int32(0))
        def tokens_back(t, carry):
            when_at(t, tail_plan)
            img, slot = t // 4, t % 4
            dx1 = dx1_s[...]
            ahead = product_back(jnp.minimum(t + 1, slots * 4 - 1))
            hat = hat_s[t]
            late_ref[pl.ds(L_MOD + img, 1), :] += col_sum(dx1)
            late_ref[pl.ds(L_MOD + slots + img, 1), :] += col_sum(dx1 * hat)
            own = jnp.where(slot == 0, 1.0, 0.0)
            dtok = norm_back(hat, inv_at(t), dx1 * (1.0 + mod_s[1, pl.ds(img, 1), :])) + dx_s[img] * own
            late_ref[L_PATCH_B : L_PATCH_B + 1, :] += col_sum(dtok)
            dtok = dtok.astype(BF16)
            late_ref[L_PATCH : L_PATCH + 16, :] += nn(pt_s[t], dtok)
            for p in range(pairs):
                a_s[(img * pairs + p) * 4 + slot] = dtok[:, p * 128 : (p + 1) * 128]
            dx1_s[...] = ahead
            return carry

        lax.fori_loop(0, slots * 4, tokens_back, 0)

    pl.run_scoped(
        closing,
        pltpu.VMEM((slots * HEADS, 128, toks), BF16),
        pltpu.VMEM((slots * HEADS, toks, 128), BF16),
        pltpu.VMEM((slots * pairs, toks, 128), BF16),
        pltpu.VMEM((slots, toks, d), F32),
        pltpu.VMEM((d, d), F32),
        pltpu.VMEM((toks, d), F32),
    )

    late_16[...] = late_ref[...].astype(BF16)
    advance(LATE, 0)

    def edges(t, carry):
        img, slot = t // 4, t % 4
        dtok = jnp.concatenate([a_s[(img * pairs + p) * 4 + slot] for p in range(pairs)], axis=1)
        edge_s[slot, img] = nt(wp_s[...], dtok)
        return carry

    lax.fori_loop(0, slots * 4, edges, 0)
    for i in range(slots):
        lat = shift_out([edge_s[s, i] for s in range(4)], masks)
        for s in range(4):
            edge_l[s, 0, i * 16 : (i + 1) * 16, :] = lat[s].astype(BF16)
    advance(EDGE_L, 0)
    state = {g: 1 for g in (LATE, EDGE_L)}
    for g in (*range(FC, PAIR + 3), EARLY):
        done = [k for events in (IMAGE_EVENTS, GRAD_EVENTS, BACK_EVENTS, TAIL_EVENTS) for _, h, k in events if h == g]
        assert done == list(range(1, len(done) + 1))
        state[g] = len(done) + 1
    order = list(END_EVENTS)
    order += [g for g in state for _ in range(len(groups[g]))]
    drained = {g: 0 for g in state}
    for g in order:
        if state[g] <= len(groups[g]):
            for h, stages in enumerate(groups):
                while drained[h] < state[h] - 1 - (h == g):
                    stages[drained[h]].drain()
                    drained[h] += 1
            advance(g, state[g])
            state[g] += 1
    for h, stages in enumerate(groups):
        for stage in stages[drained[h] :]:
            stage.drain()
    assert len(net.known) <= count


def step(images, smalls, bigs):
    time_bin, latents = smalls[0], smalls[3]
    qkv_weight, fc1_weight = bigs[4], bigs[6]
    d, ff = qkv_weight.shape[0], fc1_weight.shape[1]
    slots, chans, side, _ = latents.shape
    toks = side * side // 4
    planes = slots * chans * 4
    pairs = HEADS // 2
    heads = slots * HEADS
    out_shape = (
        jax.ShapeDtypeStruct((2 * ff + 4 * d, d), BF16),
        jax.ShapeDtypeStruct((images, E_ROWS, d), BF16),
        jax.ShapeDtypeStruct((images, L_ROWS, d), BF16),
        jax.ShapeDtypeStruct((2, planes, toks), F32),
    )
    scratch = [(w.shape, w.dtype) for w in bigs[4:]] + [
        ((4, 2, planes, toks), BF16), ((8, 8, d), F32), ((slots * 4, 16, toks), BF16),
        ((slots, 16, toks), BF16), ((16, d), BF16), ((16, d), BF16), ((toks, d), BF16), ((toks, d), BF16), ((slots * 4, d, toks), BF16),
        ((slots * 4, toks, d), F32), ((toks, 128), F32), ((slots * pairs, 4, toks, 128), BF16),
        ((slots * pairs, 4, toks, 128), BF16), ((heads, toks, 128), BF16), ((heads, 4, toks, toks), BF16),
        ((4, toks, toks), F32), ((4, toks, toks), F32), ((2, 1, toks), F32), ((heads, 1, toks), F32), ((heads, 1, toks), F32),
        ((heads, 64, toks), F32), ((slots * 12, toks, 128), BF16), ((slots * 12, toks, 128), BF16),
        ((slots, toks, d), BF16), ((slots, d, toks), BF16), ((slots, toks, d), BF16),
        ((slots, toks, d), F32), ((5, slots, 16, toks), F32),
        ((2 * ff + 4 * d, d), BF16), ((E_ROWS, d), F32), ((L_ROWS, d), F32), ((E_ROWS, d), BF16), ((L_ROWS, d), BF16), ((4, 2, planes, toks), BF16),
        ((3, E_ROWS, d), BF16), ((E_ROWS, d), BF16), ((3, L_ROWS, d), BF16), ((L_ROWS, d), BF16), ((3, 2, planes, toks), BF16),
    ]
    dma = pltpu.SemaphoreType.DMA
    parts_of = group_list(d, ff)
    count = sum(group_copies(images, plan) for _, _, plan in parts_of) + 2 * (3 + images - 1) + 6
    moved = [(s, BF16) for _, rows, plan in parts_of for s in group_shapes(images, rows, plan)]
    return pl.pallas_call(
        functools.partial(step_kernel, images, count),
        out_shape=out_shape,
        in_specs=[SMEM] * 3 + [VMEM] * (len(smalls) - 3) + [ANY] * len(bigs),
        out_specs=(VMEM,) * 4,
        scratch_shapes=[pltpu.VMEM(shape, kind) for shape, kind in scratch]
        + [dma((len(bigs),)), dma((3,)), dma((3,)), dma((count,)), dma((count,))]
        + [pltpu.VMEM(shape, kind) for shape, kind in moved],
        compiler_params=pltpu.CompilerParams(
            collective_id=0, has_side_effects=True, vmem_limit_bytes=64 * 1024 * 1024 - 65536
        ),
        name="step",
    )(*smalls, *bigs)


def finish_kernel(
    bins, classes, grads_hbm, early_ref, late_ref, planes_ref, ada_hbm, fada_hbm,
    out_ref, lat_ref, time_ref, class_hbm, patch_ref, patch_b_ref, ada_g_hbm, ada_b_ref, qkv_g_hbm, qv_b_ref, proj_g_ref,
    proj_b_ref, fc1_g_hbm, fc1_b_ref, fc2_g_hbm, fc2_b_ref, fada_g_hbm, fada_b_ref, out_gt_ref, out_b_ref,
    grads_ref, ada_ref, fada_ref, class_ref, ada_g_ref, qkv_g_ref, fc1_g_ref, fc2_g_ref, fada_g_ref, in_sem, out_sem,
):
    d = ada_ref.shape[0]
    ff = fc1_g_ref.shape[1]
    blocks = ff // d
    pairs = HEADS // 2
    slots, chans, side, _ = lat_ref.shape
    groups = early_ref.shape[0]
    images = groups * slots
    held = -(-images // 32) * 32

    bounds = [0, ff, 2 * ff, 2 * ff + 4 * d]
    loads = [
        pltpu.make_async_copy(grads_hbm.at[a:b, :], grads_ref.at[a:b, :], in_sem.at[i])
        for i, (a, b) in enumerate(zip(bounds[:-1], bounds[1:]))
    ]
    loads += [pltpu.make_async_copy(ada_hbm, ada_ref, in_sem.at[3]), pltpu.make_async_copy(fada_hbm, fada_ref, in_sem.at[4])]
    for c in loads:
        c.start()
    stores = []

    def send(src, dst):
        c = pltpu.make_async_copy(src, dst, out_sem.at[len(stores)])
        c.start()
        stores.append(c)

    loads[0].wait()
    fc2_g_ref[...] = grads_ref[0:ff, :].astype(F32)
    send(fc2_g_ref, fc2_g_hbm)
    loads[1].wait()
    for b in range(blocks):
        fc1_g_ref[:, b * d : (b + 1) * d] = grads_ref[ff + b * d : ff + (b + 1) * d, :].astype(F32)
    send(fc1_g_ref, fc1_g_hbm)
    loads[2].wait()
    third = d // 3
    for p in range(pairs):
        at = 2 * ff + p * (d + third)
        proj_g_ref[p * third : (p + 1) * third, :] = grads_ref[at + d : at + d + third, :].astype(F32)
        for k in range(3):
            lanes = slice(k * d + p * 128, k * d + (p + 1) * 128)
            qkv_g_ref[:, lanes] = grads_ref[at : at + d, k * 128 : (k + 1) * 128].astype(F32)
    send(qkv_g_ref, qkv_g_hbm)

    all_early = early_ref[...].reshape(groups * E_ROWS, d)
    all_late = late_ref[...].reshape(groups * L_ROWS, d)

    def chosen(block, rows, starts, steps):
        many = len(starts) * held
        line = iota((many, 1), 0)
        image = line % held
        item = line // held
        start, step = jnp.zeros_like(line), jnp.zeros_like(line)
        for k, (at, by) in enumerate(zip(starts, steps)):
            start = jnp.where(item == k, at, start)
            step = jnp.where(item == k, by, step)
        want = jnp.where(image < images, image // slots * rows + start + step * (image % slots), -1)
        return nn(flag(iota((many, groups * rows), 1) == want).astype(BF16), block)

    starts = [E_COND, E_COND + slots, E_IDS] + [E_MOD + k * slots for k in range(6)]
    picked = chosen(all_early, E_ROWS, starts, [1, 1, 0] + [1] * 6)
    items = [picked[k * held : (k + 1) * held] for k in range(9)]
    cond, ids = items[0] + items[1], items[2]
    picked = chosen(all_late, L_ROWS, [L_MOD, L_MOD + slots], [1, 1])
    dmods = [picked[:held], picked[held:]] + items[3:]
    img_row, lane = iota((held, d), 0), iota((held, d), 1)

    def id_part(k):
        return jnp.sum(jnp.where(lane == k * slots + img_row % slots, ids, 0.0), axis=1, keepdims=True)

    time_id, class_id = id_part(0), 256.0 * id_part(1) + id_part(2)

    left = jnp.concatenate(parts(swish(cond), 2), axis=0).T
    loads[3].wait()
    loads[4].wait()
    dact = jnp.zeros((held, d), F32)
    for p in range(0, 8, 2):
        pair = jnp.concatenate([dmods[p], dmods[p + 1]], axis=1).astype(BF16)
        grad = nn(left, jnp.concatenate([pair, pair], axis=0))
        if p < 6:
            lanes = slice(p * d, (p + 2) * d)
            ada_g_ref[:, lanes] = grad
            w = ada_ref[:, lanes]
        else:
            fada_g_ref[...] = grad
            w = fada_ref[...]
        dact = dact + nt(pair, w)
        if p == 4:
            send(ada_g_ref, ada_g_hbm)
    send(fada_g_ref, fada_g_hbm)
    bias_rows = [col_sum(v) for v in dmods]
    ada_b_ref[...] = jnp.concatenate(bias_rows[:6], axis=1).reshape(6 * d)
    fada_b_ref[...] = jnp.concatenate(bias_rows[6:], axis=1).reshape(2 * d)
    sig = 1.0 / (1.0 + jnp.exp(-cond))
    dcond = dact * (sig * (1.0 + cond * (1.0 - sig)))
    stack = jnp.concatenate(parts(dcond, 2), axis=0)
    for ref, ids_col, many in ((class_ref, class_id, classes), (time_ref, time_id, bins)):
        wide = -(-many // 128) * 128
        at = iota((held, wide), 1).astype(F32)
        hit = flag((at == ids_col) & (iota((held, wide), 0) < images)).astype(BF16)
        ref[...] = tn(jnp.concatenate([hit, hit], axis=0), stack)[:many]
        if many == classes:
            send(class_ref, class_hbm)

    early, late = jnp.sum(early_ref[...].astype(F32), axis=0), jnp.sum(late_ref[...].astype(F32), axis=0)
    swap = flag(iota((16, 16), 0) == (iota((16, 16), 1) ^ 3)).astype(BF16)

    def swapped(v):
        return tree([nn(swap, p) for p in parts(v, 2)] + [nn(swap, parts(v, 3)[2]), jnp.zeros_like(v)])

    patch_ref[...] = swapped(late[L_PATCH : L_PATCH + 16])
    out_gt_ref[...] = swapped(early[E_OUT : E_OUT + 16])

    def line(v, row):
        return v[row : row + 1, :]

    patch_b_ref[...] = line(late, L_PATCH_B).reshape(d)
    qv_b_ref[...] = jnp.concatenate([line(late, L_Q_B), line(late, L_V_B)], axis=1).reshape(2 * d)
    proj_b_ref[...] = line(early, E_PROJ_B).reshape(d)
    fc1_b_ref[...] = jnp.concatenate([line(early, E_FC1_B + b) for b in range(blocks)], axis=1).reshape(ff)
    fc2_b_ref[...] = line(early, E_FC2_B).reshape(d)
    tail = jnp.broadcast_to(line(early, E_OUT_B)[:, 0:16], (16, 16))
    pick = flag(iota((16, 16), 1) == (iota((16, 16), 0) ^ 3))
    column = jnp.sum(tail * pick, axis=1, keepdims=True)
    out_b_ref[...] = col_sum(jnp.where(iota((16, 16), 0) == iota((16, 16), 1), column, 0.0)).reshape(16)

    half = side // 2
    keep, spread, pick = plane_maps(slots, chans, side, half)
    for k, ref in ((0, lat_ref), (1, out_ref)):
        total = None
        for piece in parts(planes_ref[k], 3 if k == 0 else 1):
            for j in range(2):
                wide = (tn(pick[j], piece) * keep).astype(BF16)
                term = nt(wide, spread[j])
                total = term if total is None else total + term
        ref[...] = total.reshape(ref.shape).astype(ref.dtype)
    for c in stores:
        c.wait()


def finish(bins, classes, latents, grads, early, late, planes, ada_weight, fada_weight, ff):
    d = ada_weight.shape[0]
    f = lambda *shape: jax.ShapeDtypeStruct(shape, F32)
    out_shape = (
        jax.ShapeDtypeStruct(latents.shape, BF16), f(*latents.shape), f(bins, d), f(classes, d), f(16, d), f(d),
        f(d, 6 * d), f(6 * d), f(d, 3 * d), f(2 * d), f(d, d), f(d), f(d, ff), f(ff), f(ff, d), f(d), f(d, 2 * d), f(2 * d),
        f(16, d), f(16),
    )
    large = (3, 6, 8, 12, 14, 16)
    dma = pltpu.SemaphoreType.DMA
    return pl.pallas_call(
        functools.partial(finish_kernel, bins, classes),
        out_shape=out_shape,
        in_specs=[ANY] + [VMEM] * 3 + [ANY] * 2,
        out_specs=tuple(ANY if i in large else VMEM for i in range(len(out_shape))),
        scratch_shapes=[pltpu.VMEM(x.shape, x.dtype) for x in (grads, ada_weight, fada_weight)]
        + [pltpu.VMEM(out_shape[i].shape, F32) for i in large]
        + [dma((5,)), dma((len(large),))],
        compiler_params=pltpu.CompilerParams(vmem_limit_bytes=60 * 1024 * 1024),
        name="finish",
    )(grads, early, late, planes, ada_weight, fada_weight)


def local(
    images, latents, time_bin, class_label, live, time_table, class_table, patch_weight, patch_bias, ada_weight, ada_bias,
    qkv_weight, qv_bias, proj_weight, proj_bias, fc1_weight, fc1_bias, fc2_weight, fc2_bias, final_ada_weight,
    final_ada_bias, out_weight, out_bias, cotangent,
):
    d, ff = qkv_weight.shape[0], fc1_weight.shape[1]
    pos_a, pos_b = position_tables(LATENT // 2, d)
    smalls = (
        time_bin, class_label, live, latents, cotangent, patch_bias, ada_bias, qv_bias, proj_bias, fc1_bias, fc2_bias,
        final_ada_bias, out_bias, jnp.asarray(pos_a), jnp.asarray(pos_b), patch_weight, out_weight.T,
    )
    bigs = (time_table, class_table, ada_weight, final_ada_weight, qkv_weight, proj_weight, fc1_weight, fc2_weight)
    grads, early, late, planes = step(images, smalls, bigs)
    outs = list(
        finish(
            time_table.shape[0], class_table.shape[0], latents, grads, early, late, planes, ada_weight, final_ada_weight, ff
        )
    )
    outs[18] = outs[18].T
    return tuple(outs)


def solution(mesh):
    assert mesh.shape["row"] == 2 and mesh.shape["col"] == 2
    tiles = P("img", None, "row", "col")
    return jax.shard_map(
        functools.partial(local, mesh.shape["img"]),
        mesh=mesh,
        in_specs=(tiles,) + (P("img"),) * 3 + (P(),) * 18 + (tiles,),
        out_specs=(tiles, tiles) + (P(),) * 18,
        check_vma=False,
    )
```

```python
import functools

import jax
import jax.numpy as jnp
import numpy as np
from jax import lax
from jax.experimental import pallas as pl
from jax.experimental.pallas import tpu as pltpu
from jax.sharding import PartitionSpec as P

F32 = jnp.float32
BF16 = jnp.bfloat16
HEADS = 6
LATENT = 64
MESH = pl.DeviceIdType.MESH
VMEM = pl.BlockSpec(memory_space=pltpu.VMEM)
SMEM = pl.BlockSpec(memory_space=pltpu.SMEM)
ANY = pl.BlockSpec(memory_space=pl.ANY)


def nn(a, b):
    return lax.dot_general(a, b, (((1,), (0,)), ((), ())), preferred_element_type=F32)


def nt(a, b):
    return lax.dot_general(a, b, (((1,), (1,)), ((), ())), preferred_element_type=F32)


def tn(a, b):
    return lax.dot_general(a, b, (((0,), (0,)), ((), ())), preferred_element_type=F32)


def parts(v, many):
    out = []
    for _ in range(many):
        piece = v.astype(BF16)
        out.append(piece)
        v = v - piece.astype(F32)
    return out


def iota(shape, dim):
    return lax.broadcasted_iota(jnp.int32, shape, dim)


def flag(cond):
    return jnp.where(cond, 1.0, 0.0)


def swish(v):
    return v / (1.0 + jnp.exp(-v))


def position_tables(grid, width):
    quarter = width // 4
    omega = np.float32(1.0) / np.power(
        np.float32(10000.0), np.arange(quarter, dtype=np.float32) / np.float32(quarter)
    )
    angles = np.arange(grid, dtype=np.float32)[:, None] * omega[None, :].astype(np.float32)
    single = np.concatenate([np.sin(angles), np.cos(angles)], axis=1).astype(np.float32)
    blank = np.zeros_like(single)
    return np.concatenate([single, blank], axis=1), np.concatenate([blank, single], axis=1)


def plane_maps(slots, chans, side, halves):
    rows = slots * chans * side
    lanes = halves * halves
    spread = []
    keep = flag(iota((rows, lanes), 0) % side // 2 == iota((rows, lanes), 1) // halves)
    pick = []
    for j in range(2):
        col = iota((side, lanes), 0)
        spread.append(flag(col == iota((side, lanes), 1) % halves * 2 + j).astype(BF16))
        many = slots * chans * 4
        out, src = iota((many, rows), 0), iota((many, rows), 1)
        same = (out // 4 == src // side) & (out % 4 // 2 == src % 2) & (out % 2 == j)
        pick.append(flag(same).astype(BF16))
    return keep, spread, pick


def shift_masks(halves):
    row, lane = iota((16, halves * halves), 0), iota((16, halves * halves), 1)
    return row % 4 >= 2, row % 2 == 1, lane, halves


def shift_in(planes, masks):
    odd_row, odd_col, lane, side = masks
    full = side * side
    down = [
        jnp.where(
            odd_row,
            jnp.where(lane < side, pltpu.roll(planes[s ^ 2], side, 1), pltpu.roll(planes[s], side, 1)),
            planes[s],
        )
        for s in range(4)
    ]
    return [
        jnp.where(
            odd_col,
            jnp.where(
                lane % side == 0, pltpu.roll(down[s ^ 1], full - side + 1, 1), pltpu.roll(down[s], 1, 1)
            ),
            down[s],
        )
        for s in range(4)
    ]


def shift_out(planes, masks):
    odd_row, odd_col, lane, side = masks
    full = side * side
    up = [
        jnp.where(
            odd_row,
            jnp.where(
                lane >= full - side,
                pltpu.roll(planes[s ^ 2], full - side, 1),
                pltpu.roll(planes[s], full - side, 1),
            ),
            planes[s],
        )
        for s in range(4)
    ]
    return [
        jnp.where(
            odd_col,
            jnp.where(
                lane % side == side - 1, pltpu.roll(up[s ^ 1], side - 1, 1), pltpu.roll(up[s], full - 1, 1)
            ),
            up[s],
        )
        for s in range(4)
    ]


def mate(slot):
    row, col = lax.axis_index("row"), lax.axis_index("col")
    return {"row": row ^ (slot >> 1), "col": col ^ (slot & 1)}


def greet(devices):
    barrier = pltpu.get_barrier_semaphore()
    for device in devices:
        pl.semaphore_signal(barrier, inc=1, device_id=device, device_id_type=MESH)
    pl.semaphore_wait(barrier, len(devices))


def norm(v):
    share = 1.0 / v.shape[-1]
    centred = v - jnp.sum(v, axis=-1, keepdims=True) * share
    spread = jnp.sum(centred * centred, axis=-1, keepdims=True) * share
    inv = lax.rsqrt(spread + 1e-06)
    return centred * inv, inv


def norm_back(hat, inv, grad):
    share = 1.0 / hat.shape[-1]
    first = jnp.sum(grad, axis=-1, keepdims=True) * share
    second = jnp.sum(grad * hat, axis=-1, keepdims=True) * share
    return inv * (grad - first - hat * second)


def col_sum(v):
    return jnp.sum(v, axis=0, keepdims=True)


E_OUT, E_PROJ_B, E_FC2_B, E_FC1_B, E_OUT_B, E_MOD, E_COND, E_IDS, E_ROWS = 0, 16, 17, 18, 22, 23, 41, 47, 48
L_PATCH, L_PATCH_B, L_MOD, L_Q_B, L_V_B, L_ROWS = 0, 16, 17, 23, 24, 32


def tree(terms):
    while len(terms) > 1:
        terms = [terms[i] + terms[i + 1] for i in range(0, len(terms), 2)]
    return terms[0]


class Copies:
    def __init__(self, send_sem, recv_sem):
        self.send_sem, self.recv_sem, self.known = send_sem, recv_sem, {}

    def make(self, key, src, dst, device):
        at = self.known.setdefault(key, len(self.known))
        return pltpu.make_async_remote_copy(
            src_ref=src, dst_ref=dst, send_sem=self.send_sem.at[at], recv_sem=self.recv_sem.at[at],
            device_id=device, device_id_type=MESH,
        )


class Stage:
    def __init__(self, copies, reduce=None):
        self.copies, self.reduce = copies, reduce

    def start(self):
        for c in self.copies():
            c.start()

    def finish(self):
        for c in self.copies():
            c.wait_recv()
        if self.reduce is not None:
            self.reduce()

    def drain(self):
        for c in self.copies():
            c.wait_send()


def far(distance):
    return {"img": lax.axis_index("img") ^ distance}


def rows_at(start, many):
    return pl.ds(pl.multiple_of(start, 16), many)


def ways(images, plan):
    bits = images.bit_length() - 1
    kept = ["".join(x for x in way if not x.isdigit() or int(x) < bits) for way in plan]
    return [way for way in kept if way]


def shared_bits(images, plan):
    return max([int(x) + 1 for way in ways(images, plan) for x in way if x.isdigit()] + [0])


def members(way):
    return 1 << len(way)


def position(way):
    total = 0
    for x in way:
        if x.isdigit():
            side = (lax.axis_index("img") >> int(x)) & 1
        else:
            side = lax.axis_index({"c": "col", "r": "row"}[x])
        total = 2 * total + side
    return total


def partner(way, delta):
    device, flips = {}, 0
    for k, x in enumerate(reversed(way)):
        if delta >> k & 1:
            if x.isdigit():
                flips |= 1 << int(x)
            else:
                name = {"c": "col", "r": "row"}[x]
                device[name] = 1 - lax.axis_index(name)
    if flips:
        device["img"] = lax.axis_index("img") ^ flips
    return device


def group_shapes(images, rows, plan):
    d, shapes = 384, []
    for way in ways(images, plan):
        many = members(way)
        rows //= many
        shapes += [(many - 1, rows, d), (rows, d)]
    high = images >> shared_bits(images, plan)
    if high > 1:
        shapes += [(high - 1, rows, d), (rows, d)]
    return shapes


def group_copies(images, plan):
    return 2 * sum(members(way) - 1 for way in ways(images, plan)) + (images >> shared_bits(images, plan)) - 1


def group_stages(name, images, base, rows, plan, grads, out, bufs, net):
    bufs = list(bufs)
    known = ways(images, plan)
    shared = shared_bits(images, plan)
    high = images >> shared

    def add(*refs):
        return tree([r.astype(F32) for r in refs]).astype(BF16)

    def scatter(k, way, held, many, got, total, last):
        count = members(way)

        def copies():
            return [
                net.make(f"{name}s{k}.{e}", held((position(way) ^ e) * many, many), got.at[e - 1], partner(way, e))
                for e in range(1, count)
            ]

        def reduce():
            total[...] = add(held(position(way) * many, many)[...], *[got[e] for e in range(count - 1)])
            if last:
                out[rows_at(base + start(len(known)), many), :] = total[...]

        return Stage(copies, reduce)

    sizes = [rows]
    for way in known:
        sizes.append(sizes[-1] // members(way))

    def start(level):
        total = 0
        for k in range(level):
            total = total + position(known[k]) * sizes[k + 1]
        return total

    stages = []

    def held(at, many):
        return grads.at[rows_at(base + at, many), :]

    for k, way in enumerate(known):
        got, total = bufs[:2]
        del bufs[:2]
        stages.append(scatter(k, way, held, sizes[k + 1], got, total, high == 1 and k == len(known) - 1))

        def held(at, many, total=total):
            return total.at[rows_at(at, many), :]

    if high > 1:
        got, final = bufs[:2]
        summed, many = total, sizes[-1]

        def copies():
            return [net.make(f"{name}h{e}", summed, got.at[e - 1], far(e << shared)) for e in range(1, high)]

        def reduce():
            final[...] = add(summed[...], *[got[e] for e in range(high - 1)])
            out[rows_at(base + start(len(known)), many), :] = final[...]

        stages.append(Stage(copies, reduce))

    def gather(k, way):
        def copies():
            at = out.at[rows_at(base + start(k + 1), sizes[k + 1]), :]
            return [net.make(f"{name}g{k}.{e}", at, at, partner(way, e)) for e in range(1, members(way))]

        return Stage(copies)

    for k in reversed(range(len(known))):
        stages.append(gather(k, known[k]))
    return stages


def sum_stages(name, images, block, got, total, out, net):
    def c0():
        return [net.make(name + "m" + str(s), block, got.at[s - 1], mate(s)) for s in (1, 2, 3)]

    def r0():
        t = tree([r.astype(F32) for r in (block[...], got[0], got[1], got[2])]).astype(BF16)
        total[...] = t
        out[lax.axis_index("img")] = t

    def c1():
        at = out.at[lax.axis_index("img")]
        return [net.make(name + "i" + str(d), total, at, far(d)) for d in range(1, images)]

    return [Stage(c0, r0), Stage(c1)]


def edge_stages(name, edge, got, out, net):
    def c0():
        return [net.make(name + str(s), edge.at[s], got.at[s - 1], mate(s)) for s in (1, 2, 3)]

    def r0():
        out[...] = tree([r.astype(F32) for r in (edge[0], got[1], got[0], got[2])])

    return [Stage(c0, r0)]


SLOW = (("c", "r", "0", "12"), ("c", "0", "1", "r2"), ("c", "1", "r", "02"))
FAST = (("c", "r0", "12"), ("c", "01", "r2"), ("c", "r012"))
FC, PAIR, EARLY, LATE, EDGE_L = 0, 3, 6, 7, 8
IMAGE_EVENTS = ((2, 0, 1),)
GRAD_EVENTS = ()
BACK_EVENTS = ((1, 0, 2), (1, 1, 1), (1, 2, 1), (3, 0, 3), (3, 6, 1), (4, 1, 2), (4, 2, 2), (5, 0, 4), (5, 3, 1), (6, 1, 3), (6, 2, 3), (7, 0, 5), (7, 3, 2), (8, 1, 4), (8, 2, 4), (8, 4, 1), (8, 6, 2))
TAIL_EVENTS = ((0, 0, 6), (0, 3, 3), (2, 1, 5), (2, 2, 5), (4, 5, 1), (8, 0, 7), (8, 1, 6), (8, 2, 6), (8, 3, 4), (8, 4, 2), (11, 0, 8))
END_EVENTS = (4, 3, 5, 1, 2, 7, 8, 4, 3, 1, 2, 5, 7, 4, 5, 4, 5)


def group_list(d, ff):
    large, rows = 2 * ff // 3, d + d // 3
    out = [(k * large, large, SLOW[k]) for k in range(3)]
    return out + [(2 * ff + k * rows, rows, FAST[k]) for k in range(3)]


def step_kernel(images, count, *refs):
    refs = list(refs)

    def take(n):
        out = refs[:n]
        del refs[:n]
        return out

    (time_ref, class_ref, live_ref, lat_ref, cot_ref, patch_b_ref, ada_b_ref, qv_b_ref, proj_b_ref, fc1_b_ref, fc2_b_ref,
     fada_b_ref, out_b_ref, pos_a_ref, pos_b_ref, patch_w_ref, out_wt_ref) = take(17)
    hbm = take(8)
    out_ref, early_out, late_out, planes_out = take(4)
    held = take(4)
    qkv_ref, proj_ref, fc1_ref, fc2_ref = held
    (planes_ref, mod_s, pt_s, gy_s, wp_s, wo_s, x1_s, x1_b, x1t_s, hat_s, inv_s, k_s, v_s, q_s, e_s, sa_s, sb_s, top_s,
     linv_s, delta_s, of_s, a_s, b_s, dm_s, x2t_s, da_s, dx_s, edge_s,
     grads_ref, early_ref, late_ref, early_16, late_16, edge_l, early_got, early_sum, late_got, late_sum, edge_l_got) = take(39)
    load_sem, gather_send, gather_recv, send_sem, recv_sem = take(5)
    bufs = refs

    d = qkv_ref.shape[0]
    slots, chans, side, _ = lat_ref.shape
    toks = x1_s.shape[0]
    pairs = HEADS // 2
    ff = fc1_ref.shape[1]
    blocks = ff // d
    half = side // 2
    bins, classes = hbm[0].shape[0], hbm[1].shape[0]

    loads = [pltpu.make_async_copy(a, b, load_sem.at[4 + i]) for i, (a, b) in enumerate(zip(hbm[4:], held))]
    net = Copies(send_sem, recv_sem)
    groups = []
    for g, (base, rows, plan) in enumerate(group_list(d, ff)):
        n = len(group_shapes(images, rows, plan))
        groups.append(group_stages("g" + str(g), images, base, rows, plan, grads_ref, out_ref, bufs[:n], net))
        del bufs[:n]
    groups.append(sum_stages("e", images, early_16, early_got, early_sum, early_out, net))
    groups.append(sum_stages("l", images, late_16, late_got, late_sum, late_out, net))
    groups.append(edge_stages("x", edge_l, edge_l_got, planes_out, net))
    def advance(g, k):
        if k > 0:
            groups[g][k - 1].finish()
        if k < len(groups[g]):
            groups[g][k].start()

    def row_of(ref, start, many):
        return ref[...].astype(F32).reshape(1, ref.shape[0])[:, start : start + many]

    early_ref[...] = jnp.zeros_like(early_ref)
    late_ref[...] = jnp.zeros_like(late_ref)

    swap = flag(iota((16, 16), 0) == (iota((16, 16), 1) ^ 3)).astype(BF16)
    wp_s[...] = nn(swap, patch_w_ref[...]).astype(BF16)
    wo_s[...] = nn(swap, out_wt_ref[...]).astype(BF16)
    out_bias = jnp.sum(
        flag(iota((16, 16), 1) == (iota((16, 16), 0) ^ 3)) * row_of(out_b_ref, 0, 16), axis=1, keepdims=True
    )

    inv_lane = iota((toks, 128), 1)

    def opening(time_table_ref, class_table_ref, ada_ref, fada_ref, pos_s):
        tables = [
            pltpu.make_async_copy(a, b, load_sem.at[i])
            for i, (a, b) in enumerate(zip(hbm[:4], (time_table_ref, class_table_ref, ada_ref, fada_ref)))
        ]
        for c in tables + loads:
            c.start()
        greet([mate(s) for s in (1, 2, 3)] + [far(k) for k in range(1, images)])
        keep, spread, pick = plane_maps(slots, chans, side, half)
        for k, ref in enumerate((lat_ref, cot_ref)):
            tile = ref[...].reshape(slots * chans * side, side)
            total = None
            for j in range(2):
                wide = (nn(tile, spread[j]) * keep).astype(BF16)
                term = nn(pick[j], wide)
                total = term if total is None else total + term
            planes_ref[0, k] = total.astype(BF16)
        gathers = []
        for s in (1, 2, 3):
            c = pltpu.make_async_remote_copy(
                src_ref=planes_ref.at[0], dst_ref=planes_ref.at[s], send_sem=gather_send.at[s - 1], recv_sem=gather_recv.at[s - 1],
                device_id=mate(s), device_id_type=MESH,
            )
            c.start()
            gathers.append(c)

        my_row, my_col = lax.axis_index("row"), lax.axis_index("col")
        patch_b = row_of(patch_b_ref, 0, d)
        for s in range(4):
            ta = pos_a_ref[pl.ds(pl.multiple_of((my_row ^ (s >> 1)) * half, half), half), :]
            tb = pos_b_ref[pl.ds(pl.multiple_of((my_col ^ (s & 1)) * half, half), half), :] + patch_b
            for a in range(half):
                pos_s[s, a * half : (a + 1) * half, :] = ta[a : a + 1, :] + tb

        def onehot(ids_ref, many):
            row, lane = iota((16, many), 0), iota((16, many), 1)
            hit = jnp.zeros((16, many), F32)
            for i in range(slots):
                hit = hit + flag((row == i) & (lane == ids_ref[i]))
            return hit.astype(BF16)

        for c in tables:
            c.wait()
        cond = nn(onehot(time_ref, bins), time_table_ref[...]) + nn(onehot(class_ref, classes), class_table_ref[...])
        cond = cond[:8]
        act = parts(swish(cond), 3)
        act = jnp.concatenate([p.astype(F32) for p in act] + [jnp.zeros((8, d), F32)], axis=0).astype(BF16)
        for p in range(8):
            w = ada_ref[:, p * d : (p + 1) * d] if p < 6 else fada_ref[:, (p - 6) * d : (p - 5) * d]
            m = nn(act, w)
            b = row_of(ada_b_ref, p * d, d) if p < 6 else row_of(fada_b_ref, (p - 6) * d, d)
            mod_s[p] = m[0:8] + m[8:16] + m[16:24] + b
        row, lane = iota((8, d), 0), iota((8, d), 1)
        ids = jnp.zeros((8, d), F32)
        for i in range(slots):
            for k, v in enumerate((time_ref[i], class_ref[i] // 256, class_ref[i] % 256)):
                ids = ids + jnp.where((row == 0) & (lane == k * slots + i), 0.25 * v.astype(F32), 0.0)
        high = cond.astype(BF16).astype(F32)
        early_ref[E_COND : E_COND + slots, :] = 0.25 * high[:slots]
        early_ref[E_COND + slots : E_COND + 2 * slots, :] = 0.25 * (cond - high)[:slots]
        early_ref[E_IDS : E_IDS + 1, :] = ids[0:1]

        for c in gathers:
            c.wait_recv()
        masks = shift_masks(half)
        live = [live_ref[i].astype(F32) for i in range(slots)]
        for i in range(slots):
            lat = shift_in([planes_ref[s, 0, i * 16 : (i + 1) * 16, :].astype(F32) for s in range(4)], masks)
            cot = shift_in([planes_ref[s, 1, i * 16 : (i + 1) * 16, :].astype(F32) for s in range(4)], masks)
            for s in range(4):
                pt_s[i * 4 + s] = lat[s].astype(BF16)
            gy_s[i] = (cot[0] * live[i]).astype(BF16)

        v_bias = row_of(qv_b_ref, d, d)

        def token_norm(t, x1_buf):
            img, slot = t // 4, t % 4
            tok = tn(pt_s[t], wp_s[...]) + pos_s[slot]
            dx_s[img] = tok
            hat, inv = norm(tok)
            hat_s[t] = hat
            inv_s[...] = jnp.where(inv_lane == t, inv, inv_s[...])
            x1_buf[...] = (hat * (1.0 + mod_s[1, pl.ds(img, 1), :]) + mod_s[0, pl.ds(img, 1), :]).astype(BF16)

        def token_keys(t, x1_buf):
            img, slot = t // 4, t % 4
            x1 = x1_buf[...]
            keys = nn(x1, qkv_ref[:, d : 2 * d]).astype(BF16)
            vals = (nn(x1, qkv_ref[:, 2 * d :]) + v_bias).astype(BF16)
            for p in range(pairs):
                k_s[img * pairs + p, slot] = keys[:, p * 128 : (p + 1) * 128]
                v_s[img * pairs + p, slot] = vals[:, p * 128 : (p + 1) * 128]
            x1t_s[t] = x1.T

        def reverse(n):
            return n // 4 * 4 + 3 - n % 4

        token_norm(jnp.int32(3), x1_s)
        loads[0].wait()

        def tokens(n, carry):
            token_norm(reverse(2 * n + 1), x1_b)
            token_keys(reverse(2 * n), x1_s)
            token_norm(reverse(jnp.minimum(2 * n + 2, slots * 4 - 1)), x1_s)
            token_keys(reverse(2 * n + 1), x1_b)
            return carry

        lax.fori_loop(0, slots * 2, tokens, 0)

        for c in gathers:
            c.wait_send()

    pl.run_scoped(
        opening,
        *[pltpu.VMEM(hbm[i].shape, BF16) for i in range(4)],
        pltpu.VMEM((4, toks, d), F32),
    )
    masks = shift_masks(half)

    lane128 = iota((1, 128), 1) // 64
    head_mask = [flag(lane128 == h) for h in range(2)]

    q_bias = row_of(qv_b_ref, 0, d)

    def queries(img, carry):
        query = tn(x1t_s[img * 4], qkv_ref[:, :d]) + q_bias
        query = query.astype(BF16).astype(F32) * 0.125
        for p in range(pairs):
            for h in range(2):
                q_s[img * HEADS + p * 2 + h] = (query[:, p * 128 : (p + 1) * 128] * head_mask[h]).astype(BF16)
        return carry

    lax.fori_loop(0, slots, queries, 0)

    def scores(idx, h, buf):
        top = None
        for c in range(4):
            s = nt(k_s[idx, c], q_s[idx * 2 + h])
            buf[c] = s
            m = jnp.max(s, axis=0, keepdims=True)
            top = m if top is None else jnp.maximum(top, m)
        top_s[h] = top

    def softmax(idx, h, buf, vt):
        head = idx * 2 + h
        top, total, acc = top_s[h], None, None
        for c in range(4):
            e = jnp.exp(buf[c] - top)
            l = col_sum(e)
            total = l if total is None else total + l
            eb = e.astype(BF16)
            e_s[head, c] = eb
            o = nn(vt[c][h * 64 : (h + 1) * 64], eb)
            acc = o if acc is None else acc + o
        linv = 1.0 / total
        linv_s[head] = linv
        of_s[head] = acc * linv

    scores(jnp.int32(0), 0, sa_s)

    def attend(idx, carry):
        vt = [v_s[idx, c].T for c in range(4)]
        scores(idx, 1, sb_s)
        softmax(idx, 0, sa_s, vt)
        scores(jnp.minimum(idx + 1, slots * pairs - 1), 0, sa_s)
        softmax(idx, 1, sb_s, vt)
        return carry

    lax.fori_loop(0, slots * pairs, attend, 0)
    for c in loads[1:]:
        c.wait()
    proj_b, fc1_b, fc2_b = row_of(proj_b_ref, 0, d), row_of(fc1_b_ref, 0, ff), row_of(fc2_b_ref, 0, d)

    def closing(dot_s, dom_s, dq_s, dxq_s, acc_s, dx1_s):
        def pair_row(k):
            return 2 * ff + k * (d + d // 3)

        def wide(ref, img, b):
            return jnp.concatenate([ref[img * 12 + b * 3 + j] for j in range(3)], axis=1)

        def fc2_grad(b, carry):
            total = tree([tn(wide(a_s, img, b), dm_s[img]) for img in range(2)])
            for img in range(2, slots):
                total = total + tn(wide(a_s, img, b), dm_s[img])
            grads_ref[rows_at(b * d, d), :] = total.astype(BF16)
            started(b, 0)
            return carry

        def started(b, before):
            for g in range(FC, PAIR):
                last = -(-(g + 1) * (2 * ff // 3) // d) - 1 - before
                if 0 <= last < blocks:

                    @pl.when(b == last)
                    def _():
                        advance(g, 0)

        def when_at(i, plan):
            for at, events in plan.items():

                @pl.when(i == at)
                def _():
                    for g, k in events:
                        advance(g, k)

        image_plan, grad_plan, back_plan, tail_plan = {}, {}, {}, {}
        for plan, events in ((image_plan, IMAGE_EVENTS), (grad_plan, GRAD_EVENTS), (back_plan, BACK_EVENTS), (tail_plan, TAIL_EVENTS)):
            for at, g, k in events:
                if k <= len(groups[g]):
                    plan.setdefault(at, []).append((g, k))

        def inv_at(t):
            return jnp.sum(jnp.where(inv_lane == t, inv_s[...], 0.0), axis=1, keepdims=True)

        def image(img, carry):
            def mod_row(p):
                return mod_s[p, pl.ds(img, 1), :]

            ot = jnp.concatenate([of_s[img * HEADS + h] for h in range(HEADS)], axis=0).astype(BF16)
            branch = tn(ot, proj_ref[...]) + proj_b
            g1 = mod_row(2)
            resid = dx_s[img] + g1 * branch
            hat2, inv2 = norm(resid)
            sa_s[img] = hat2[:, :toks]
            sb_s[img, :, : d - toks] = hat2[:, toks:]
            inv_s[...] = jnp.where(inv_lane == slots * 4 + img, inv2, inv_s[...])
            x2 = (hat2 * (1.0 + mod_row(4)) + mod_row(3)).astype(BF16)
            x2t_s[img] = x2.T
            mlp = jnp.zeros((toks, d), F32)
            k0, k1 = 0.7978845608028654, 0.044715
            def first(b):
                return nn(x2, fc1_ref[:, b * d : (b + 1) * d])

            u = first(0)
            for b in range(blocks):
                at_b = slice(b * d, (b + 1) * d)
                ahead = first(b + 1) if b + 1 < blocks else None
                u = u + fc1_b[:, at_b]
                sq = u * u
                inner = k0 + (k0 * k1) * sq
                cdf = 0.5 + 0.5 * jnp.tanh(u * inner)
                hidden = u * cdf
                slope = cdf + (hidden - hidden * cdf) * (6.0 * inner - 4.0 * k0)
                hidden = hidden.astype(BF16)
                slope = slope.astype(BF16)
                for j in range(3):
                    a_s[img * 12 + b * 3 + j] = hidden[:, j * 128 : (j + 1) * 128]
                    b_s[img * 12 + b * 3 + j] = slope[:, j * 128 : (j + 1) * 128]
                mlp = mlp + nn(hidden, fc2_ref[at_b, :])
                u = ahead
            mlp = mlp + fc2_b
            g2 = mod_row(5)
            x3 = resid + g2 * mlp
            hatf, invf = norm(x3)
            scf = 1.0 + mod_row(7)
            xf = (hatf * scf + mod_row(6)).astype(BF16)
            edge_s[4, img] = (nt(wo_s[...], xf) + out_bias) * live_ref[img].astype(F32)
            gy = gy_s[img]
            early_ref[E_OUT : E_OUT + 16, :] += nn(gy, xf)
            early_ref[E_OUT_B : E_OUT_B + 1, 0:16] += nt(jnp.ones((8, toks), BF16), gy)[0:1]
            dxf = tn(gy, wo_s[...])

            def put_mod(p, v):
                early_ref[pl.ds(E_MOD + (p - 2) * slots + img, 1), :] = v

            put_mod(6, col_sum(dxf))
            put_mod(7, col_sum(dxf * hatf))
            dx3 = norm_back(hatf, invf, dxf * scf)
            dm = (g2 * dx3).astype(BF16)
            dm_s[img] = dm
            put_mod(5, col_sum(mlp * dx3))
            early_ref[E_FC2_B : E_FC2_B + 1, :] += col_sum(dm.astype(F32))
            dx_s[img] = dx3
            return carry

        lax.fori_loop(0, slots, image, 0)
        lax.fori_loop(0, blocks, fc2_grad, 0)

        def image_back(img, carry):
            when_at(img, image_plan)

            def mod_row(p):
                return mod_s[p, pl.ds(img, 1), :]

            def put_mod(p, v):
                early_ref[pl.ds(E_MOD + (p - 2) * slots + img, 1), :] = v

            g1, dm = mod_row(2), dm_s[img]
            hat2 = jnp.concatenate([sa_s[img], sb_s[img, :, : d - toks]], axis=1)
            inv2 = inv_at(slots * 4 + img)
            dx2 = jnp.zeros((toks, d), F32)
            def second(b):
                return nt(dm, fc2_ref[b * d : (b + 1) * d, :])

            dh = second(0)
            for b in range(blocks):
                ahead = second(b + 1) if b + 1 < blocks else None
                slope = jnp.concatenate([b_s[img * 12 + b * 3 + j] for j in range(3)], axis=1).astype(F32)
                du = (dh * slope).astype(BF16)
                for j in range(3):
                    b_s[img * 12 + b * 3 + j] = du[:, j * 128 : (j + 1) * 128]
                early_ref[E_FC1_B + b : E_FC1_B + b + 1, :] += col_sum(du.astype(F32))
                dx2 = dx2 + nt(du, fc1_ref[:, b * d : (b + 1) * d])
                dh = ahead
            put_mod(3, col_sum(dx2))
            put_mod(4, col_sum(dx2 * hat2))
            dx = dx_s[img] + norm_back(hat2, inv2, dx2 * (1.0 + mod_row(4)))
            dx_s[img] = dx
            ot = jnp.concatenate([of_s[img * HEADS + h] for h in range(HEADS)], axis=0).astype(BF16)
            branch = tn(ot, proj_ref[...]) + proj_b
            put_mod(2, col_sum(branch * dx))
            da = (g1 * dx).astype(BF16)
            da_s[img] = da
            early_ref[E_PROJ_B : E_PROJ_B + 1, :] += col_sum(da.astype(F32))
            dot = nt(proj_ref[...], da)
            blank = jnp.zeros((64, toks), F32)
            for hd in range(HEADS):
                head = img * HEADS + hd
                piece = dot[hd * 64 : (hd + 1) * 64]
                linv = linv_s[head]
                delta_s[head] = col_sum(piece * of_s[head]) * linv
                piece = piece * linv
                wide = jnp.concatenate([piece, blank] if hd % 2 == 0 else [blank, piece], axis=0).astype(BF16)
                dot_s[head] = wide
                dom_s[head] = wide.T
            return carry

        lax.fori_loop(0, slots, image_back, 0)

        def fc1_grad(b, carry):
            when_at(b, grad_plan)
            total = tree([nn(x2t_s[img], wide(b_s, img, b)) for img in range(2)])
            for img in range(2, slots):
                total = total + nn(x2t_s[img], wide(b_s, img, b))
            grads_ref[rows_at(ff + b * d, d), :] = total.astype(BF16)
            started(b, blocks)
            return carry

        lax.fori_loop(0, blocks, fc1_grad, 0)
        total = None
        for img in range(slots):
            ot = jnp.concatenate([of_s[img * HEADS + h] for h in range(HEADS)], axis=0).astype(BF16)
            term = nn(ot, da_s[img])
            total = term if total is None else total + term
        for k in range(pairs):
            grads_ref[pair_row(k) + d : pair_row(k + 1), :] = total[k * (d // 3) : (k + 1) * (d // 3)].astype(BF16)
        blank = jnp.zeros((16, toks), F32)
        for i in range(slots):
            out = shift_out([edge_s[4, i], blank, blank, blank], masks)
            for s in range(4):
                edge_l[s, 1, i * 16 : (i + 1) * 16, :] = out[s].astype(BF16)
        early_16[...] = early_ref[...].astype(BF16)
        advance(EARLY, 0)

        acc_s[...] = jnp.zeros_like(acc_s)

        def attend_back(it, carry):
            when_at(it, back_plan)
            p, img = it // slots, it % slots
            idx = img * pairs + p
            dqt = [None, None]
            jobs = [(c, h) for c in range(4) for h in range(2)]

            def product(job):
                return nn(v_s[idx, job[0]], dot_s[idx * 2 + job[1]])

            dp = product(jobs[0])
            gathered = None
            sum_v = None
            for n, (c, h) in enumerate(jobs):
                head = idx * 2 + h
                ahead = product(jobs[n + 1]) if n + 1 < len(jobs) else None
                if h == 0:
                    kt = k_s[idx, c].T
                    dk, dv = None, None
                e = e_s[head, c]
                ds = (e.astype(F32) * (dp - delta_s[head])).astype(BF16)
                dk_h, dv_h = nn(ds, q_s[head]), nn(e, dom_s[head])
                dk = dk_h if dk is None else dk + dk_h
                dv = dv_h if dv is None else dv + dv_h
                dq_h = nn(kt[h * 64 : (h + 1) * 64], ds)
                dqt[h] = dq_h if dqt[h] is None else dqt[h] + dq_h
                dp = ahead
                if h == 1:
                    dk, dv = dk.astype(BF16), dv.astype(BF16)
                    a_s[idx * 4 + c] = dk
                    b_s[idx * 4 + c] = dv
                    sv = col_sum(dv.astype(F32))
                    sum_v = sv if sum_v is None else sum_v + sv
                    term = nn(x1t_s[img * 4 + c], jnp.concatenate([dk, dv], axis=1))
                    gathered = term if gathered is None else gathered + term
            dq = (jnp.concatenate(dqt, axis=0) * 0.125).T.astype(BF16)
            dq_s[idx] = dq
            lanes = pl.ds(pl.multiple_of(p * 128, 128), 128)
            late_ref[L_V_B : L_V_B + 1, lanes] += sum_v
            late_ref[L_Q_B : L_Q_B + 1, lanes] += col_sum(dq.astype(F32))
            acc_s[:, 128:] += gathered
            acc_s[:, :128] += nn(x1t_s[img * 4], dq)

            for pair in range(pairs):

                @pl.when(it == pair * slots + slots - 1)
                def _():
                    at = pair_row(pair)
                    grads_ref[at : at + d, :] = acc_s[...].astype(BF16)
                    acc_s[...] = jnp.zeros_like(acc_s)
                    advance(PAIR + pair, 0)

            return carry

        lax.fori_loop(0, slots * pairs, attend_back, 0)

        def joined(ref, img, slot):
            return [ref[(img * pairs + p) * 4 + slot] for p in range(pairs)]

        def query_back(img, carry):
            dq = jnp.concatenate([dq_s[img * pairs + p] for p in range(pairs)], axis=1)
            dxq_s[img] = nt(dq, qkv_ref[:, :d])
            return carry

        lax.fori_loop(0, slots, query_back, 0)

        def product_back(t):
            img, slot = t // 4, t % 4
            dkv = jnp.concatenate(joined(a_s, img, slot) + joined(b_s, img, slot), axis=1)
            own = jnp.where(slot == 0, 1.0, 0.0)
            return nt(dkv, qkv_ref[:, d:]) + dxq_s[img] * own

        dx1_s[...] = product_back(jnp.int32(0))
        def tokens_back(t, carry):
            when_at(t, tail_plan)
            img, slot = t // 4, t % 4
            dx1 = dx1_s[...]
            ahead = product_back(jnp.minimum(t + 1, slots * 4 - 1))
            hat = hat_s[t]
            late_ref[pl.ds(L_MOD + img, 1), :] += col_sum(dx1)
            late_ref[pl.ds(L_MOD + slots + img, 1), :] += col_sum(dx1 * hat)
            own = jnp.where(slot == 0, 1.0, 0.0)
            dtok = norm_back(hat, inv_at(t), dx1 * (1.0 + mod_s[1, pl.ds(img, 1), :])) + dx_s[img] * own
            late_ref[L_PATCH_B : L_PATCH_B + 1, :] += col_sum(dtok)
            dtok = dtok.astype(BF16)
            late_ref[L_PATCH : L_PATCH + 16, :] += nn(pt_s[t], dtok)
            for p in range(pairs):
                a_s[(img * pairs + p) * 4 + slot] = dtok[:, p * 128 : (p + 1) * 128]
            dx1_s[...] = ahead
            return carry

        lax.fori_loop(0, slots * 4, tokens_back, 0)

    pl.run_scoped(
        closing,
        pltpu.VMEM((slots * HEADS, 128, toks), BF16),
        pltpu.VMEM((slots * HEADS, toks, 128), BF16),
        pltpu.VMEM((slots * pairs, toks, 128), BF16),
        pltpu.VMEM((slots, toks, d), F32),
        pltpu.VMEM((d, d), F32),
        pltpu.VMEM((toks, d), F32),
    )

    late_16[...] = late_ref[...].astype(BF16)
    advance(LATE, 0)

    def edges(t, carry):
        img, slot = t // 4, t % 4
        dtok = jnp.concatenate([a_s[(img * pairs + p) * 4 + slot] for p in range(pairs)], axis=1)
        edge_s[slot, img] = nt(wp_s[...], dtok)
        return carry

    lax.fori_loop(0, slots * 4, edges, 0)
    for i in range(slots):
        lat = shift_out([edge_s[s, i] for s in range(4)], masks)
        for s in range(4):
            edge_l[s, 0, i * 16 : (i + 1) * 16, :] = lat[s].astype(BF16)
    advance(EDGE_L, 0)
    state = {g: 1 for g in (LATE, EDGE_L)}
    for g in (*range(FC, PAIR + 3), EARLY):
        done = [k for events in (IMAGE_EVENTS, GRAD_EVENTS, BACK_EVENTS, TAIL_EVENTS) for _, h, k in events if h == g]
        assert done == list(range(1, len(done) + 1))
        state[g] = len(done) + 1
    order = list(END_EVENTS)
    order += [g for g in state for _ in range(len(groups[g]))]
    drained = {g: 0 for g in state}
    for g in order:
        if state[g] <= len(groups[g]):
            for h, stages in enumerate(groups):
                while drained[h] < state[h] - 1 - (h == g):
                    stages[drained[h]].drain()
                    drained[h] += 1
            advance(g, state[g])
            state[g] += 1
    for h, stages in enumerate(groups):
        for stage in stages[drained[h] :]:
            stage.drain()
    assert len(net.known) <= count


def step(images, smalls, bigs):
    time_bin, latents = smalls[0], smalls[3]
    qkv_weight, fc1_weight = bigs[4], bigs[6]
    d, ff = qkv_weight.shape[0], fc1_weight.shape[1]
    slots, chans, side, _ = latents.shape
    toks = side * side // 4
    planes = slots * chans * 4
    pairs = HEADS // 2
    heads = slots * HEADS
    out_shape = (
        jax.ShapeDtypeStruct((2 * ff + 4 * d, d), BF16),
        jax.ShapeDtypeStruct((images, E_ROWS, d), BF16),
        jax.ShapeDtypeStruct((images, L_ROWS, d), BF16),
        jax.ShapeDtypeStruct((2, planes, toks), F32),
    )
    scratch = [(w.shape, w.dtype) for w in bigs[4:]] + [
        ((4, 2, planes, toks), BF16), ((8, 8, d), F32), ((slots * 4, 16, toks), BF16),
        ((slots, 16, toks), BF16), ((16, d), BF16), ((16, d), BF16), ((toks, d), BF16), ((toks, d), BF16), ((slots * 4, d, toks), BF16),
        ((slots * 4, toks, d), F32), ((toks, 128), F32), ((slots * pairs, 4, toks, 128), BF16),
        ((slots * pairs, 4, toks, 128), BF16), ((heads, toks, 128), BF16), ((heads, 4, toks, toks), BF16),
        ((4, toks, toks), F32), ((4, toks, toks), F32), ((2, 1, toks), F32), ((heads, 1, toks), F32), ((heads, 1, toks), F32),
        ((heads, 64, toks), F32), ((slots * 12, toks, 128), BF16), ((slots * 12, toks, 128), BF16),
        ((slots, toks, d), BF16), ((slots, d, toks), BF16), ((slots, toks, d), BF16),
        ((slots, toks, d), F32), ((5, slots, 16, toks), F32),
        ((2 * ff + 4 * d, d), BF16), ((E_ROWS, d), F32), ((L_ROWS, d), F32), ((E_ROWS, d), BF16), ((L_ROWS, d), BF16), ((4, 2, planes, toks), BF16),
        ((3, E_ROWS, d), BF16), ((E_ROWS, d), BF16), ((3, L_ROWS, d), BF16), ((L_ROWS, d), BF16), ((3, 2, planes, toks), BF16),
    ]
    dma = pltpu.SemaphoreType.DMA
    parts_of = group_list(d, ff)
    count = sum(group_copies(images, plan) for _, _, plan in parts_of) + 2 * (3 + images - 1) + 6
    moved = [(s, BF16) for _, rows, plan in parts_of for s in group_shapes(images, rows, plan)]
    return pl.pallas_call(
        functools.partial(step_kernel, images, count),
        out_shape=out_shape,
        in_specs=[SMEM] * 3 + [VMEM] * (len(smalls) - 3) + [ANY] * len(bigs),
        out_specs=(VMEM,) * 4,
        scratch_shapes=[pltpu.VMEM(shape, kind) for shape, kind in scratch]
        + [dma((len(bigs),)), dma((3,)), dma((3,)), dma((count,)), dma((count,))]
        + [pltpu.VMEM(shape, kind) for shape, kind in moved],
        compiler_params=pltpu.CompilerParams(
            collective_id=0, has_side_effects=True, vmem_limit_bytes=64 * 1024 * 1024 - 65536
        ),
        name="step",
    )(*smalls, *bigs)


def finish_kernel(bins, classes, *refs):
    hbm_in, hbm_out, refs = refs[:6], refs[6:26], refs[26:]
    grads_ref, early_ref, late_ref, planes_ref, ada_ref, fada_ref = refs[:6]
    (out_ref, lat_ref, time_ref, class_ref, patch_ref, patch_b_ref, ada_g_ref, ada_b_ref, qkv_g_ref, qv_b_ref, proj_g_ref,
     proj_b_ref, fc1_g_ref, fc1_b_ref, fc2_g_ref, fc2_b_ref, fada_g_ref, fada_b_ref, out_gt_ref, out_b_ref) = outs = refs[6:26]
    in_sem, out_sem = refs[26:]
    d = ada_ref.shape[0]
    ff = fc1_g_ref.shape[1]
    blocks = ff // d
    pairs = HEADS // 2
    slots, chans, side, _ = lat_ref.shape
    groups = early_ref.shape[0]
    images = groups * slots
    held = -(-images // 32) * 32

    loads = []

    def fetch(src, dst):
        c = pltpu.make_async_copy(src, dst, in_sem.at[len(loads)])
        c.start()
        loads.append(c)

    for k in (1, 2):
        fetch(hbm_in[k], refs[k])
    bounds = [b * d for b in range(2 * blocks + 1)] + [2 * ff + 4 * d]
    for a, b in zip(bounds[:-1], bounds[1:]):
        fetch(hbm_in[0].at[a:b, :], grads_ref.at[a:b, :])
    for k in (4, 5, 3):
        fetch(hbm_in[k], refs[k])
    stores = []

    def send(k, *at):
        src, dst = outs[k], hbm_out[k]
        if at:
            src, dst = src.at[at], dst.at[at]
        c = pltpu.make_async_copy(src, dst, out_sem.at[len(stores)])
        c.start()
        stores.append(c)

    loads[0].wait()
    loads[1].wait()

    all_early = early_ref[...].reshape(groups * E_ROWS, d)
    all_late = late_ref[...].reshape(groups * L_ROWS, d)

    def chosen(block, rows, starts, steps):
        many = len(starts) * held
        line = iota((many, 1), 0)
        image = line % held
        item = line // held
        start, step = jnp.zeros_like(line), jnp.zeros_like(line)
        for k, (at, by) in enumerate(zip(starts, steps)):
            start = jnp.where(item == k, at, start)
            step = jnp.where(item == k, by, step)
        want = jnp.where(image < images, image // slots * rows + start + step * (image % slots), -1)
        return nn(flag(iota((many, groups * rows), 1) == want).astype(BF16), block)

    starts = [E_COND, E_COND + slots, E_IDS] + [E_MOD + k * slots for k in range(6)]
    picked = chosen(all_early, E_ROWS, starts, [1, 1, 0] + [1] * 6)
    items = [picked[k * held : (k + 1) * held] for k in range(9)]
    cond, ids = items[0] + items[1], items[2]
    picked = chosen(all_late, L_ROWS, [L_MOD, L_MOD + slots], [1, 1])
    dmods = [picked[:held], picked[held:]] + items[3:]
    img_row, lane = iota((held, d), 0), iota((held, d), 1)

    def id_part(k):
        return jnp.sum(jnp.where(lane == k * slots + img_row % slots, ids, 0.0), axis=1, keepdims=True)

    time_id, class_id = id_part(0), 256.0 * id_part(1) + id_part(2)

    left = jnp.concatenate(parts(swish(cond), 2), axis=0).T
    pairs_of = [jnp.concatenate([dmods[p], dmods[p + 1]], axis=1).astype(BF16) for p in range(0, 8, 2)]
    for k, pair in enumerate(pairs_of):
        grad = nn(left, jnp.concatenate([pair, pair], axis=0))
        if k < 3:
            lanes = slice(2 * k * d, 2 * (k + 1) * d)
            ada_g_ref[:, lanes] = grad
            send(6, slice(None), lanes)
        else:
            fada_g_ref[...] = grad
            send(16)

    for b in range(blocks):
        at = slice(b * d, (b + 1) * d)
        loads[2 + b].wait()
        fc2_g_ref[at, :] = grads_ref[at, :].astype(F32)
        send(14, at, slice(None))
    for b in range(blocks):
        at = slice(b * d, (b + 1) * d)
        loads[2 + blocks + b].wait()
        fc1_g_ref[:, at] = grads_ref[ff + b * d : ff + (b + 1) * d, :].astype(F32)
        send(12, slice(None), at)
    loads[2 + 2 * blocks].wait()
    third = d // 3
    for p in range(pairs):
        at = 2 * ff + p * (d + third)
        proj_g_ref[p * third : (p + 1) * third, :] = grads_ref[at + d : at + d + third, :].astype(F32)
        for k in range(3):
            lanes = slice(k * d + p * 128, k * d + (p + 1) * 128)
            qkv_g_ref[:, lanes] = grads_ref[at : at + d, k * 128 : (k + 1) * 128].astype(F32)
    send(8)
    send(10)

    for c in loads[3 + 2 * blocks :]:
        c.wait()
    dact = jnp.zeros((held, d), F32)
    for k, pair in enumerate(pairs_of):
        w = ada_ref[:, 2 * k * d : 2 * (k + 1) * d] if k < 3 else fada_ref[...]
        dact = dact + nt(pair, w)
    bias_rows = [col_sum(v) for v in dmods]
    ada_b_ref[...] = jnp.concatenate(bias_rows[:6], axis=1).reshape(6 * d)
    fada_b_ref[...] = jnp.concatenate(bias_rows[6:], axis=1).reshape(2 * d)
    sig = 1.0 / (1.0 + jnp.exp(-cond))
    dcond = dact * (sig * (1.0 + cond * (1.0 - sig)))
    stack = jnp.concatenate(parts(dcond, 2), axis=0)
    for ref, ids_col, many in ((class_ref, class_id, classes), (time_ref, time_id, bins)):
        wide = -(-many // 128) * 128
        at = iota((held, wide), 1).astype(F32)
        hit = flag((at == ids_col) & (iota((held, wide), 0) < images)).astype(BF16)
        ref[...] = tn(jnp.concatenate([hit, hit], axis=0), stack)[:many]
    send(3)
    send(2)

    early, late = jnp.sum(early_ref[...].astype(F32), axis=0), jnp.sum(late_ref[...].astype(F32), axis=0)
    swap = flag(iota((16, 16), 0) == (iota((16, 16), 1) ^ 3)).astype(BF16)

    def swapped(v):
        return tree([nn(swap, p) for p in parts(v, 2)] + [nn(swap, parts(v, 3)[2]), jnp.zeros_like(v)])

    patch_ref[...] = swapped(late[L_PATCH : L_PATCH + 16])
    out_gt_ref[...] = swapped(early[E_OUT : E_OUT + 16])

    def line(v, row):
        return v[row : row + 1, :]

    patch_b_ref[...] = line(late, L_PATCH_B).reshape(d)
    qv_b_ref[...] = jnp.concatenate([line(late, L_Q_B), line(late, L_V_B)], axis=1).reshape(2 * d)
    proj_b_ref[...] = line(early, E_PROJ_B).reshape(d)
    fc1_b_ref[...] = jnp.concatenate([line(early, E_FC1_B + b) for b in range(blocks)], axis=1).reshape(ff)
    fc2_b_ref[...] = line(early, E_FC2_B).reshape(d)
    tail = jnp.broadcast_to(line(early, E_OUT_B)[:, 0:16], (16, 16))
    pick = flag(iota((16, 16), 1) == (iota((16, 16), 0) ^ 3))
    column = jnp.sum(tail * pick, axis=1, keepdims=True)
    out_b_ref[...] = col_sum(jnp.where(iota((16, 16), 0) == iota((16, 16), 1), column, 0.0)).reshape(16)

    half = side // 2
    keep, spread, pick = plane_maps(slots, chans, side, half)
    for k in (4, 5, 7, 9, 11, 13, 15, 17, 18, 19):
        send(k)
    for k, ref in ((0, lat_ref), (1, out_ref)):
        many = 2 - k
        planes = jnp.concatenate(parts(planes_ref[k], many), axis=0)
        pieces, maps = [], []
        for j in range(2):
            wide = tn(jnp.concatenate([pick[j]] * many, axis=0), planes) * keep
            pieces += parts(wide, many)
            maps += [spread[j]] * many
        total = nt(jnp.concatenate(pieces, axis=1), jnp.concatenate(maps, axis=1))
        ref[...] = total.reshape(ref.shape).astype(ref.dtype)
        send(1 - k)
    for c in stores:
        c.wait()


def finish(bins, classes, latents, grads, early, late, planes, ada_weight, fada_weight, ff):
    d = ada_weight.shape[0]
    f = lambda *shape: jax.ShapeDtypeStruct(shape, F32)
    out_shape = (
        jax.ShapeDtypeStruct(latents.shape, BF16), f(*latents.shape), f(bins, d), f(classes, d), f(16, d), f(d),
        f(d, 6 * d), f(6 * d), f(d, 3 * d), f(2 * d), f(d, d), f(d), f(d, ff), f(ff), f(ff, d), f(d), f(d, 2 * d), f(2 * d),
        f(16, d), f(16),
    )
    ins = (grads, early, late, planes, ada_weight, fada_weight)
    dma = pltpu.SemaphoreType.DMA
    return pl.pallas_call(
        functools.partial(finish_kernel, bins, classes),
        out_shape=out_shape,
        in_specs=[ANY] * 6,
        out_specs=(ANY,) * len(out_shape),
        scratch_shapes=[pltpu.VMEM(x.shape, x.dtype) for x in ins + out_shape]
        + [dma((6 + 2 * (ff // d),)), dma((20 + 2 * (ff // d),))],
        compiler_params=pltpu.CompilerParams(vmem_limit_bytes=60 * 1024 * 1024),
        name="finish",
    )(*ins)


def local(
    images, latents, time_bin, class_label, live, time_table, class_table, patch_weight, patch_bias, ada_weight, ada_bias,
    qkv_weight, qv_bias, proj_weight, proj_bias, fc1_weight, fc1_bias, fc2_weight, fc2_bias, final_ada_weight,
    final_ada_bias, out_weight, out_bias, cotangent,
):
    d, ff = qkv_weight.shape[0], fc1_weight.shape[1]
    pos_a, pos_b = position_tables(LATENT // 2, d)
    smalls = (
        time_bin, class_label, live, latents, cotangent, patch_bias, ada_bias, qv_bias, proj_bias, fc1_bias, fc2_bias,
        final_ada_bias, out_bias, jnp.asarray(pos_a), jnp.asarray(pos_b), patch_weight, out_weight.T,
    )
    bigs = (time_table, class_table, ada_weight, final_ada_weight, qkv_weight, proj_weight, fc1_weight, fc2_weight)
    grads, early, late, planes = step(images, smalls, bigs)
    outs = list(
        finish(
            time_table.shape[0], class_table.shape[0], latents, grads, early, late, planes, ada_weight, final_ada_weight, ff
        )
    )
    outs[18] = outs[18].T
    return tuple(outs)


def solution(mesh):
    assert mesh.shape["row"] == 2 and mesh.shape["col"] == 2
    tiles = P("img", None, "row", "col")
    return jax.shard_map(
        functools.partial(local, mesh.shape["img"]),
        mesh=mesh,
        in_specs=(tiles,) + (P("img"),) * 3 + (P(),) * 18 + (tiles,),
        out_specs=(tiles, tiles) + (P(),) * 18,
        check_vma=False,
    )
```

```python
import functools

import jax
import jax.numpy as jnp
import numpy as np
from jax import lax
from jax.experimental import pallas as pl
from jax.experimental.pallas import tpu as pltpu
from jax.sharding import PartitionSpec as P

F32 = jnp.float32
BF16 = jnp.bfloat16
HEADS = 6
LATENT = 64
MESH = pl.DeviceIdType.MESH
VMEM = pl.BlockSpec(memory_space=pltpu.VMEM)
SMEM = pl.BlockSpec(memory_space=pltpu.SMEM)
ANY = pl.BlockSpec(memory_space=pl.ANY)


def nn(a, b):
    return lax.dot_general(a, b, (((1,), (0,)), ((), ())), preferred_element_type=F32)


def nt(a, b):
    return lax.dot_general(a, b, (((1,), (1,)), ((), ())), preferred_element_type=F32)


def tn(a, b):
    return lax.dot_general(a, b, (((0,), (0,)), ((), ())), preferred_element_type=F32)


def parts(v, many):
    out = []
    for _ in range(many):
        piece = v.astype(BF16)
        out.append(piece)
        v = v - piece.astype(F32)
    return out


def iota(shape, dim):
    return lax.broadcasted_iota(jnp.int32, shape, dim)


def flag(cond):
    return jnp.where(cond, 1.0, 0.0)


def swish(v):
    return v / (1.0 + jnp.exp(-v))


def position_tables(grid, width):
    quarter = width // 4
    omega = np.float32(1.0) / np.power(
        np.float32(10000.0), np.arange(quarter, dtype=np.float32) / np.float32(quarter)
    )
    angles = np.arange(grid, dtype=np.float32)[:, None] * omega[None, :].astype(np.float32)
    single = np.concatenate([np.sin(angles), np.cos(angles)], axis=1).astype(np.float32)
    blank = np.zeros_like(single)
    return np.concatenate([single, blank], axis=1), np.concatenate([blank, single], axis=1)


def plane_maps(slots, chans, side, halves):
    rows = slots * chans * side
    lanes = halves * halves
    spread = []
    keep = flag(iota((rows, lanes), 0) % side // 2 == iota((rows, lanes), 1) // halves)
    pick = []
    for j in range(2):
        col = iota((side, lanes), 0)
        spread.append(flag(col == iota((side, lanes), 1) % halves * 2 + j).astype(BF16))
        many = slots * chans * 4
        out, src = iota((many, rows), 0), iota((many, rows), 1)
        same = (out // 4 == src // side) & (out % 4 // 2 == src % 2) & (out % 2 == j)
        pick.append(flag(same).astype(BF16))
    return keep, spread, pick


def shift_masks(halves):
    row, lane = iota((16, halves * halves), 0), iota((16, halves * halves), 1)
    return row % 4 >= 2, row % 2 == 1, lane, halves


def shift_in(planes, masks):
    odd_row, odd_col, lane, side = masks
    full = side * side
    down = [
        jnp.where(
            odd_row,
            jnp.where(lane < side, pltpu.roll(planes[s ^ 2], side, 1), pltpu.roll(planes[s], side, 1)),
            planes[s],
        )
        for s in range(4)
    ]
    return [
        jnp.where(
            odd_col,
            jnp.where(
                lane % side == 0, pltpu.roll(down[s ^ 1], full - side + 1, 1), pltpu.roll(down[s], 1, 1)
            ),
            down[s],
        )
        for s in range(4)
    ]


def shift_out(planes, masks):
    odd_row, odd_col, lane, side = masks
    full = side * side
    up = [
        jnp.where(
            odd_row,
            jnp.where(
                lane >= full - side,
                pltpu.roll(planes[s ^ 2], full - side, 1),
                pltpu.roll(planes[s], full - side, 1),
            ),
            planes[s],
        )
        for s in range(4)
    ]
    return [
        jnp.where(
            odd_col,
            jnp.where(
                lane % side == side - 1, pltpu.roll(up[s ^ 1], side - 1, 1), pltpu.roll(up[s], full - 1, 1)
            ),
            up[s],
        )
        for s in range(4)
    ]


def mate(slot):
    row, col = lax.axis_index("row"), lax.axis_index("col")
    return {"row": row ^ (slot >> 1), "col": col ^ (slot & 1)}


def greet(devices):
    barrier = pltpu.get_barrier_semaphore()
    for device in devices:
        pl.semaphore_signal(barrier, inc=1, device_id=device, device_id_type=MESH)
    pl.semaphore_wait(barrier, len(devices))


def norm(v):
    share = 1.0 / v.shape[-1]
    centred = v - jnp.sum(v, axis=-1, keepdims=True) * share
    spread = jnp.sum(centred * centred, axis=-1, keepdims=True) * share
    inv = lax.rsqrt(spread + 1e-06)
    return centred * inv, inv


def norm_back(hat, inv, grad):
    share = 1.0 / hat.shape[-1]
    first = jnp.sum(grad, axis=-1, keepdims=True) * share
    second = jnp.sum(grad * hat, axis=-1, keepdims=True) * share
    return inv * (grad - first - hat * second)


def col_sum(v):
    return jnp.sum(v, axis=0, keepdims=True)


E_OUT, E_PROJ_B, E_FC2_B, E_FC1_B, E_OUT_B, E_MOD, E_COND, E_IDS, E_ROWS = 0, 16, 17, 18, 22, 23, 41, 47, 48
L_PATCH, L_PATCH_B, L_MOD, L_Q_B, L_V_B, L_ROWS = 0, 16, 17, 23, 24, 32


def tree(terms):
    while len(terms) > 1:
        terms = [terms[i] + terms[i + 1] for i in range(0, len(terms), 2)]
    return terms[0]


class Copies:
    def __init__(self, send_sem, recv_sem):
        self.send_sem, self.recv_sem, self.known = send_sem, recv_sem, {}

    def make(self, key, src, dst, device):
        at = self.known.setdefault(key, len(self.known))
        return pltpu.make_async_remote_copy(
            src_ref=src, dst_ref=dst, send_sem=self.send_sem.at[at], recv_sem=self.recv_sem.at[at],
            device_id=device, device_id_type=MESH,
        )


class Stage:
    def __init__(self, copies, reduce=None):
        self.copies, self.reduce = copies, reduce

    def start(self):
        for c in self.copies():
            c.start()

    def finish(self):
        for c in self.copies():
            c.wait_recv()
        if self.reduce is not None:
            self.reduce()

    def drain(self):
        for c in self.copies():
            c.wait_send()


def far(distance):
    return {"img": lax.axis_index("img") ^ distance}


def rows_at(start, many):
    return pl.ds(pl.multiple_of(start, 16), many)


def ways(images, plan):
    bits = images.bit_length() - 1
    kept = ["".join(x for x in way if not x.isdigit() or int(x) < bits) for way in plan]
    return [way for way in kept if way]


def shared_bits(images, plan):
    return max([int(x) + 1 for way in ways(images, plan) for x in way if x.isdigit()] + [0])


def members(way):
    return 1 << len(way)


def position(way):
    total = 0
    for x in way:
        if x.isdigit():
            side = (lax.axis_index("img") >> int(x)) & 1
        else:
            side = lax.axis_index({"c": "col", "r": "row"}[x])
        total = 2 * total + side
    return total


def partner(way, delta):
    device, flips = {}, 0
    for k, x in enumerate(reversed(way)):
        if delta >> k & 1:
            if x.isdigit():
                flips |= 1 << int(x)
            else:
                name = {"c": "col", "r": "row"}[x]
                device[name] = 1 - lax.axis_index(name)
    if flips:
        device["img"] = lax.axis_index("img") ^ flips
    return device


def group_shapes(images, rows, plan):
    d, shapes = 384, []
    for way in ways(images, plan):
        many = members(way)
        rows //= many
        shapes += [(many - 1, rows, d), (rows, d)]
    high = images >> shared_bits(images, plan)
    if high > 1:
        shapes += [(high - 1, rows, d), (rows, d)]
    return shapes


def group_copies(images, plan):
    return 2 * sum(members(way) - 1 for way in ways(images, plan)) + (images >> shared_bits(images, plan)) - 1


def group_stages(name, images, base, rows, plan, grads, out, bufs, net):
    bufs = list(bufs)
    known = ways(images, plan)
    shared = shared_bits(images, plan)
    high = images >> shared

    def add(*refs):
        return tree([r.astype(F32) for r in refs]).astype(BF16)

    def scatter(k, way, held, many, got, total, last):
        count = members(way)

        def copies():
            return [
                net.make(f"{name}s{k}.{e}", held((position(way) ^ e) * many, many), got.at[e - 1], partner(way, e))
                for e in range(1, count)
            ]

        def reduce():
            total[...] = add(held(position(way) * many, many)[...], *[got[e] for e in range(count - 1)])
            if last:
                out[rows_at(base + start(len(known)), many), :] = total[...]

        return Stage(copies, reduce)

    sizes = [rows]
    for way in known:
        sizes.append(sizes[-1] // members(way))

    def start(level):
        total = 0
        for k in range(level):
            total = total + position(known[k]) * sizes[k + 1]
        return total

    stages = []

    def held(at, many):
        return grads.at[rows_at(base + at, many), :]

    for k, way in enumerate(known):
        got, total = bufs[:2]
        del bufs[:2]
        stages.append(scatter(k, way, held, sizes[k + 1], got, total, high == 1 and k == len(known) - 1))

        def held(at, many, total=total):
            return total.at[rows_at(at, many), :]

    if high > 1:
        got, final = bufs[:2]
        summed, many = total, sizes[-1]

        def copies():
            return [net.make(f"{name}h{e}", summed, got.at[e - 1], far(e << shared)) for e in range(1, high)]

        def reduce():
            final[...] = add(summed[...], *[got[e] for e in range(high - 1)])
            out[rows_at(base + start(len(known)), many), :] = final[...]

        stages.append(Stage(copies, reduce))

    def gather(k, way):
        def copies():
            at = out.at[rows_at(base + start(k + 1), sizes[k + 1]), :]
            return [net.make(f"{name}g{k}.{e}", at, at, partner(way, e)) for e in range(1, members(way))]

        return Stage(copies)

    for k in reversed(range(len(known))):
        stages.append(gather(k, known[k]))
    return stages


def sum_stages(name, images, block, got, total, out, net):
    def c0():
        return [net.make(name + "m" + str(s), block, got.at[s - 1], mate(s)) for s in (1, 2, 3)]

    def r0():
        t = tree([r.astype(F32) for r in (block[...], got[0], got[1], got[2])]).astype(BF16)
        total[...] = t
        out[lax.axis_index("img")] = t

    def c1():
        at = out.at[lax.axis_index("img")]
        return [net.make(name + "i" + str(d), total, at, far(d)) for d in range(1, images)]

    return [Stage(c0, r0), Stage(c1)]


def edge_stages(name, edge, got, out, net):
    def c0():
        return [net.make(name + str(s), edge.at[s], got.at[s - 1], mate(s)) for s in (1, 2, 3)]

    def r0():
        out[...] = tree([r.astype(F32) for r in (edge[0], got[1], got[0], got[2])])

    return [Stage(c0, r0)]


SLOW = (("c", "r", "0", "12"), ("c", "0", "1", "r2"), ("c", "1", "r", "02"))
FAST = (("c", "r0", "12"), ("c", "01", "r2"), ("c", "r012"))
FC, PAIR, EARLY, LATE, EDGE_L = 0, 3, 6, 7, 8
IMAGE_EVENTS = ((2, 0, 1),)
GRAD_EVENTS = ()
BACK_EVENTS = ((1, 0, 2), (1, 1, 1), (1, 2, 1), (3, 0, 3), (3, 6, 1), (4, 1, 2), (4, 2, 2), (5, 0, 4), (5, 3, 1), (6, 1, 3), (6, 2, 3), (8, 0, 5), (8, 3, 2), (8, 4, 1), (8, 6, 2))
TAIL_EVENTS = ((0, 1, 4), (0, 2, 4), (2, 0, 6), (4, 3, 3), (4, 5, 1), (6, 1, 5), (6, 2, 5), (8, 4, 2))
END_EVENTS = (0, 3, 1, 2, 4, 5, 0, 7, 8, 3, 1, 2, 4, 3, 7, 1, 2, 5, 5, 4, 4)


def group_list(d, ff):
    large, rows = 2 * ff // 3, d + d // 3
    out = [(k * large, large, SLOW[k]) for k in range(3)]
    return out + [(2 * ff + k * rows, rows, FAST[k]) for k in range(3)]


def step_kernel(images, count, *refs):
    refs = list(refs)

    def take(n):
        out = refs[:n]
        del refs[:n]
        return out

    (time_ref, class_ref, live_ref, lat_ref, cot_ref, patch_b_ref, ada_b_ref, qv_b_ref, proj_b_ref, fc1_b_ref, fc2_b_ref,
     fada_b_ref, out_b_ref, pos_a_ref, pos_b_ref, patch_w_ref, out_wt_ref) = take(17)
    hbm = take(8)
    out_ref, early_out, late_out, planes_out = take(4)
    held = take(4)
    qkv_ref, proj_ref, fc1_ref, fc2_ref = held
    (planes_ref, mod_s, pt_s, gy_s, wp_s, wo_s, x1_s, x1_b, x1t_s, hat_s, inv_s, k_s, v_s, q_s, e_s, sa_s, sb_s, top_s,
     linv_s, delta_s, of_s, a_s, b_s, dm_s, x2t_s, da_s, dx_s, edge_s,
     grads_ref, early_ref, late_ref, early_16, late_16, edge_l, early_got, early_sum, late_got, late_sum, edge_l_got) = take(39)
    load_sem, gather_send, gather_recv, send_sem, recv_sem = take(5)
    bufs = refs

    d = qkv_ref.shape[0]
    slots, chans, side, _ = lat_ref.shape
    toks = x1_s.shape[0]
    pairs = HEADS // 2
    ff = fc1_ref.shape[1]
    blocks = ff // d
    half = side // 2
    bins, classes = hbm[0].shape[0], hbm[1].shape[0]

    loads = [pltpu.make_async_copy(a, b, load_sem.at[4 + i]) for i, (a, b) in enumerate(zip(hbm[4:], held))]
    net = Copies(send_sem, recv_sem)
    groups = []
    for g, (base, rows, plan) in enumerate(group_list(d, ff)):
        n = len(group_shapes(images, rows, plan))
        groups.append(group_stages("g" + str(g), images, base, rows, plan, grads_ref, out_ref, bufs[:n], net))
        del bufs[:n]
    groups.append(sum_stages("e", images, early_16, early_got, early_sum, early_out, net))
    groups.append(sum_stages("l", images, late_16, late_got, late_sum, late_out, net))
    groups.append(edge_stages("x", edge_l, edge_l_got, planes_out, net))
    def advance(g, k):
        if k > 0:
            groups[g][k - 1].finish()
        if k < len(groups[g]):
            groups[g][k].start()

    def row_of(ref, start, many):
        return ref[...].astype(F32).reshape(1, ref.shape[0])[:, start : start + many]

    early_ref[...] = jnp.zeros_like(early_ref)
    late_ref[...] = jnp.zeros_like(late_ref)

    swap = flag(iota((16, 16), 0) == (iota((16, 16), 1) ^ 3)).astype(BF16)
    wp_s[...] = nn(swap, patch_w_ref[...]).astype(BF16)
    wo_s[...] = nn(swap, out_wt_ref[...]).astype(BF16)
    out_bias = jnp.sum(
        flag(iota((16, 16), 1) == (iota((16, 16), 0) ^ 3)) * row_of(out_b_ref, 0, 16), axis=1, keepdims=True
    )

    inv_lane = iota((toks, 128), 1)

    def opening(time_table_ref, class_table_ref, ada_ref, fada_ref, pos_s):
        tables = [
            pltpu.make_async_copy(a, b, load_sem.at[i])
            for i, (a, b) in enumerate(zip(hbm[:4], (time_table_ref, class_table_ref, ada_ref, fada_ref)))
        ]
        for c in tables + loads:
            c.start()
        greet([mate(s) for s in (1, 2, 3)] + [far(k) for k in range(1, images)])
        keep, spread, pick = plane_maps(slots, chans, side, half)
        for k, ref in enumerate((lat_ref, cot_ref)):
            tile = ref[...].reshape(slots * chans * side, side)
            total = None
            for j in range(2):
                wide = (nn(tile, spread[j]) * keep).astype(BF16)
                term = nn(pick[j], wide)
                total = term if total is None else total + term
            planes_ref[0, k] = total.astype(BF16)
        gathers = []
        for s in (1, 2, 3):
            c = pltpu.make_async_remote_copy(
                src_ref=planes_ref.at[0], dst_ref=planes_ref.at[s], send_sem=gather_send.at[s - 1], recv_sem=gather_recv.at[s - 1],
                device_id=mate(s), device_id_type=MESH,
            )
            c.start()
            gathers.append(c)

        my_row, my_col = lax.axis_index("row"), lax.axis_index("col")
        patch_b = row_of(patch_b_ref, 0, d)
        for s in range(4):
            ta = pos_a_ref[pl.ds(pl.multiple_of((my_row ^ (s >> 1)) * half, half), half), :]
            tb = pos_b_ref[pl.ds(pl.multiple_of((my_col ^ (s & 1)) * half, half), half), :] + patch_b
            for a in range(half):
                pos_s[s, a * half : (a + 1) * half, :] = ta[a : a + 1, :] + tb

        def onehot(ids_ref, many):
            row, lane = iota((16, many), 0), iota((16, many), 1)
            hit = jnp.zeros((16, many), F32)
            for i in range(slots):
                hit = hit + flag((row == i) & (lane == ids_ref[i]))
            return hit.astype(BF16)

        for c in tables:
            c.wait()
        cond = nn(onehot(time_ref, bins), time_table_ref[...]) + nn(onehot(class_ref, classes), class_table_ref[...])
        cond = cond[:8]
        act = parts(swish(cond), 3)
        act = jnp.concatenate([p.astype(F32) for p in act] + [jnp.zeros((8, d), F32)], axis=0).astype(BF16)
        for p in range(8):
            w = ada_ref[:, p * d : (p + 1) * d] if p < 6 else fada_ref[:, (p - 6) * d : (p - 5) * d]
            m = nn(act, w)
            b = row_of(ada_b_ref, p * d, d) if p < 6 else row_of(fada_b_ref, (p - 6) * d, d)
            mod_s[p] = m[0:8] + m[8:16] + m[16:24] + b
        row, lane = iota((8, d), 0), iota((8, d), 1)
        ids = jnp.zeros((8, d), F32)
        for i in range(slots):
            for k, v in enumerate((time_ref[i], class_ref[i] // 256, class_ref[i] % 256)):
                ids = ids + jnp.where((row == 0) & (lane == k * slots + i), 0.25 * v.astype(F32), 0.0)
        high = cond.astype(BF16).astype(F32)
        early_ref[E_COND : E_COND + slots, :] = 0.25 * high[:slots]
        early_ref[E_COND + slots : E_COND + 2 * slots, :] = 0.25 * (cond - high)[:slots]
        early_ref[E_IDS : E_IDS + 1, :] = ids[0:1]

        for c in gathers:
            c.wait_recv()
        masks = shift_masks(half)
        live = [live_ref[i].astype(F32) for i in range(slots)]
        for i in range(slots):
            lat = shift_in([planes_ref[s, 0, i * 16 : (i + 1) * 16, :].astype(F32) for s in range(4)], masks)
            cot = shift_in([planes_ref[s, 1, i * 16 : (i + 1) * 16, :].astype(F32) for s in range(4)], masks)
            for s in range(4):
                pt_s[i * 4 + s] = lat[s].astype(BF16)
            gy_s[i] = (cot[0] * live[i]).astype(BF16)

        v_bias = row_of(qv_b_ref, d, d)

        def token_norm(t, x1_buf):
            img, slot = t // 4, t % 4
            tok = tn(pt_s[t], wp_s[...]) + pos_s[slot]
            dx_s[img] = tok
            hat, inv = norm(tok)
            hat_s[t] = hat
            inv_s[...] = jnp.where(inv_lane == t, inv, inv_s[...])
            x1_buf[...] = (hat * (1.0 + mod_s[1, pl.ds(img, 1), :]) + mod_s[0, pl.ds(img, 1), :]).astype(BF16)

        def token_keys(t, x1_buf):
            img, slot = t // 4, t % 4
            x1 = x1_buf[...]
            keys = nn(x1, qkv_ref[:, d : 2 * d]).astype(BF16)
            vals = (nn(x1, qkv_ref[:, 2 * d :]) + v_bias).astype(BF16)
            for p in range(pairs):
                k_s[img * pairs + p, slot] = keys[:, p * 128 : (p + 1) * 128]
                v_s[img * pairs + p, slot] = vals[:, p * 128 : (p + 1) * 128]
            x1t_s[t] = x1.T

        def reverse(n):
            return n // 4 * 4 + 3 - n % 4

        token_norm(jnp.int32(3), x1_s)
        loads[0].wait()

        def tokens(n, carry):
            token_norm(reverse(2 * n + 1), x1_b)
            token_keys(reverse(2 * n), x1_s)
            token_norm(reverse(jnp.minimum(2 * n + 2, slots * 4 - 1)), x1_s)
            token_keys(reverse(2 * n + 1), x1_b)
            return carry

        lax.fori_loop(0, slots * 2, tokens, 0)

        for c in gathers:
            c.wait_send()

    pl.run_scoped(
        opening,
        *[pltpu.VMEM(hbm[i].shape, BF16) for i in range(4)],
        pltpu.VMEM((4, toks, d), F32),
    )
    masks = shift_masks(half)

    lane128 = iota((1, 128), 1) // 64
    head_mask = [flag(lane128 == h) for h in range(2)]

    q_bias = row_of(qv_b_ref, 0, d)

    def queries(img, carry):
        query = tn(x1t_s[img * 4], qkv_ref[:, :d]) + q_bias
        query = query.astype(BF16).astype(F32) * 0.125
        for p in range(pairs):
            for h in range(2):
                q_s[img * HEADS + p * 2 + h] = (query[:, p * 128 : (p + 1) * 128] * head_mask[h]).astype(BF16)
        return carry

    lax.fori_loop(0, slots, queries, 0)

    def scores(idx, h, buf):
        top = None
        for c in range(4):
            s = nt(k_s[idx, c], q_s[idx * 2 + h])
            buf[c] = s
            m = jnp.max(s, axis=0, keepdims=True)
            top = m if top is None else jnp.maximum(top, m)
        top_s[h] = top

    def softmax(idx, h, buf, vt):
        head = idx * 2 + h
        top, total, acc = top_s[h], None, None
        for c in range(4):
            e = jnp.exp(buf[c] - top)
            l = col_sum(e)
            total = l if total is None else total + l
            eb = e.astype(BF16)
            e_s[head, c] = eb
            o = nn(vt[c][h * 64 : (h + 1) * 64], eb)
            acc = o if acc is None else acc + o
        linv = 1.0 / total
        linv_s[head] = linv
        of_s[head] = acc * linv

    scores(jnp.int32(0), 0, sa_s)

    def attend(idx, carry):
        vt = [v_s[idx, c].T for c in range(4)]
        scores(idx, 1, sb_s)
        softmax(idx, 0, sa_s, vt)
        scores(jnp.minimum(idx + 1, slots * pairs - 1), 0, sa_s)
        softmax(idx, 1, sb_s, vt)
        return carry

    lax.fori_loop(0, slots * pairs, attend, 0)
    for c in loads[1:]:
        c.wait()
    proj_b, fc1_b, fc2_b = row_of(proj_b_ref, 0, d), row_of(fc1_b_ref, 0, ff), row_of(fc2_b_ref, 0, d)

    def closing(dot_s, dom_s, dq_s, dxq_s, acc_s, dx1_s):
        def pair_row(k):
            return 2 * ff + k * (d + d // 3)

        def wide(ref, img, b):
            return jnp.concatenate([ref[img * 12 + b * 3 + j] for j in range(3)], axis=1)

        def fc2_grad(b, carry):
            total = tree([tn(wide(a_s, img, b), dm_s[img]) for img in range(2)])
            for img in range(2, slots):
                total = total + tn(wide(a_s, img, b), dm_s[img])
            grads_ref[rows_at(b * d, d), :] = total.astype(BF16)
            started(b, 0)
            return carry

        def started(b, before):
            for g in range(FC, PAIR):
                last = -(-(g + 1) * (2 * ff // 3) // d) - 1 - before
                if 0 <= last < blocks:

                    @pl.when(b == last)
                    def _():
                        advance(g, 0)

        def when_at(i, plan):
            for at, events in plan.items():

                @pl.when(i == at)
                def _():
                    for g, k in events:
                        advance(g, k)

        image_plan, grad_plan, back_plan, tail_plan = {}, {}, {}, {}
        for plan, events in ((image_plan, IMAGE_EVENTS), (grad_plan, GRAD_EVENTS), (back_plan, BACK_EVENTS), (tail_plan, TAIL_EVENTS)):
            for at, g, k in events:
                if k <= len(groups[g]):
                    plan.setdefault(at, []).append((g, k))

        def inv_at(t):
            return jnp.sum(jnp.where(inv_lane == t, inv_s[...], 0.0), axis=1, keepdims=True)

        def image(img, carry):
            def mod_row(p):
                return mod_s[p, pl.ds(img, 1), :]

            ot = jnp.concatenate([of_s[img * HEADS + h] for h in range(HEADS)], axis=0).astype(BF16)
            branch = tn(ot, proj_ref[...]) + proj_b
            g1 = mod_row(2)
            resid = dx_s[img] + g1 * branch
            hat2, inv2 = norm(resid)
            sa_s[img] = hat2[:, :toks]
            sb_s[img, :, : d - toks] = hat2[:, toks:]
            inv_s[...] = jnp.where(inv_lane == slots * 4 + img, inv2, inv_s[...])
            x2 = (hat2 * (1.0 + mod_row(4)) + mod_row(3)).astype(BF16)
            x2t_s[img] = x2.T
            hiddens = []
            k0, k1 = 0.7978845608028654, 0.044715
            def first(b):
                return nn(x2, fc1_ref[:, b * d : (b + 1) * d])

            u = first(0)
            for b in range(blocks):
                at_b = slice(b * d, (b + 1) * d)
                ahead = first(b + 1) if b + 1 < blocks else None
                u = u + fc1_b[:, at_b]
                sq = u * u
                inner = k0 + (k0 * k1) * sq
                cdf = 0.5 + 0.5 * jnp.tanh(u * inner)
                hidden = u * cdf
                slope = cdf + (hidden - hidden * cdf) * (6.0 * inner - 4.0 * k0)
                hidden = hidden.astype(BF16)
                slope = slope.astype(BF16)
                for j in range(3):
                    a_s[img * 12 + b * 3 + j] = hidden[:, j * 128 : (j + 1) * 128]
                    b_s[img * 12 + b * 3 + j] = slope[:, j * 128 : (j + 1) * 128]
                hiddens.append(hidden)
                u = ahead
            mlp = nn(jnp.concatenate(hiddens, axis=1), fc2_ref[...])
            mlp = mlp + fc2_b
            g2 = mod_row(5)
            x3 = resid + g2 * mlp
            hatf, invf = norm(x3)
            scf = 1.0 + mod_row(7)
            xf = (hatf * scf + mod_row(6)).astype(BF16)
            edge_s[4, img] = (nt(wo_s[...], xf) + out_bias) * live_ref[img].astype(F32)
            gy = gy_s[img]
            early_ref[E_OUT : E_OUT + 16, :] += nn(gy, xf)
            early_ref[E_OUT_B : E_OUT_B + 1, 0:16] += nt(jnp.ones((8, toks), BF16), gy)[0:1]
            dxf = tn(gy, wo_s[...])

            def put_mod(p, v):
                early_ref[pl.ds(E_MOD + (p - 2) * slots + img, 1), :] = v

            put_mod(6, col_sum(dxf))
            put_mod(7, col_sum(dxf * hatf))
            dx3 = norm_back(hatf, invf, dxf * scf)
            dm = (g2 * dx3).astype(BF16)
            dm_s[img] = dm
            put_mod(5, col_sum(mlp * dx3))
            early_ref[E_FC2_B : E_FC2_B + 1, :] += col_sum(dm.astype(F32))
            dx_s[img] = dx3
            return carry

        lax.fori_loop(0, slots, image, 0)
        lax.fori_loop(0, blocks, fc2_grad, 0)

        def image_back(img, carry):
            when_at(img, image_plan)

            def mod_row(p):
                return mod_s[p, pl.ds(img, 1), :]

            def put_mod(p, v):
                early_ref[pl.ds(E_MOD + (p - 2) * slots + img, 1), :] = v

            g1, dm = mod_row(2), dm_s[img]
            hat2 = jnp.concatenate([sa_s[img], sb_s[img, :, : d - toks]], axis=1)
            inv2 = inv_at(slots * 4 + img)
            dus = []
            def second(b):
                return nt(dm, fc2_ref[b * d : (b + 1) * d, :])

            dh = second(0)
            for b in range(blocks):
                ahead = second(b + 1) if b + 1 < blocks else None
                slope = jnp.concatenate([b_s[img * 12 + b * 3 + j] for j in range(3)], axis=1).astype(F32)
                du = (dh * slope).astype(BF16)
                for j in range(3):
                    b_s[img * 12 + b * 3 + j] = du[:, j * 128 : (j + 1) * 128]
                early_ref[E_FC1_B + b : E_FC1_B + b + 1, :] += col_sum(du.astype(F32))
                dus.append(du)
                dh = ahead
            dx2 = nt(jnp.concatenate(dus, axis=1), fc1_ref[...])
            put_mod(3, col_sum(dx2))
            put_mod(4, col_sum(dx2 * hat2))
            dx = dx_s[img] + norm_back(hat2, inv2, dx2 * (1.0 + mod_row(4)))
            dx_s[img] = dx
            ot = jnp.concatenate([of_s[img * HEADS + h] for h in range(HEADS)], axis=0).astype(BF16)
            branch = tn(ot, proj_ref[...]) + proj_b
            put_mod(2, col_sum(branch * dx))
            da = (g1 * dx).astype(BF16)
            da_s[img] = da
            early_ref[E_PROJ_B : E_PROJ_B + 1, :] += col_sum(da.astype(F32))
            dot = nt(proj_ref[...], da)
            blank = jnp.zeros((64, toks), F32)
            for hd in range(HEADS):
                head = img * HEADS + hd
                piece = dot[hd * 64 : (hd + 1) * 64]
                linv = linv_s[head]
                delta_s[head] = col_sum(piece * of_s[head]) * linv
                piece = piece * linv
                wide = jnp.concatenate([piece, blank] if hd % 2 == 0 else [blank, piece], axis=0).astype(BF16)
                dot_s[head] = wide
                dom_s[head] = wide.T
            return carry

        lax.fori_loop(0, slots, image_back, 0)

        def fc1_grad(b, carry):
            when_at(b, grad_plan)
            total = tree([nn(x2t_s[img], wide(b_s, img, b)) for img in range(2)])
            for img in range(2, slots):
                total = total + nn(x2t_s[img], wide(b_s, img, b))
            grads_ref[rows_at(ff + b * d, d), :] = total.astype(BF16)
            started(b, blocks)
            return carry

        lax.fori_loop(0, blocks, fc1_grad, 0)
        total = None
        for img in range(slots):
            ot = jnp.concatenate([of_s[img * HEADS + h] for h in range(HEADS)], axis=0).astype(BF16)
            term = nn(ot, da_s[img])
            total = term if total is None else total + term
        for k in range(pairs):
            grads_ref[pair_row(k) + d : pair_row(k + 1), :] = total[k * (d // 3) : (k + 1) * (d // 3)].astype(BF16)
        blank = jnp.zeros((16, toks), F32)
        for i in range(slots):
            out = shift_out([edge_s[4, i], blank, blank, blank], masks)
            for s in range(4):
                edge_l[s, 1, i * 16 : (i + 1) * 16, :] = out[s].astype(BF16)
        early_16[...] = early_ref[...].astype(BF16)
        advance(EARLY, 0)

        acc_s[...] = jnp.zeros_like(acc_s)

        def attend_back(it, carry):
            when_at(it, back_plan)
            p, img = it // slots, it % slots
            idx = img * pairs + p
            dqt = [None, None]
            jobs = [(c, h) for c in range(4) for h in range(2)]

            def product(job):
                return nn(v_s[idx, job[0]], dot_s[idx * 2 + job[1]])

            dp, soon = product(jobs[0]), product(jobs[1])
            gathered = None
            sum_v = None
            dkv = []
            for n, (c, h) in enumerate(jobs):
                head = idx * 2 + h
                ahead = product(jobs[n + 2]) if n + 2 < len(jobs) else None
                if h == 0:
                    kt = k_s[idx, c].T
                    dk, dv = None, None
                e = e_s[head, c]
                ds = (e.astype(F32) * (dp - delta_s[head])).astype(BF16)
                dk_h, dv_h = nn(ds, q_s[head]), nn(e, dom_s[head])
                dk = dk_h if dk is None else dk + dk_h
                dv = dv_h if dv is None else dv + dv_h
                dq_h = nn(kt[h * 64 : (h + 1) * 64], ds)
                dqt[h] = dq_h if dqt[h] is None else dqt[h] + dq_h
                dp, soon = soon, ahead
                if h == 1:
                    dk, dv = dk.astype(BF16), dv.astype(BF16)
                    a_s[idx * 4 + c] = dk
                    b_s[idx * 4 + c] = dv
                    sv = col_sum(dv.astype(F32))
                    sum_v = sv if sum_v is None else sum_v + sv
                    dkv.append(jnp.concatenate([dk, dv], axis=1))
            x1t = jnp.concatenate([x1t_s[img * 4 + c] for c in range(4)], axis=1)
            gathered = nn(x1t, jnp.concatenate(dkv, axis=0))
            dq = (jnp.concatenate(dqt, axis=0) * 0.125).T.astype(BF16)
            dq_s[idx] = dq
            lanes = pl.ds(pl.multiple_of(p * 128, 128), 128)
            late_ref[L_V_B : L_V_B + 1, lanes] += sum_v
            late_ref[L_Q_B : L_Q_B + 1, lanes] += col_sum(dq.astype(F32))
            acc_s[:, 128:] += gathered
            acc_s[:, :128] += nn(x1t_s[img * 4], dq)

            for pair in range(pairs):

                @pl.when(it == pair * slots + slots - 1)
                def _():
                    at = pair_row(pair)
                    grads_ref[at : at + d, :] = acc_s[...].astype(BF16)
                    acc_s[...] = jnp.zeros_like(acc_s)
                    advance(PAIR + pair, 0)

            return carry

        lax.fori_loop(0, slots * pairs, attend_back, 0)

        def joined(ref, img, slot):
            return [ref[(img * pairs + p) * 4 + slot] for p in range(pairs)]

        def query_back(img, carry):
            dq = jnp.concatenate([dq_s[img * pairs + p] for p in range(pairs)], axis=1)
            dxq_s[img] = nt(dq, qkv_ref[:, :d])
            return carry

        lax.fori_loop(0, slots, query_back, 0)

        def product_back(t):
            img, slot = t // 4, t % 4
            dkv = jnp.concatenate(joined(a_s, img, slot) + joined(b_s, img, slot), axis=1)
            own = jnp.where(slot == 0, 1.0, 0.0)
            return nt(dkv, qkv_ref[:, d:]) + dxq_s[img] * own

        dx1_s[...] = product_back(jnp.int32(0))
        def tokens_back(t, carry):
            when_at(t, tail_plan)
            img, slot = t // 4, t % 4
            dx1 = dx1_s[...]
            ahead = product_back(jnp.minimum(t + 1, slots * 4 - 1))
            hat = hat_s[t]
            late_ref[pl.ds(L_MOD + img, 1), :] += col_sum(dx1)
            late_ref[pl.ds(L_MOD + slots + img, 1), :] += col_sum(dx1 * hat)
            own = jnp.where(slot == 0, 1.0, 0.0)
            dtok = norm_back(hat, inv_at(t), dx1 * (1.0 + mod_s[1, pl.ds(img, 1), :])) + dx_s[img] * own
            late_ref[L_PATCH_B : L_PATCH_B + 1, :] += col_sum(dtok)
            dtok = dtok.astype(BF16)
            late_ref[L_PATCH : L_PATCH + 16, :] += nn(pt_s[t], dtok)
            for p in range(pairs):
                a_s[(img * pairs + p) * 4 + slot] = dtok[:, p * 128 : (p + 1) * 128]
            dx1_s[...] = ahead
            return carry

        lax.fori_loop(0, slots * 4, tokens_back, 0)

    pl.run_scoped(
        closing,
        pltpu.VMEM((slots * HEADS, 128, toks), BF16),
        pltpu.VMEM((slots * HEADS, toks, 128), BF16),
        pltpu.VMEM((slots * pairs, toks, 128), BF16),
        pltpu.VMEM((slots, toks, d), F32),
        pltpu.VMEM((d, d), F32),
        pltpu.VMEM((toks, d), F32),
    )

    late_16[...] = late_ref[...].astype(BF16)
    advance(LATE, 0)

    def edges(t, carry):
        img, slot = t // 4, t % 4
        dtok = jnp.concatenate([a_s[(img * pairs + p) * 4 + slot] for p in range(pairs)], axis=1)
        edge_s[slot, img] = nt(wp_s[...], dtok)
        return carry

    lax.fori_loop(0, slots * 4, edges, 0)
    for i in range(slots):
        lat = shift_out([edge_s[s, i] for s in range(4)], masks)
        for s in range(4):
            edge_l[s, 0, i * 16 : (i + 1) * 16, :] = lat[s].astype(BF16)
    advance(EDGE_L, 0)
    state = {g: 1 for g in (LATE, EDGE_L)}
    for g in (*range(FC, PAIR + 3), EARLY):
        done = [k for events in (IMAGE_EVENTS, GRAD_EVENTS, BACK_EVENTS, TAIL_EVENTS) for _, h, k in events if h == g]
        assert done == list(range(1, len(done) + 1))
        state[g] = len(done) + 1
    order = list(END_EVENTS)
    order += [g for g in state for _ in range(len(groups[g]))]
    drained = {g: 0 for g in state}
    for g in order:
        if state[g] <= len(groups[g]):
            for h, stages in enumerate(groups):
                while drained[h] < state[h] - 1 - (h == g):
                    stages[drained[h]].drain()
                    drained[h] += 1
            advance(g, state[g])
            state[g] += 1
    for h, stages in enumerate(groups):
        for stage in stages[drained[h] :]:
            stage.drain()
    assert len(net.known) <= count


def step(images, smalls, bigs):
    time_bin, latents = smalls[0], smalls[3]
    qkv_weight, fc1_weight = bigs[4], bigs[6]
    d, ff = qkv_weight.shape[0], fc1_weight.shape[1]
    slots, chans, side, _ = latents.shape
    toks = side * side // 4
    planes = slots * chans * 4
    pairs = HEADS // 2
    heads = slots * HEADS
    out_shape = (
        jax.ShapeDtypeStruct((2 * ff + 4 * d, d), BF16),
        jax.ShapeDtypeStruct((images, E_ROWS, d), BF16),
        jax.ShapeDtypeStruct((images, L_ROWS, d), BF16),
        jax.ShapeDtypeStruct((2, planes, toks), F32),
    )
    scratch = [(w.shape, w.dtype) for w in bigs[4:]] + [
        ((4, 2, planes, toks), BF16), ((8, 8, d), F32), ((slots * 4, 16, toks), BF16),
        ((slots, 16, toks), BF16), ((16, d), BF16), ((16, d), BF16), ((toks, d), BF16), ((toks, d), BF16), ((slots * 4, d, toks), BF16),
        ((slots * 4, toks, d), F32), ((toks, 128), F32), ((slots * pairs, 4, toks, 128), BF16),
        ((slots * pairs, 4, toks, 128), BF16), ((heads, toks, 128), BF16), ((heads, 4, toks, toks), BF16),
        ((4, toks, toks), F32), ((4, toks, toks), F32), ((2, 1, toks), F32), ((heads, 1, toks), F32), ((heads, 1, toks), F32),
        ((heads, 64, toks), F32), ((slots * 12, toks, 128), BF16), ((slots * 12, toks, 128), BF16),
        ((slots, toks, d), BF16), ((slots, d, toks), BF16), ((slots, toks, d), BF16),
        ((slots, toks, d), F32), ((5, slots, 16, toks), F32),
        ((2 * ff + 4 * d, d), BF16), ((E_ROWS, d), F32), ((L_ROWS, d), F32), ((E_ROWS, d), BF16), ((L_ROWS, d), BF16), ((4, 2, planes, toks), BF16),
        ((3, E_ROWS, d), BF16), ((E_ROWS, d), BF16), ((3, L_ROWS, d), BF16), ((L_ROWS, d), BF16), ((3, 2, planes, toks), BF16),
    ]
    dma = pltpu.SemaphoreType.DMA
    parts_of = group_list(d, ff)
    count = sum(group_copies(images, plan) for _, _, plan in parts_of) + 2 * (3 + images - 1) + 6
    moved = [(s, BF16) for _, rows, plan in parts_of for s in group_shapes(images, rows, plan)]
    return pl.pallas_call(
        functools.partial(step_kernel, images, count),
        out_shape=out_shape,
        in_specs=[SMEM] * 3 + [VMEM] * (len(smalls) - 3) + [ANY] * len(bigs),
        out_specs=(VMEM,) * 4,
        scratch_shapes=[pltpu.VMEM(shape, kind) for shape, kind in scratch]
        + [dma((len(bigs),)), dma((3,)), dma((3,)), dma((count,)), dma((count,))]
        + [pltpu.VMEM(shape, kind) for shape, kind in moved],
        compiler_params=pltpu.CompilerParams(
            collective_id=0, has_side_effects=True, vmem_limit_bytes=64 * 1024 * 1024 - 65536
        ),
        name="step",
    )(*smalls, *bigs)


def finish_kernel(bins, classes, *refs):
    hbm_in, hbm_out, refs = refs[:6], refs[6:26], refs[26:]
    grads_ref, early_ref, late_ref, planes_ref, ada_ref, fada_ref = refs[:6]
    (out_ref, lat_ref, time_ref, class_ref, patch_ref, patch_b_ref, ada_g_ref, ada_b_ref, qkv_g_ref, qv_b_ref, proj_g_ref,
     proj_b_ref, fc1_g_ref, fc1_b_ref, fc2_g_ref, fc2_b_ref, fada_g_ref, fada_b_ref, out_gt_ref, out_b_ref) = outs = refs[6:26]
    in_sem, out_sem = refs[26:]
    d = ada_ref.shape[0]
    ff = fc1_g_ref.shape[1]
    blocks = ff // d
    pairs = HEADS // 2
    slots, chans, side, _ = lat_ref.shape
    groups = early_ref.shape[0]
    images = groups * slots
    held = -(-images // 32) * 32

    loads = []

    def fetch(src, dst):
        c = pltpu.make_async_copy(src, dst, in_sem.at[len(loads)])
        c.start()
        loads.append(c)

    for k in (1, 2):
        fetch(hbm_in[k], refs[k])
    bounds = [b * d for b in range(2 * blocks + 1)] + [2 * ff + 4 * d]
    for a, b in zip(bounds[:-1], bounds[1:]):
        fetch(hbm_in[0].at[a:b, :], grads_ref.at[a:b, :])
    for k in (4, 5, 3):
        fetch(hbm_in[k], refs[k])
    stores = []

    def send(k, *at):
        src, dst = outs[k], hbm_out[k]
        if at:
            src, dst = src.at[at], dst.at[at]
        c = pltpu.make_async_copy(src, dst, out_sem.at[len(stores)])
        c.start()
        stores.append(c)

    loads[0].wait()
    loads[1].wait()

    all_early = early_ref[...].reshape(groups * E_ROWS, d)
    all_late = late_ref[...].reshape(groups * L_ROWS, d)

    def chosen(block, rows, starts, steps):
        many = len(starts) * held
        line = iota((many, 1), 0)
        image = line % held
        item = line // held
        start, step = jnp.zeros_like(line), jnp.zeros_like(line)
        for k, (at, by) in enumerate(zip(starts, steps)):
            start = jnp.where(item == k, at, start)
            step = jnp.where(item == k, by, step)
        want = jnp.where(image < images, image // slots * rows + start + step * (image % slots), -1)
        return nn(flag(iota((many, groups * rows), 1) == want).astype(BF16), block)

    starts = [E_COND, E_COND + slots, E_IDS] + [E_MOD + k * slots for k in range(6)]
    picked = chosen(all_early, E_ROWS, starts, [1, 1, 0] + [1] * 6)
    items = [picked[k * held : (k + 1) * held] for k in range(9)]
    cond, ids = items[0] + items[1], items[2]
    picked = chosen(all_late, L_ROWS, [L_MOD, L_MOD + slots], [1, 1])
    dmods = [picked[:held], picked[held:]] + items[3:]
    img_row, lane = iota((held, d), 0), iota((held, d), 1)

    def id_part(k):
        return jnp.sum(jnp.where(lane == k * slots + img_row % slots, ids, 0.0), axis=1, keepdims=True)

    time_id, class_id = id_part(0), 256.0 * id_part(1) + id_part(2)

    left = jnp.concatenate(parts(swish(cond), 2), axis=0).T
    pairs_of = [jnp.concatenate([dmods[p], dmods[p + 1]], axis=1).astype(BF16) for p in range(0, 8, 2)]
    for k, pair in enumerate(pairs_of):
        grad = nn(left, jnp.concatenate([pair, pair], axis=0))
        if k < 3:
            lanes = slice(2 * k * d, 2 * (k + 1) * d)
            ada_g_ref[:, lanes] = grad
            send(6, slice(None), lanes)
        else:
            fada_g_ref[...] = grad
            send(16)

    for b in range(blocks):
        at = slice(b * d, (b + 1) * d)
        loads[2 + b].wait()
        fc2_g_ref[at, :] = grads_ref[at, :].astype(F32)
        send(14, at, slice(None))
    for b in range(blocks):
        at = slice(b * d, (b + 1) * d)
        loads[2 + blocks + b].wait()
        fc1_g_ref[:, at] = grads_ref[ff + b * d : ff + (b + 1) * d, :].astype(F32)
        send(12, slice(None), at)
    loads[2 + 2 * blocks].wait()
    third = d // 3
    for p in range(pairs):
        at = 2 * ff + p * (d + third)
        proj_g_ref[p * third : (p + 1) * third, :] = grads_ref[at + d : at + d + third, :].astype(F32)
        for k in range(3):
            lanes = slice(k * d + p * 128, k * d + (p + 1) * 128)
            qkv_g_ref[:, lanes] = grads_ref[at : at + d, k * 128 : (k + 1) * 128].astype(F32)
    send(8)
    send(10)

    for c in loads[3 + 2 * blocks :]:
        c.wait()
    dact = jnp.zeros((held, d), F32)
    for k, pair in enumerate(pairs_of):
        w = ada_ref[:, 2 * k * d : 2 * (k + 1) * d] if k < 3 else fada_ref[...]
        dact = dact + nt(pair, w)
    bias_rows = [col_sum(v) for v in dmods]
    ada_b_ref[...] = jnp.concatenate(bias_rows[:6], axis=1).reshape(6 * d)
    fada_b_ref[...] = jnp.concatenate(bias_rows[6:], axis=1).reshape(2 * d)
    sig = 1.0 / (1.0 + jnp.exp(-cond))
    dcond = dact * (sig * (1.0 + cond * (1.0 - sig)))
    stack = jnp.concatenate(parts(dcond, 2), axis=0)
    for ref, ids_col, many in ((class_ref, class_id, classes), (time_ref, time_id, bins)):
        wide = -(-many // 128) * 128
        at = iota((held, wide), 1).astype(F32)
        hit = flag((at == ids_col) & (iota((held, wide), 0) < images)).astype(BF16)
        ref[...] = tn(jnp.concatenate([hit, hit], axis=0), stack)[:many]
    send(3)
    send(2)

    early, late = jnp.sum(early_ref[...].astype(F32), axis=0), jnp.sum(late_ref[...].astype(F32), axis=0)
    swap = flag(iota((16, 16), 0) == (iota((16, 16), 1) ^ 3)).astype(BF16)

    def swapped(v):
        return tree([nn(swap, p) for p in parts(v, 2)] + [nn(swap, parts(v, 3)[2]), jnp.zeros_like(v)])

    patch_ref[...] = swapped(late[L_PATCH : L_PATCH + 16])
    out_gt_ref[...] = swapped(early[E_OUT : E_OUT + 16])

    def line(v, row):
        return v[row : row + 1, :]

    patch_b_ref[...] = line(late, L_PATCH_B).reshape(d)
    qv_b_ref[...] = jnp.concatenate([line(late, L_Q_B), line(late, L_V_B)], axis=1).reshape(2 * d)
    proj_b_ref[...] = line(early, E_PROJ_B).reshape(d)
    fc1_b_ref[...] = jnp.concatenate([line(early, E_FC1_B + b) for b in range(blocks)], axis=1).reshape(ff)
    fc2_b_ref[...] = line(early, E_FC2_B).reshape(d)
    tail = jnp.broadcast_to(line(early, E_OUT_B)[:, 0:16], (16, 16))
    pick = flag(iota((16, 16), 1) == (iota((16, 16), 0) ^ 3))
    column = jnp.sum(tail * pick, axis=1, keepdims=True)
    out_b_ref[...] = col_sum(jnp.where(iota((16, 16), 0) == iota((16, 16), 1), column, 0.0)).reshape(16)

    half = side // 2
    keep, spread, pick = plane_maps(slots, chans, side, half)
    for k in (4, 5, 7, 9, 11, 13, 15, 17, 18, 19):
        send(k)
    for k, ref in ((0, lat_ref), (1, out_ref)):
        many = 2 - k
        planes = jnp.concatenate(parts(planes_ref[k], many), axis=0)
        pieces, maps = [], []
        for j in range(2):
            wide = tn(jnp.concatenate([pick[j]] * many, axis=0), planes) * keep
            pieces += parts(wide, many)
            maps += [spread[j]] * many
        total = nt(jnp.concatenate(pieces, axis=1), jnp.concatenate(maps, axis=1))
        ref[...] = total.reshape(ref.shape).astype(ref.dtype)
        send(1 - k)
    for c in stores:
        c.wait()


def finish(bins, classes, latents, grads, early, late, planes, ada_weight, fada_weight, ff):
    d = ada_weight.shape[0]
    f = lambda *shape: jax.ShapeDtypeStruct(shape, F32)
    out_shape = (
        jax.ShapeDtypeStruct(latents.shape, BF16), f(*latents.shape), f(bins, d), f(classes, d), f(16, d), f(d),
        f(d, 6 * d), f(6 * d), f(d, 3 * d), f(2 * d), f(d, d), f(d), f(d, ff), f(ff), f(ff, d), f(d), f(d, 2 * d), f(2 * d),
        f(16, d), f(16),
    )
    ins = (grads, early, late, planes, ada_weight, fada_weight)
    dma = pltpu.SemaphoreType.DMA
    return pl.pallas_call(
        functools.partial(finish_kernel, bins, classes),
        out_shape=out_shape,
        in_specs=[ANY] * 6,
        out_specs=(ANY,) * len(out_shape),
        scratch_shapes=[pltpu.VMEM(x.shape, x.dtype) for x in ins + out_shape]
        + [dma((6 + 2 * (ff // d),)), dma((20 + 2 * (ff // d),))],
        compiler_params=pltpu.CompilerParams(vmem_limit_bytes=60 * 1024 * 1024),
        name="finish",
    )(*ins)


def local(
    images, latents, time_bin, class_label, live, time_table, class_table, patch_weight, patch_bias, ada_weight, ada_bias,
    qkv_weight, qv_bias, proj_weight, proj_bias, fc1_weight, fc1_bias, fc2_weight, fc2_bias, final_ada_weight,
    final_ada_bias, out_weight, out_bias, cotangent,
):
    d, ff = qkv_weight.shape[0], fc1_weight.shape[1]
    pos_a, pos_b = position_tables(LATENT // 2, d)
    smalls = (
        time_bin, class_label, live, latents, cotangent, patch_bias, ada_bias, qv_bias, proj_bias, fc1_bias, fc2_bias,
        final_ada_bias, out_bias, jnp.asarray(pos_a), jnp.asarray(pos_b), patch_weight, out_weight.T,
    )
    bigs = (time_table, class_table, ada_weight, final_ada_weight, qkv_weight, proj_weight, fc1_weight, fc2_weight)
    grads, early, late, planes = step(images, smalls, bigs)
    outs = list(
        finish(
            time_table.shape[0], class_table.shape[0], latents, grads, early, late, planes, ada_weight, final_ada_weight, ff
        )
    )
    outs[18] = outs[18].T
    return tuple(outs)


def solution(mesh):
    assert mesh.shape["row"] == 2 and mesh.shape["col"] == 2
    tiles = P("img", None, "row", "col")
    return jax.shard_map(
        functools.partial(local, mesh.shape["img"]),
        mesh=mesh,
        in_specs=(tiles,) + (P("img"),) * 3 + (P(),) * 18 + (tiles,),
        out_specs=(tiles, tiles) + (P(),) * 18,
        check_vma=False,
    )
```

```python
import functools

import jax
import jax.numpy as jnp
import numpy as np
from jax import lax
from jax.experimental import pallas as pl
from jax.experimental.pallas import tpu as pltpu
from jax.sharding import PartitionSpec as P

F32 = jnp.float32
BF16 = jnp.bfloat16
HEADS = 6
LATENT = 64
MESH = pl.DeviceIdType.MESH
VMEM = pl.BlockSpec(memory_space=pltpu.VMEM)
SMEM = pl.BlockSpec(memory_space=pltpu.SMEM)
ANY = pl.BlockSpec(memory_space=pl.ANY)


def nn(a, b):
    return lax.dot_general(a, b, (((1,), (0,)), ((), ())), preferred_element_type=F32)


def nt(a, b):
    return lax.dot_general(a, b, (((1,), (1,)), ((), ())), preferred_element_type=F32)


def tn(a, b):
    return lax.dot_general(a, b, (((0,), (0,)), ((), ())), preferred_element_type=F32)


def parts(v, many):
    out = []
    for _ in range(many):
        piece = v.astype(BF16)
        out.append(piece)
        v = v - piece.astype(F32)
    return out


def iota(shape, dim):
    return lax.broadcasted_iota(jnp.int32, shape, dim)


def flag(cond):
    return jnp.where(cond, 1.0, 0.0)


def swish(v):
    return v / (1.0 + jnp.exp(-v))


def position_tables(grid, width):
    quarter = width // 4
    omega = np.float32(1.0) / np.power(
        np.float32(10000.0), np.arange(quarter, dtype=np.float32) / np.float32(quarter)
    )
    angles = np.arange(grid, dtype=np.float32)[:, None] * omega[None, :].astype(np.float32)
    single = np.concatenate([np.sin(angles), np.cos(angles)], axis=1).astype(np.float32)
    blank = np.zeros_like(single)
    return np.concatenate([single, blank], axis=1), np.concatenate([blank, single], axis=1)


def plane_maps(slots, chans, side, halves):
    rows = slots * chans * side
    lanes = halves * halves
    spread = []
    keep = flag(iota((rows, lanes), 0) % side // 2 == iota((rows, lanes), 1) // halves)
    pick = []
    for j in range(2):
        col = iota((side, lanes), 0)
        spread.append(flag(col == iota((side, lanes), 1) % halves * 2 + j).astype(BF16))
        many = slots * chans * 4
        out, src = iota((many, rows), 0), iota((many, rows), 1)
        same = (out // 4 == src // side) & (out % 4 // 2 == src % 2) & (out % 2 == j)
        pick.append(flag(same).astype(BF16))
    return keep, spread, pick


def shift_masks(halves):
    row, lane = iota((16, halves * halves), 0), iota((16, halves * halves), 1)
    return row % 4 >= 2, row % 2 == 1, lane, halves


def shift_in(planes, masks):
    odd_row, odd_col, lane, side = masks
    full = side * side
    down = [
        jnp.where(
            odd_row,
            jnp.where(lane < side, pltpu.roll(planes[s ^ 2], side, 1), pltpu.roll(planes[s], side, 1)),
            planes[s],
        )
        for s in range(4)
    ]
    return [
        jnp.where(
            odd_col,
            jnp.where(
                lane % side == 0, pltpu.roll(down[s ^ 1], full - side + 1, 1), pltpu.roll(down[s], 1, 1)
            ),
            down[s],
        )
        for s in range(4)
    ]


def shift_out(planes, masks):
    odd_row, odd_col, lane, side = masks
    full = side * side
    up = [
        jnp.where(
            odd_row,
            jnp.where(
                lane >= full - side,
                pltpu.roll(planes[s ^ 2], full - side, 1),
                pltpu.roll(planes[s], full - side, 1),
            ),
            planes[s],
        )
        for s in range(4)
    ]
    return [
        jnp.where(
            odd_col,
            jnp.where(
                lane % side == side - 1, pltpu.roll(up[s ^ 1], side - 1, 1), pltpu.roll(up[s], full - 1, 1)
            ),
            up[s],
        )
        for s in range(4)
    ]


def mate(slot):
    row, col = lax.axis_index("row"), lax.axis_index("col")
    return {"row": row ^ (slot >> 1), "col": col ^ (slot & 1)}


def norm(v):
    share = 1.0 / v.shape[-1]
    centred = v - jnp.sum(v, axis=-1, keepdims=True) * share
    spread = jnp.sum(centred * centred, axis=-1, keepdims=True) * share
    inv = lax.rsqrt(spread + 1e-06)
    return centred * inv, inv


def norm_back(hat, inv, grad):
    share = 1.0 / hat.shape[-1]
    first = jnp.sum(grad, axis=-1, keepdims=True) * share
    second = jnp.sum(grad * hat, axis=-1, keepdims=True) * share
    return inv * (grad - first - hat * second)


def col_sum(v):
    return jnp.sum(v, axis=0, keepdims=True)


E_OUT, E_PROJ_B, E_FC2_B, E_FC1_B, E_OUT_B, E_MOD, E_COND, E_IDS, E_ROWS = 0, 16, 17, 18, 22, 23, 41, 47, 48
L_PATCH, L_PATCH_B, L_MOD, L_Q_B, L_V_B, L_ROWS = 0, 16, 17, 23, 24, 32


def tree(terms):
    while len(terms) > 1:
        terms = [terms[i] + terms[i + 1] for i in range(0, len(terms), 2)]
    return terms[0]


class Copies:
    def __init__(self, send_sem, recv_sem):
        self.send_sem, self.recv_sem, self.known = send_sem, recv_sem, {}

    def make(self, key, src, dst, device):
        at = self.known.setdefault(key, len(self.known))
        return pltpu.make_async_remote_copy(
            src_ref=src, dst_ref=dst, send_sem=self.send_sem.at[at], recv_sem=self.recv_sem.at[at],
            device_id=device, device_id_type=MESH,
        )


class Stage:
    def __init__(self, copies, reduce=None):
        self.copies, self.reduce = copies, reduce

    def start(self):
        for c in self.copies():
            c.start()

    def finish(self):
        for c in self.copies():
            c.wait_recv()
        if self.reduce is not None:
            self.reduce()

    def drain(self):
        for c in self.copies():
            c.wait_send()


def far(distance):
    return {"img": lax.axis_index("img") ^ distance}


def rows_at(start, many):
    return pl.ds(pl.multiple_of(start, 16), many)


def ways(images, plan):
    bits = images.bit_length() - 1
    kept = ["".join(x for x in way if not x.isdigit() or int(x) < bits) for way in plan]
    return [way for way in kept if way]


def shared_bits(images, plan):
    return max([int(x) + 1 for way in ways(images, plan) for x in way if x.isdigit()] + [0])


def members(way):
    return 1 << len(way)


def position(way):
    total = 0
    for x in way:
        if x.isdigit():
            side = (lax.axis_index("img") >> int(x)) & 1
        else:
            side = lax.axis_index({"c": "col", "r": "row"}[x])
        total = 2 * total + side
    return total


def partner(way, delta):
    device, flips = {}, 0
    for k, x in enumerate(reversed(way)):
        if delta >> k & 1:
            if x.isdigit():
                flips |= 1 << int(x)
            else:
                name = {"c": "col", "r": "row"}[x]
                device[name] = 1 - lax.axis_index(name)
    if flips:
        device["img"] = lax.axis_index("img") ^ flips
    return device


def group_shapes(images, rows, plan):
    d, shapes = 384, []
    for way in ways(images, plan):
        many = members(way)
        rows //= many
        shapes += [(many - 1, rows, d), (rows, d)]
    high = images >> shared_bits(images, plan)
    if high > 1:
        shapes += [(high - 1, rows, d), (rows, d)]
    return shapes


def group_copies(images, plan):
    return 2 * sum(members(way) - 1 for way in ways(images, plan)) + (images >> shared_bits(images, plan)) - 1


def group_stages(name, images, base, rows, plan, grads, out, bufs, net):
    bufs = list(bufs)
    known = ways(images, plan)
    shared = shared_bits(images, plan)
    high = images >> shared

    def add(*refs):
        return tree([r.astype(F32) for r in refs]).astype(BF16)

    def scatter(k, way, held, many, got, total, last):
        count = members(way)

        def copies():
            return [
                net.make(f"{name}s{k}.{e}", held((position(way) ^ e) * many, many), got.at[e - 1], partner(way, e))
                for e in range(1, count)
            ]

        def reduce():
            total[...] = add(held(position(way) * many, many)[...], *[got[e] for e in range(count - 1)])
            if last:
                out[rows_at(base + start(len(known)), many), :] = total[...]

        return Stage(copies, reduce)

    sizes = [rows]
    for way in known:
        sizes.append(sizes[-1] // members(way))

    def start(level):
        total = 0
        for k in range(level):
            total = total + position(known[k]) * sizes[k + 1]
        return total

    stages = []

    def held(at, many):
        return grads.at[rows_at(base + at, many), :]

    for k, way in enumerate(known):
        got, total = bufs[:2]
        del bufs[:2]
        stages.append(scatter(k, way, held, sizes[k + 1], got, total, high == 1 and k == len(known) - 1))

        def held(at, many, total=total):
            return total.at[rows_at(at, many), :]

    if high > 1:
        got, final = bufs[:2]
        summed, many = total, sizes[-1]

        def copies():
            return [net.make(f"{name}h{e}", summed, got.at[e - 1], far(e << shared)) for e in range(1, high)]

        def reduce():
            final[...] = add(summed[...], *[got[e] for e in range(high - 1)])
            out[rows_at(base + start(len(known)), many), :] = final[...]

        stages.append(Stage(copies, reduce))

    def gather(k, way):
        def copies():
            at = out.at[rows_at(base + start(k + 1), sizes[k + 1]), :]
            return [net.make(f"{name}g{k}.{e}", at, at, partner(way, e)) for e in range(1, members(way))]

        return Stage(copies)

    for k in reversed(range(len(known))):
        stages.append(gather(k, known[k]))
    return stages


def sum_stages(name, images, block, got, total, out, net):
    def c0():
        return [net.make(name + "m" + str(s), block, got.at[s - 1], mate(s)) for s in (1, 2, 3)]

    def r0():
        t = tree([r.astype(F32) for r in (block[...], got[0], got[1], got[2])]).astype(BF16)
        total[...] = t
        out[lax.axis_index("img")] = t

    def c1():
        at = out.at[lax.axis_index("img")]
        return [net.make(name + "i" + str(d), total, at, far(d)) for d in range(1, images)]

    return [Stage(c0, r0), Stage(c1)]


def edge_stages(name, edge, got, out, net):
    def c0():
        return [net.make(name + str(s), edge.at[s], got.at[s - 1], mate(s)) for s in (1, 2, 3)]

    def r0():
        out[...] = tree([r.astype(F32) for r in (edge[0], got[1], got[0], got[2])])

    return [Stage(c0, r0)]


SLOW = (("c", "r", "0", "12"), ("c", "0", "1", "r2"), ("c", "1", "r", "02"))
FAST = (("c", "r0", "12"), ("c", "01", "r2"), ("c", "r012"))
FC, PAIR, EARLY, LATE, EDGE_L = 0, 3, 6, 7, 8
IMAGE_EVENTS = ((2, 0, 1),)
GRAD_EVENTS = ()
BACK_EVENTS = ((1, 0, 2), (1, 1, 1), (1, 2, 1), (3, 0, 3), (3, 6, 1), (4, 1, 2), (4, 2, 2), (5, 0, 4), (5, 3, 1), (6, 1, 3), (6, 2, 3), (8, 0, 5), (8, 3, 2), (8, 4, 1), (8, 6, 2))
TAIL_EVENTS = ((0, 1, 4), (0, 2, 4), (2, 0, 6), (4, 3, 3), (4, 5, 1), (6, 1, 5), (6, 2, 5), (8, 4, 2))
END_EVENTS = (0, 3, 1, 2, 4, 5, 0, 7, 8, 3, 1, 2, 4, 3, 7, 1, 2, 5, 5, 4, 4)


def group_list(d, ff):
    large, rows = 2 * ff // 3, d + d // 3
    out = [(k * large, large, SLOW[k]) for k in range(3)]
    return out + [(2 * ff + k * rows, rows, FAST[k]) for k in range(3)]


def step_kernel(images, count, *refs):
    refs = list(refs)

    def take(n):
        out = refs[:n]
        del refs[:n]
        return out

    (time_ref, class_ref, live_ref, lat_ref, cot_ref, patch_b_ref, ada_b_ref, qv_b_ref, proj_b_ref, fc1_b_ref, fc2_b_ref,
     fada_b_ref, out_b_ref, pos_a_ref, pos_b_ref, patch_w_ref, out_wt_ref) = take(17)
    hbm = take(8)
    out_ref, early_out, late_out, planes_out = take(4)
    held = take(4)
    qkv_ref, proj_ref, fc1_ref, fc2_ref = held
    (planes_ref, mod_s, pt_s, gy_s, wp_s, wo_s, x1_s, x1_b, x1t_s, hat_s, inv_s, k_s, v_s, q_s, e_s, sa_s, sb_s, top_s,
     linv_s, delta_s, of_s, a_s, b_s, dm_s, x2t_s, da_s, dx_s, edge_s,
     grads_ref, early_ref, late_ref, early_16, late_16, edge_l, early_got, early_sum, late_got, late_sum, edge_l_got) = take(39)
    load_sem, gather_send, gather_recv, send_sem, recv_sem = take(5)
    bufs = refs

    d = qkv_ref.shape[0]
    slots, chans, side, _ = lat_ref.shape
    toks = x1_s.shape[0]
    pairs = HEADS // 2
    ff = fc1_ref.shape[1]
    blocks = ff // d
    half = side // 2
    bins, classes = hbm[0].shape[0], hbm[1].shape[0]

    loads = [pltpu.make_async_copy(a, b, load_sem.at[4 + i]) for i, (a, b) in enumerate(zip(hbm[4:], held))]
    net = Copies(send_sem, recv_sem)
    groups = []
    for g, (base, rows, plan) in enumerate(group_list(d, ff)):
        n = len(group_shapes(images, rows, plan))
        groups.append(group_stages("g" + str(g), images, base, rows, plan, grads_ref, out_ref, bufs[:n], net))
        del bufs[:n]
    groups.append(sum_stages("e", images, early_16, early_got, early_sum, early_out, net))
    groups.append(sum_stages("l", images, late_16, late_got, late_sum, late_out, net))
    groups.append(edge_stages("x", edge_l, edge_l_got, planes_out, net))
    def advance(g, k):
        if k > 0:
            groups[g][k - 1].finish()
        if k < len(groups[g]):
            groups[g][k].start()

    def row_of(ref, start, many):
        return ref[...].astype(F32).reshape(1, ref.shape[0])[:, start : start + many]

    early_ref[...] = jnp.zeros_like(early_ref)
    late_ref[...] = jnp.zeros_like(late_ref)

    swap = flag(iota((16, 16), 0) == (iota((16, 16), 1) ^ 3)).astype(BF16)
    wp_s[...] = nn(swap, patch_w_ref[...]).astype(BF16)
    wo_s[...] = nn(swap, out_wt_ref[...]).astype(BF16)
    out_bias = jnp.sum(
        flag(iota((16, 16), 1) == (iota((16, 16), 0) ^ 3)) * row_of(out_b_ref, 0, 16), axis=1, keepdims=True
    )

    inv_lane = iota((toks, 128), 1)

    def opening(time_table_ref, class_table_ref, ada_ref, fada_ref, pos_s):
        tables = [
            pltpu.make_async_copy(a, b, load_sem.at[i])
            for i, (a, b) in enumerate(zip(hbm[:4], (time_table_ref, class_table_ref, ada_ref, fada_ref)))
        ]
        for c in tables + loads:
            c.start()
        peers = [mate(s) for s in (1, 2, 3)] + [far(k) for k in range(1, images)]
        barrier = pltpu.get_barrier_semaphore()
        for peer in peers:
            pl.semaphore_signal(barrier, inc=1, device_id=peer, device_id_type=MESH)
        keep, spread, pick = plane_maps(slots, chans, side, half)
        for k, ref in enumerate((lat_ref, cot_ref)):
            tile = ref[...].reshape(slots * chans * side, side)
            total = None
            for j in range(2):
                wide = (nn(tile, spread[j]) * keep).astype(BF16)
                term = nn(pick[j], wide)
                total = term if total is None else total + term
            planes_ref[0, k] = total.astype(BF16)
        pl.semaphore_wait(barrier, len(peers))
        gathers = []
        for s in (1, 2, 3):
            c = pltpu.make_async_remote_copy(
                src_ref=planes_ref.at[0], dst_ref=planes_ref.at[s], send_sem=gather_send.at[s - 1], recv_sem=gather_recv.at[s - 1],
                device_id=mate(s), device_id_type=MESH,
            )
            c.start()
            gathers.append(c)

        my_row, my_col = lax.axis_index("row"), lax.axis_index("col")
        patch_b = row_of(patch_b_ref, 0, d)
        for s in range(4):
            ta = pos_a_ref[pl.ds(pl.multiple_of((my_row ^ (s >> 1)) * half, half), half), :]
            tb = pos_b_ref[pl.ds(pl.multiple_of((my_col ^ (s & 1)) * half, half), half), :] + patch_b
            for a in range(half):
                pos_s[s, a * half : (a + 1) * half, :] = ta[a : a + 1, :] + tb

        def onehot(ids_ref, many):
            row, lane = iota((16, many), 0), iota((16, many), 1)
            hit = jnp.zeros((16, many), F32)
            for i in range(slots):
                hit = hit + flag((row == i) & (lane == ids_ref[i]))
            return hit.astype(BF16)

        for c in tables:
            c.wait()
        cond = nn(onehot(time_ref, bins), time_table_ref[...]) + nn(onehot(class_ref, classes), class_table_ref[...])
        cond = cond[:8]
        act = parts(swish(cond), 3)
        act = jnp.concatenate([p.astype(F32) for p in act] + [jnp.zeros((8, d), F32)], axis=0).astype(BF16)
        for p in range(8):
            w = ada_ref[:, p * d : (p + 1) * d] if p < 6 else fada_ref[:, (p - 6) * d : (p - 5) * d]
            m = nn(act, w)
            b = row_of(ada_b_ref, p * d, d) if p < 6 else row_of(fada_b_ref, (p - 6) * d, d)
            mod_s[p] = m[0:8] + m[8:16] + m[16:24] + b
        row, lane = iota((8, d), 0), iota((8, d), 1)
        ids = jnp.zeros((8, d), F32)
        for i in range(slots):
            for k, v in enumerate((time_ref[i], class_ref[i] // 256, class_ref[i] % 256)):
                ids = ids + jnp.where((row == 0) & (lane == k * slots + i), 0.25 * v.astype(F32), 0.0)
        high = cond.astype(BF16).astype(F32)
        early_ref[E_COND : E_COND + slots, :] = 0.25 * high[:slots]
        early_ref[E_COND + slots : E_COND + 2 * slots, :] = 0.25 * (cond - high)[:slots]
        early_ref[E_IDS : E_IDS + 1, :] = ids[0:1]

        for c in gathers:
            c.wait_recv()
        masks = shift_masks(half)
        live = [live_ref[i].astype(F32) for i in range(slots)]
        for i in range(slots):
            lat = shift_in([planes_ref[s, 0, i * 16 : (i + 1) * 16, :].astype(F32) for s in range(4)], masks)
            cot = shift_in([planes_ref[s, 1, i * 16 : (i + 1) * 16, :].astype(F32) for s in range(4)], masks)
            for s in range(4):
                pt_s[i * 4 + s] = lat[s].astype(BF16)
            gy_s[i] = (cot[0] * live[i]).astype(BF16)

        v_bias = row_of(qv_b_ref, d, d)

        def token_norm(t, x1_buf):
            img, slot = t // 4, t % 4
            tok = tn(pt_s[t], wp_s[...]) + pos_s[slot]
            dx_s[img] = tok
            hat, inv = norm(tok)
            hat_s[t] = hat
            inv_s[...] = jnp.where(inv_lane == t, inv, inv_s[...])
            x1_buf[...] = (hat * (1.0 + mod_s[1, pl.ds(img, 1), :]) + mod_s[0, pl.ds(img, 1), :]).astype(BF16)

        def token_keys(t, x1_buf):
            img, slot = t // 4, t % 4
            x1 = x1_buf[...]
            keys = nn(x1, qkv_ref[:, d : 2 * d]).astype(BF16)
            vals = (nn(x1, qkv_ref[:, 2 * d :]) + v_bias).astype(BF16)
            for p in range(pairs):
                k_s[img * pairs + p, slot] = keys[:, p * 128 : (p + 1) * 128]
                v_s[img * pairs + p, slot] = vals[:, p * 128 : (p + 1) * 128]
            x1t_s[t] = x1.T

        def reverse(n):
            return n // 4 * 4 + 3 - n % 4

        token_norm(jnp.int32(3), x1_s)
        loads[0].wait()

        def tokens(n, carry):
            token_norm(reverse(2 * n + 1), x1_b)
            token_keys(reverse(2 * n), x1_s)
            token_norm(reverse(jnp.minimum(2 * n + 2, slots * 4 - 1)), x1_s)
            token_keys(reverse(2 * n + 1), x1_b)
            return carry

        lax.fori_loop(0, slots * 2, tokens, 0)

        for c in gathers:
            c.wait_send()

    pl.run_scoped(
        opening,
        *[pltpu.VMEM(hbm[i].shape, BF16) for i in range(4)],
        pltpu.VMEM((4, toks, d), F32),
    )
    masks = shift_masks(half)

    lane128 = iota((1, 128), 1) // 64
    head_mask = [flag(lane128 == h) for h in range(2)]

    q_bias = row_of(qv_b_ref, 0, d)

    def queries(img, carry):
        query = tn(x1t_s[img * 4], qkv_ref[:, :d]) + q_bias
        query = query.astype(BF16).astype(F32) * 0.125
        for p in range(pairs):
            for h in range(2):
                q_s[img * HEADS + p * 2 + h] = (query[:, p * 128 : (p + 1) * 128] * head_mask[h]).astype(BF16)
        return carry

    lax.fori_loop(0, slots, queries, 0)

    def scores(idx, h, buf):
        top = None
        for c in range(4):
            s = nt(k_s[idx, c], q_s[idx * 2 + h])
            buf[c] = s
            m = jnp.max(s, axis=0, keepdims=True)
            top = m if top is None else jnp.maximum(top, m)
        top_s[h] = top

    def softmax(idx, h, buf, vt):
        head = idx * 2 + h
        top, total, acc = top_s[h], None, None
        for c in range(4):
            e = jnp.exp(buf[c] - top)
            l = col_sum(e)
            total = l if total is None else total + l
            eb = e.astype(BF16)
            e_s[head, c] = eb
            o = nn(vt[c][h * 64 : (h + 1) * 64], eb)
            acc = o if acc is None else acc + o
        linv = 1.0 / total
        linv_s[head] = linv
        of_s[head] = acc * linv

    scores(jnp.int32(0), 0, sa_s)

    def attend(idx, carry):
        vt = [v_s[idx, c].T for c in range(4)]
        scores(idx, 1, sb_s)
        softmax(idx, 0, sa_s, vt)
        scores(jnp.minimum(idx + 1, slots * pairs - 1), 0, sa_s)
        softmax(idx, 1, sb_s, vt)
        return carry

    lax.fori_loop(0, slots * pairs, attend, 0)
    for c in loads[1:]:
        c.wait()
    proj_b, fc1_b, fc2_b = row_of(proj_b_ref, 0, d), row_of(fc1_b_ref, 0, ff), row_of(fc2_b_ref, 0, d)

    def closing(dot_s, dom_s, dq_s, dxq_s, acc_s, dx1_s):
        def pair_row(k):
            return 2 * ff + k * (d + d // 3)

        def wide(ref, img, b):
            return jnp.concatenate([ref[img * 12 + b * 3 + j] for j in range(3)], axis=1)

        def fc2_grad(b, carry):
            total = tree([tn(wide(a_s, img, b), dm_s[img]) for img in range(2)])
            for img in range(2, slots):
                total = total + tn(wide(a_s, img, b), dm_s[img])
            grads_ref[rows_at(b * d, d), :] = total.astype(BF16)
            started(b, 0)
            return carry

        def started(b, before):
            for g in range(FC, PAIR):
                last = -(-(g + 1) * (2 * ff // 3) // d) - 1 - before
                if 0 <= last < blocks:

                    @pl.when(b == last)
                    def _():
                        advance(g, 0)

        def when_at(i, plan):
            for at, events in plan.items():

                @pl.when(i == at)
                def _():
                    for g, k in events:
                        advance(g, k)

        image_plan, grad_plan, back_plan, tail_plan = {}, {}, {}, {}
        for plan, events in ((image_plan, IMAGE_EVENTS), (grad_plan, GRAD_EVENTS), (back_plan, BACK_EVENTS), (tail_plan, TAIL_EVENTS)):
            for at, g, k in events:
                if k <= len(groups[g]):
                    plan.setdefault(at, []).append((g, k))

        def inv_at(t):
            return jnp.sum(jnp.where(inv_lane == t, inv_s[...], 0.0), axis=1, keepdims=True)

        def image(img, carry):
            def mod_row(p):
                return mod_s[p, pl.ds(img, 1), :]

            ot = jnp.concatenate([of_s[img * HEADS + h] for h in range(HEADS)], axis=0).astype(BF16)
            branch = tn(ot, proj_ref[...]) + proj_b
            g1 = mod_row(2)
            resid = dx_s[img] + g1 * branch
            hat2, inv2 = norm(resid)
            sa_s[img] = hat2[:, :toks]
            sb_s[img, :, : d - toks] = hat2[:, toks:]
            inv_s[...] = jnp.where(inv_lane == slots * 4 + img, inv2, inv_s[...])
            x2 = (hat2 * (1.0 + mod_row(4)) + mod_row(3)).astype(BF16)
            x2t_s[img] = x2.T
            hiddens = []
            k0, k1 = 0.7978845608028654, 0.044715
            def first(b):
                return nn(x2, fc1_ref[:, b * d : (b + 1) * d])

            u = first(0)
            for b in range(blocks):
                at_b = slice(b * d, (b + 1) * d)
                ahead = first(b + 1) if b + 1 < blocks else None
                u = u + fc1_b[:, at_b]
                sq = u * u
                inner = k0 + (k0 * k1) * sq
                cdf = 0.5 + 0.5 * jnp.tanh(u * inner)
                hidden = u * cdf
                slope = cdf + (hidden - hidden * cdf) * (6.0 * inner - 4.0 * k0)
                hidden = hidden.astype(BF16)
                slope = slope.astype(BF16)
                for j in range(3):
                    a_s[img * 12 + b * 3 + j] = hidden[:, j * 128 : (j + 1) * 128]
                    b_s[img * 12 + b * 3 + j] = slope[:, j * 128 : (j + 1) * 128]
                hiddens.append(hidden)
                u = ahead
            mlp = nn(jnp.concatenate(hiddens, axis=1), fc2_ref[...])
            mlp = mlp + fc2_b
            g2 = mod_row(5)
            x3 = resid + g2 * mlp
            hatf, invf = norm(x3)
            scf = 1.0 + mod_row(7)
            xf = (hatf * scf + mod_row(6)).astype(BF16)
            edge_s[4, img] = (nt(wo_s[...], xf) + out_bias) * live_ref[img].astype(F32)
            gy = gy_s[img]
            early_ref[E_OUT : E_OUT + 16, :] += nn(gy, xf)
            early_ref[E_OUT_B : E_OUT_B + 1, 0:16] += nt(jnp.ones((8, toks), BF16), gy)[0:1]
            dxf = tn(gy, wo_s[...])

            def put_mod(p, v):
                early_ref[pl.ds(E_MOD + (p - 2) * slots + img, 1), :] = v

            put_mod(6, col_sum(dxf))
            put_mod(7, col_sum(dxf * hatf))
            dx3 = norm_back(hatf, invf, dxf * scf)
            dm = (g2 * dx3).astype(BF16)
            dm_s[img] = dm
            put_mod(5, col_sum(mlp * dx3))
            early_ref[E_FC2_B : E_FC2_B + 1, :] += col_sum(dm.astype(F32))
            dx_s[img] = dx3
            return carry

        lax.fori_loop(0, slots, image, 0)
        lax.fori_loop(0, blocks, fc2_grad, 0)

        def image_back(img, carry):
            when_at(img, image_plan)

            def mod_row(p):
                return mod_s[p, pl.ds(img, 1), :]

            def put_mod(p, v):
                early_ref[pl.ds(E_MOD + (p - 2) * slots + img, 1), :] = v

            g1, dm = mod_row(2), dm_s[img]
            hat2 = jnp.concatenate([sa_s[img], sb_s[img, :, : d - toks]], axis=1)
            inv2 = inv_at(slots * 4 + img)
            dus = []
            def second(b):
                return nt(dm, fc2_ref[b * d : (b + 1) * d, :])

            dh = second(0)
            for b in range(blocks):
                ahead = second(b + 1) if b + 1 < blocks else None
                slope = jnp.concatenate([b_s[img * 12 + b * 3 + j] for j in range(3)], axis=1).astype(F32)
                du = (dh * slope).astype(BF16)
                for j in range(3):
                    b_s[img * 12 + b * 3 + j] = du[:, j * 128 : (j + 1) * 128]
                early_ref[E_FC1_B + b : E_FC1_B + b + 1, :] += col_sum(du.astype(F32))
                dus.append(du)
                dh = ahead
            dx2 = nt(jnp.concatenate(dus, axis=1), fc1_ref[...])
            put_mod(3, col_sum(dx2))
            put_mod(4, col_sum(dx2 * hat2))
            dx = dx_s[img] + norm_back(hat2, inv2, dx2 * (1.0 + mod_row(4)))
            dx_s[img] = dx
            ot = jnp.concatenate([of_s[img * HEADS + h] for h in range(HEADS)], axis=0).astype(BF16)
            branch = tn(ot, proj_ref[...]) + proj_b
            put_mod(2, col_sum(branch * dx))
            da = (g1 * dx).astype(BF16)
            da_s[img] = da
            early_ref[E_PROJ_B : E_PROJ_B + 1, :] += col_sum(da.astype(F32))
            dot = nt(proj_ref[...], da)
            blank = jnp.zeros((64, toks), F32)
            for hd in range(HEADS):
                head = img * HEADS + hd
                piece = dot[hd * 64 : (hd + 1) * 64]
                linv = linv_s[head]
                delta_s[head] = col_sum(piece * of_s[head]) * linv
                piece = piece * linv
                wide = jnp.concatenate([piece, blank] if hd % 2 == 0 else [blank, piece], axis=0).astype(BF16)
                dot_s[head] = wide
                dom_s[head] = wide.T
            return carry

        lax.fori_loop(0, slots, image_back, 0)

        def fc1_grad(b, carry):
            when_at(b, grad_plan)
            total = tree([nn(x2t_s[img], wide(b_s, img, b)) for img in range(2)])
            for img in range(2, slots):
                total = total + nn(x2t_s[img], wide(b_s, img, b))
            grads_ref[rows_at(ff + b * d, d), :] = total.astype(BF16)
            started(b, blocks)
            return carry

        lax.fori_loop(0, blocks, fc1_grad, 0)
        total = None
        for img in range(slots):
            ot = jnp.concatenate([of_s[img * HEADS + h] for h in range(HEADS)], axis=0).astype(BF16)
            term = nn(ot, da_s[img])
            total = term if total is None else total + term
        for k in range(pairs):
            grads_ref[pair_row(k) + d : pair_row(k + 1), :] = total[k * (d // 3) : (k + 1) * (d // 3)].astype(BF16)
        blank = jnp.zeros((16, toks), F32)
        for i in range(slots):
            out = shift_out([edge_s[4, i], blank, blank, blank], masks)
            for s in range(4):
                edge_l[s, 1, i * 16 : (i + 1) * 16, :] = out[s].astype(BF16)
        early_16[...] = early_ref[...].astype(BF16)
        advance(EARLY, 0)

        acc_s[...] = jnp.zeros_like(acc_s)

        def attend_back(it, carry):
            when_at(it, back_plan)
            p, img = it // slots, it % slots
            idx = img * pairs + p
            dqt = [None, None]
            jobs = [(c, h) for c in range(4) for h in range(2)]

            def product(job):
                return nn(v_s[idx, job[0]], dot_s[idx * 2 + job[1]])

            dp, soon = product(jobs[0]), product(jobs[1])
            gathered = None
            sum_v = None
            dkv = []
            for n, (c, h) in enumerate(jobs):
                head = idx * 2 + h
                ahead = product(jobs[n + 2]) if n + 2 < len(jobs) else None
                if h == 0:
                    kt = k_s[idx, c].T
                    dk, dv = None, None
                e = e_s[head, c]
                ds = (e.astype(F32) * (dp - delta_s[head])).astype(BF16)
                dk_h, dv_h = nn(ds, q_s[head]), nn(e, dom_s[head])
                dk = dk_h if dk is None else dk + dk_h
                dv = dv_h if dv is None else dv + dv_h
                dq_h = nn(kt[h * 64 : (h + 1) * 64], ds)
                dqt[h] = dq_h if dqt[h] is None else dqt[h] + dq_h
                dp, soon = soon, ahead
                if h == 1:
                    dk, dv = dk.astype(BF16), dv.astype(BF16)
                    a_s[idx * 4 + c] = dk
                    b_s[idx * 4 + c] = dv
                    sv = col_sum(dv.astype(F32))
                    sum_v = sv if sum_v is None else sum_v + sv
                    dkv.append(jnp.concatenate([dk, dv], axis=1))
            x1t = jnp.concatenate([x1t_s[img * 4 + c] for c in range(4)], axis=1)
            gathered = nn(x1t, jnp.concatenate(dkv, axis=0))
            dq = (jnp.concatenate(dqt, axis=0) * 0.125).T.astype(BF16)
            dq_s[idx] = dq
            lanes = pl.ds(pl.multiple_of(p * 128, 128), 128)
            late_ref[L_V_B : L_V_B + 1, lanes] += sum_v
            late_ref[L_Q_B : L_Q_B + 1, lanes] += col_sum(dq.astype(F32))
            acc_s[:, 128:] += gathered
            acc_s[:, :128] += nn(x1t_s[img * 4], dq)

            for pair in range(pairs):

                @pl.when(it == pair * slots + slots - 1)
                def _():
                    at = pair_row(pair)
                    grads_ref[at : at + d, :] = acc_s[...].astype(BF16)
                    acc_s[...] = jnp.zeros_like(acc_s)
                    advance(PAIR + pair, 0)

            return carry

        lax.fori_loop(0, slots * pairs, attend_back, 0)

        def joined(ref, img, slot):
            return [ref[(img * pairs + p) * 4 + slot] for p in range(pairs)]

        def query_back(img, carry):
            dq = jnp.concatenate([dq_s[img * pairs + p] for p in range(pairs)], axis=1)
            dxq_s[img] = nt(dq, qkv_ref[:, :d])
            return carry

        lax.fori_loop(0, slots, query_back, 0)

        def product_back(t):
            img, slot = t // 4, t % 4
            dkv = jnp.concatenate(joined(a_s, img, slot) + joined(b_s, img, slot), axis=1)
            own = jnp.where(slot == 0, 1.0, 0.0)
            return nt(dkv, qkv_ref[:, d:]) + dxq_s[img] * own

        dx1_s[...] = product_back(jnp.int32(0))
        def tokens_back(t, carry):
            when_at(t, tail_plan)
            img, slot = t // 4, t % 4
            dx1 = dx1_s[...]
            ahead = product_back(jnp.minimum(t + 1, slots * 4 - 1))
            hat = hat_s[t]
            late_ref[pl.ds(L_MOD + img, 1), :] += col_sum(dx1)
            late_ref[pl.ds(L_MOD + slots + img, 1), :] += col_sum(dx1 * hat)
            own = jnp.where(slot == 0, 1.0, 0.0)
            dtok = norm_back(hat, inv_at(t), dx1 * (1.0 + mod_s[1, pl.ds(img, 1), :])) + dx_s[img] * own
            late_ref[L_PATCH_B : L_PATCH_B + 1, :] += col_sum(dtok)
            dtok = dtok.astype(BF16)
            late_ref[L_PATCH : L_PATCH + 16, :] += nn(pt_s[t], dtok)
            for p in range(pairs):
                a_s[(img * pairs + p) * 4 + slot] = dtok[:, p * 128 : (p + 1) * 128]
            dx1_s[...] = ahead
            return carry

        lax.fori_loop(0, slots * 4, tokens_back, 0)

    pl.run_scoped(
        closing,
        pltpu.VMEM((slots * HEADS, 128, toks), BF16),
        pltpu.VMEM((slots * HEADS, toks, 128), BF16),
        pltpu.VMEM((slots * pairs, toks, 128), BF16),
        pltpu.VMEM((slots, toks, d), F32),
        pltpu.VMEM((d, d), F32),
        pltpu.VMEM((toks, d), F32),
    )

    late_16[...] = late_ref[...].astype(BF16)
    advance(LATE, 0)

    def edges(t, carry):
        img, slot = t // 4, t % 4
        dtok = jnp.concatenate([a_s[(img * pairs + p) * 4 + slot] for p in range(pairs)], axis=1)
        edge_s[slot, img] = nt(wp_s[...], dtok)
        return carry

    lax.fori_loop(0, slots * 4, edges, 0)
    for i in range(slots):
        lat = shift_out([edge_s[s, i] for s in range(4)], masks)
        for s in range(4):
            edge_l[s, 0, i * 16 : (i + 1) * 16, :] = lat[s].astype(BF16)
    advance(EDGE_L, 0)
    state = {g: 1 for g in (LATE, EDGE_L)}
    for g in (*range(FC, PAIR + 3), EARLY):
        done = [k for events in (IMAGE_EVENTS, GRAD_EVENTS, BACK_EVENTS, TAIL_EVENTS) for _, h, k in events if h == g]
        assert done == list(range(1, len(done) + 1))
        state[g] = len(done) + 1
    order = list(END_EVENTS)
    order += [g for g in state for _ in range(len(groups[g]))]
    drained = {g: 0 for g in state}
    for g in order:
        if state[g] <= len(groups[g]):
            for h, stages in enumerate(groups):
                while drained[h] < state[h] - 1 - (h == g):
                    stages[drained[h]].drain()
                    drained[h] += 1
            advance(g, state[g])
            state[g] += 1
    for h, stages in enumerate(groups):
        for stage in stages[drained[h] :]:
            stage.drain()
    assert len(net.known) <= count


def step(images, smalls, bigs):
    time_bin, latents = smalls[0], smalls[3]
    qkv_weight, fc1_weight = bigs[4], bigs[6]
    d, ff = qkv_weight.shape[0], fc1_weight.shape[1]
    slots, chans, side, _ = latents.shape
    toks = side * side // 4
    planes = slots * chans * 4
    pairs = HEADS // 2
    heads = slots * HEADS
    out_shape = (
        jax.ShapeDtypeStruct((2 * ff + 4 * d, d), BF16),
        jax.ShapeDtypeStruct((images, E_ROWS, d), BF16),
        jax.ShapeDtypeStruct((images, L_ROWS, d), BF16),
        jax.ShapeDtypeStruct((2, planes, toks), F32),
    )
    scratch = [(w.shape, w.dtype) for w in bigs[4:]] + [
        ((4, 2, planes, toks), BF16), ((8, 8, d), F32), ((slots * 4, 16, toks), BF16),
        ((slots, 16, toks), BF16), ((16, d), BF16), ((16, d), BF16), ((toks, d), BF16), ((toks, d), BF16), ((slots * 4, d, toks), BF16),
        ((slots * 4, toks, d), F32), ((toks, 128), F32), ((slots * pairs, 4, toks, 128), BF16),
        ((slots * pairs, 4, toks, 128), BF16), ((heads, toks, 128), BF16), ((heads, 4, toks, toks), BF16),
        ((4, toks, toks), F32), ((4, toks, toks), F32), ((2, 1, toks), F32), ((heads, 1, toks), F32), ((heads, 1, toks), F32),
        ((heads, 64, toks), F32), ((slots * 12, toks, 128), BF16), ((slots * 12, toks, 128), BF16),
        ((slots, toks, d), BF16), ((slots, d, toks), BF16), ((slots, toks, d), BF16),
        ((slots, toks, d), F32), ((5, slots, 16, toks), F32),
        ((2 * ff + 4 * d, d), BF16), ((E_ROWS, d), F32), ((L_ROWS, d), F32), ((E_ROWS, d), BF16), ((L_ROWS, d), BF16), ((4, 2, planes, toks), BF16),
        ((3, E_ROWS, d), BF16), ((E_ROWS, d), BF16), ((3, L_ROWS, d), BF16), ((L_ROWS, d), BF16), ((3, 2, planes, toks), BF16),
    ]
    dma = pltpu.SemaphoreType.DMA
    parts_of = group_list(d, ff)
    count = sum(group_copies(images, plan) for _, _, plan in parts_of) + 2 * (3 + images - 1) + 6
    moved = [(s, BF16) for _, rows, plan in parts_of for s in group_shapes(images, rows, plan)]
    return pl.pallas_call(
        functools.partial(step_kernel, images, count),
        out_shape=out_shape,
        in_specs=[SMEM] * 3 + [VMEM] * (len(smalls) - 3) + [ANY] * len(bigs),
        out_specs=(VMEM,) * 4,
        scratch_shapes=[pltpu.VMEM(shape, kind) for shape, kind in scratch]
        + [dma((len(bigs),)), dma((3,)), dma((3,)), dma((count,)), dma((count,))]
        + [pltpu.VMEM(shape, kind) for shape, kind in moved],
        compiler_params=pltpu.CompilerParams(
            collective_id=0, has_side_effects=True, vmem_limit_bytes=64 * 1024 * 1024 - 65536
        ),
        name="step",
    )(*smalls, *bigs)


def finish_kernel(bins, classes, *refs):
    hbm_in, hbm_out, refs = refs[:6], refs[6:26], refs[26:]
    grads_ref, early_ref, late_ref, planes_ref, ada_ref, fada_ref = refs[:6]
    (out_ref, lat_ref, time_ref, class_ref, patch_ref, patch_b_ref, ada_g_ref, ada_b_ref, qkv_g_ref, qv_b_ref, proj_g_ref,
     proj_b_ref, fc1_g_ref, fc1_b_ref, fc2_g_ref, fc2_b_ref, fada_g_ref, fada_b_ref, out_gt_ref, out_b_ref) = outs = refs[6:26]
    in_sem, out_sem = refs[26:]
    d = ada_ref.shape[0]
    ff = fc1_g_ref.shape[1]
    blocks = ff // d
    pairs = HEADS // 2
    slots, chans, side, _ = lat_ref.shape
    groups = early_ref.shape[0]
    images = groups * slots
    held = -(-images // 32) * 32

    loads = []

    def fetch(src, dst):
        c = pltpu.make_async_copy(src, dst, in_sem.at[len(loads)])
        c.start()
        loads.append(c)

    for k in (1, 2):
        fetch(hbm_in[k], refs[k])
    bounds = [b * d for b in range(2 * blocks + 1)] + [2 * ff + 4 * d]
    for a, b in zip(bounds[:-1], bounds[1:]):
        fetch(hbm_in[0].at[a:b, :], grads_ref.at[a:b, :])
    for k in (4, 5, 3):
        fetch(hbm_in[k], refs[k])
    stores = []

    def send(k, *at):
        src, dst = outs[k], hbm_out[k]
        if at:
            src, dst = src.at[at], dst.at[at]
        c = pltpu.make_async_copy(src, dst, out_sem.at[len(stores)])
        c.start()
        stores.append(c)

    loads[0].wait()
    loads[1].wait()

    all_early = early_ref[...].reshape(groups * E_ROWS, d)
    all_late = late_ref[...].reshape(groups * L_ROWS, d)

    def chosen(block, rows, starts, steps):
        many = len(starts) * held
        line = iota((many, 1), 0)
        image = line % held
        item = line // held
        start, step = jnp.zeros_like(line), jnp.zeros_like(line)
        for k, (at, by) in enumerate(zip(starts, steps)):
            start = jnp.where(item == k, at, start)
            step = jnp.where(item == k, by, step)
        want = jnp.where(image < images, image // slots * rows + start + step * (image % slots), -1)
        return nn(flag(iota((many, groups * rows), 1) == want).astype(BF16), block)

    starts = [E_COND, E_COND + slots, E_IDS] + [E_MOD + k * slots for k in range(6)]
    picked = chosen(all_early, E_ROWS, starts, [1, 1, 0] + [1] * 6)
    items = [picked[k * held : (k + 1) * held] for k in range(9)]
    cond, ids = items[0] + items[1], items[2]
    picked = chosen(all_late, L_ROWS, [L_MOD, L_MOD + slots], [1, 1])
    dmods = [picked[:held], picked[held:]] + items[3:]
    img_row, lane = iota((held, d), 0), iota((held, d), 1)

    def id_part(k):
        return jnp.sum(jnp.where(lane == k * slots + img_row % slots, ids, 0.0), axis=1, keepdims=True)

    time_id, class_id = id_part(0), 256.0 * id_part(1) + id_part(2)

    left = jnp.concatenate(parts(swish(cond), 2), axis=0).T
    pairs_of = [jnp.concatenate([dmods[p], dmods[p + 1]], axis=1).astype(BF16) for p in range(0, 8, 2)]
    for k, pair in enumerate(pairs_of):
        grad = nn(left, jnp.concatenate([pair, pair], axis=0))
        if k < 3:
            lanes = slice(2 * k * d, 2 * (k + 1) * d)
            ada_g_ref[:, lanes] = grad
            send(6, slice(None), lanes)
        else:
            fada_g_ref[...] = grad
            send(16)

    for b in range(blocks):
        at = slice(b * d, (b + 1) * d)
        loads[2 + b].wait()
        fc2_g_ref[at, :] = grads_ref[at, :].astype(F32)
        send(14, at, slice(None))
    for b in range(blocks):
        at = slice(b * d, (b + 1) * d)
        loads[2 + blocks + b].wait()
        fc1_g_ref[:, at] = grads_ref[ff + b * d : ff + (b + 1) * d, :].astype(F32)
        send(12, slice(None), at)
    loads[2 + 2 * blocks].wait()
    third = d // 3
    for p in range(pairs):
        at = 2 * ff + p * (d + third)
        proj_g_ref[p * third : (p + 1) * third, :] = grads_ref[at + d : at + d + third, :].astype(F32)
        for k in range(3):
            lanes = slice(k * d + p * 128, k * d + (p + 1) * 128)
            qkv_g_ref[:, lanes] = grads_ref[at : at + d, k * 128 : (k + 1) * 128].astype(F32)
    send(8)
    send(10)

    for c in loads[3 + 2 * blocks :]:
        c.wait()
    dact = jnp.zeros((held, d), F32)
    for k, pair in enumerate(pairs_of):
        w = ada_ref[:, 2 * k * d : 2 * (k + 1) * d] if k < 3 else fada_ref[...]
        dact = dact + nt(pair, w)
    bias_rows = [col_sum(v) for v in dmods]
    ada_b_ref[...] = jnp.concatenate(bias_rows[:6], axis=1).reshape(6 * d)
    fada_b_ref[...] = jnp.concatenate(bias_rows[6:], axis=1).reshape(2 * d)
    sig = 1.0 / (1.0 + jnp.exp(-cond))
    dcond = dact * (sig * (1.0 + cond * (1.0 - sig)))
    stack = jnp.concatenate(parts(dcond, 2), axis=0)
    for ref, ids_col, many in ((class_ref, class_id, classes), (time_ref, time_id, bins)):
        wide = -(-many // 128) * 128
        at = iota((held, wide), 1).astype(F32)
        hit = flag((at == ids_col) & (iota((held, wide), 0) < images)).astype(BF16)
        ref[...] = tn(jnp.concatenate([hit, hit], axis=0), stack)[:many]
    send(3)
    send(2)

    early, late = jnp.sum(early_ref[...].astype(F32), axis=0), jnp.sum(late_ref[...].astype(F32), axis=0)
    swap = flag(iota((16, 16), 0) == (iota((16, 16), 1) ^ 3)).astype(BF16)

    def swapped(v):
        return tree([nn(swap, p) for p in parts(v, 2)] + [nn(swap, parts(v, 3)[2]), jnp.zeros_like(v)])

    patch_ref[...] = swapped(late[L_PATCH : L_PATCH + 16])
    out_gt_ref[...] = swapped(early[E_OUT : E_OUT + 16])

    def line(v, row):
        return v[row : row + 1, :]

    patch_b_ref[...] = line(late, L_PATCH_B).reshape(d)
    qv_b_ref[...] = jnp.concatenate([line(late, L_Q_B), line(late, L_V_B)], axis=1).reshape(2 * d)
    proj_b_ref[...] = line(early, E_PROJ_B).reshape(d)
    fc1_b_ref[...] = jnp.concatenate([line(early, E_FC1_B + b) for b in range(blocks)], axis=1).reshape(ff)
    fc2_b_ref[...] = line(early, E_FC2_B).reshape(d)
    tail = jnp.broadcast_to(line(early, E_OUT_B)[:, 0:16], (16, 16))
    pick = flag(iota((16, 16), 1) == (iota((16, 16), 0) ^ 3))
    column = jnp.sum(tail * pick, axis=1, keepdims=True)
    out_b_ref[...] = col_sum(jnp.where(iota((16, 16), 0) == iota((16, 16), 1), column, 0.0)).reshape(16)

    half = side // 2
    keep, spread, pick = plane_maps(slots, chans, side, half)
    for k in (4, 5, 7, 9, 11, 13, 15, 17, 18, 19):
        send(k)
    for k, ref in ((0, lat_ref), (1, out_ref)):
        many = 2 - k
        planes = jnp.concatenate(parts(planes_ref[k], many), axis=0)
        pieces, maps = [], []
        for j in range(2):
            wide = tn(jnp.concatenate([pick[j]] * many, axis=0), planes) * keep
            pieces += parts(wide, many)
            maps += [spread[j]] * many
        total = nt(jnp.concatenate(pieces, axis=1), jnp.concatenate(maps, axis=1))
        ref[...] = total.reshape(ref.shape).astype(ref.dtype)
        send(1 - k)
    for c in stores:
        c.wait()


def finish(bins, classes, latents, grads, early, late, planes, ada_weight, fada_weight, ff):
    d = ada_weight.shape[0]
    f = lambda *shape: jax.ShapeDtypeStruct(shape, F32)
    out_shape = (
        jax.ShapeDtypeStruct(latents.shape, BF16), f(*latents.shape), f(bins, d), f(classes, d), f(16, d), f(d),
        f(d, 6 * d), f(6 * d), f(d, 3 * d), f(2 * d), f(d, d), f(d), f(d, ff), f(ff), f(ff, d), f(d), f(d, 2 * d), f(2 * d),
        f(16, d), f(16),
    )
    ins = (grads, early, late, planes, ada_weight, fada_weight)
    dma = pltpu.SemaphoreType.DMA
    return pl.pallas_call(
        functools.partial(finish_kernel, bins, classes),
        out_shape=out_shape,
        in_specs=[ANY] * 6,
        out_specs=(ANY,) * len(out_shape),
        scratch_shapes=[pltpu.VMEM(x.shape, x.dtype) for x in ins + out_shape]
        + [dma((6 + 2 * (ff // d),)), dma((20 + 2 * (ff // d),))],
        compiler_params=pltpu.CompilerParams(vmem_limit_bytes=60 * 1024 * 1024),
        name="finish",
    )(*ins)


def local(
    images, latents, time_bin, class_label, live, time_table, class_table, patch_weight, patch_bias, ada_weight, ada_bias,
    qkv_weight, qv_bias, proj_weight, proj_bias, fc1_weight, fc1_bias, fc2_weight, fc2_bias, final_ada_weight,
    final_ada_bias, out_weight, out_bias, cotangent,
):
    d, ff = qkv_weight.shape[0], fc1_weight.shape[1]
    pos_a, pos_b = position_tables(LATENT // 2, d)
    smalls = (
        time_bin, class_label, live, latents, cotangent, patch_bias, ada_bias, qv_bias, proj_bias, fc1_bias, fc2_bias,
        final_ada_bias, out_bias, jnp.asarray(pos_a), jnp.asarray(pos_b), patch_weight, out_weight.T,
    )
    bigs = (time_table, class_table, ada_weight, final_ada_weight, qkv_weight, proj_weight, fc1_weight, fc2_weight)
    grads, early, late, planes = step(images, smalls, bigs)
    outs = list(
        finish(
            time_table.shape[0], class_table.shape[0], latents, grads, early, late, planes, ada_weight, final_ada_weight, ff
        )
    )
    outs[18] = outs[18].T
    return tuple(outs)


def solution(mesh):
    assert mesh.shape["row"] == 2 and mesh.shape["col"] == 2
    tiles = P("img", None, "row", "col")
    return jax.shard_map(
        functools.partial(local, mesh.shape["img"]),
        mesh=mesh,
        in_specs=(tiles,) + (P("img"),) * 3 + (P(),) * 18 + (tiles,),
        out_specs=(tiles, tiles) + (P(),) * 18,
        check_vma=False,
    )
```
